32 devices in a mesh: group: 2 (over x), space: 16 (over z, y, core).
Axes of the slice: x: 2, y: 2, z: 4, core: 2. Of those that a mesh axis runs over, the one named last changes fastest.
Arguments:
- columns_in: bfloat16 [8192, 1024], P(('group', 'space')), parts along dimension 0, may hold values from -6 to 6
- cotangent: bfloat16 [8192, 1024], P(('group', 'space')), parts along dimension 0, may hold values from -6 to 6
- conv_weight: bfloat16 [7, 16, 16], replicated, may hold values from -0.5 to 0.5
- mix_weight: bfloat16 [1024, 1024], replicated, may hold values from -0.1875 to 0.1875
- neighbours: int32 [4096, 7], P('space'), may hold values from 0 to 4095, as said below
- rotations: int32 [4096], P('space'), may hold values from 0 to 5
- pentagons: int32 [4096], P('space'), may hold values 0 or 1
Outputs:
- grad_input: bfloat16 [8192, 1024], P(('group', 'space')), parts along dimension 0
- grad_mix: float32 [1024, 2048], P('space', 'group'), parts along dimension 1
- grad_conv: float32 [14, 16, 16], P('group'), parts along dimension 0
The draws below stay inside these ranges and needn't reach their ends.
There are 2 independent parts, one for each index of `group`. The reference program is written for one: setup_inputs(seed, part) draws one part's arguments, and reference() takes and returns one part's arrays. A program takes and returns all parts, laid end to end along the dimension named above; an argument that names none is the same for every part. Nothing has to cross between parts.
Inputs may be any that keep to these rules, and one draw needn't show every extreme that they name: `neighbours`: entry 0 of each row is the column itself. Every other entry lies in the column's own grid row of 256 consecutive column indices or in the row just before or after it, the last row of the grid followed by the first. The relation is symmetric: if b is a neighbour of a, then a is a neighbour of b.
All inputs are finite; a program needn't handle non-finite values. No bound on the sum of `pentagons` on one device may be relied on, other than what follows from the above.
Results may differ from the reference program's by a relative error of at most 0.005.
Values may be sent and summed in bfloat16 or wider, within the bound.
No kernel may reach another device: no remote copies, remote signals or barrier semaphores. Data moves between devices by JAX's collectives and lax.ppermute only.
A program may use at most 128 MiB of HBM per device.

```python
import jax
import jax.numpy as jnp

C = 16
LEV = 64
F = 1024
TAPS = 7
ROW = 256
COLS = 4096


def draw_neighbours(key, part):
    grid_rows = COLS // ROW
    shears = jax.random.randint(key, (grid_rows,), 0, ROW, dtype=jnp.int32)
    column_ids = jnp.arange(COLS, dtype=jnp.int32)
    row_ids = column_ids // ROW
    place = column_ids % ROW
    above = (row_ids + 1) % grid_rows
    below = (row_ids - 1 + grid_rows) % grid_rows
    shear_here = shears[row_ids]
    shear_below = shears[below]

    def locate(row_index, place_index):
        return row_index * ROW + place_index % ROW
    return jnp.stack([column_ids, locate(row_ids, place + 1), locate(above, place + shear_here), locate(above, place + shear_here - 1), locate(row_ids, place - 1), locate(below, place - shear_below), locate(below, place - shear_below + 1)], axis=1).astype(jnp.int32)


def with_ends(entries, stream_key, smallest, largest):
    longest = entries.shape.index(max(entries.shape))
    spots = []
    for shift in (0, 1):
        where = [jax.random.randint(jax.random.fold_in(stream_key, axis), (), 0, length) for axis, length in enumerate(entries.shape)]
        where[longest] = (where[longest] + shift) % entries.shape[longest]
        spots.append(tuple(where))
    return entries.at[spots[0]].set(smallest).at[spots[1]].set(largest)


def with_spikes(drawn, own_key, source, target, blocks, factor):
    owner, partner = [(jnp.arange(drawn.shape[axis_at]) // (drawn.shape[axis_at] // blocks)).reshape([-1 if axis == axis_at else 1 for axis in range(drawn.ndim)]) for axis_at in (source, target)]
    chosen = jax.random.permutation(own_key, blocks)[partner]
    strong = (owner == chosen) | (owner == (partner + blocks // 2) % blocks)
    return jnp.where(strong, factor * drawn, drawn)


def levels(own_key, extent, shards, low, top_value):
    gain = 1.0
    for position, shards_of in shards:
        draws = jax.random.uniform(jax.random.fold_in(jax.random.fold_in(own_key, 6), position), (shards_of,), jnp.float32, low / len(shards), top_value / len(shards))
        gain = gain * jnp.repeat(jnp.exp(draws), extent[position] // shards_of).reshape((-1,) + (1,) * (len(extent) - 1 - position))
    return gain


def centred(rng, extent, width, most, shards=(), held_as=jnp.bfloat16):
    factor_of = levels(rng, extent, shards, -0.22, 0.18) if shards else 1.0
    entries = jax.random.normal(rng, extent, jnp.float32) * width * factor_of
    return jnp.minimum(jnp.maximum(entries, -most), most).astype(held_as)


def gaussian_with(stream_key, shape, scale, most, shards, heavy, kind=jnp.bfloat16):
    values = scale * jax.random.normal(stream_key, shape, jnp.float32)
    if shards:
        values = values * levels(stream_key, shape, shards, -0.22, 0.18)
    return jnp.clip(with_spikes(values, jax.random.fold_in(stream_key, 3), *heavy), -most, most).astype(kind)


def setup_inputs(seed: int = 0, part: int = 0) -> dict:
    splits = jax.random.split(jax.random.key(seed), 8)
    part_splits = jax.random.split(jax.random.fold_in(splits[7], part), 8)
    return {
        "columns_in": gaussian_with(part_splits[0], (COLS, F), 1.0, 6.0, ((0, 16),), (0, 1, 16, 2.0)),
        "cotangent": centred(part_splits[1], (COLS, F), 1.0, 6.0, ((0, 16),)),
        "conv_weight": centred(splits[2], (TAPS, C, C), (TAPS * C) ** -0.5, 0.5),
        "mix_weight": centred(splits[3], (F, F), F ** -0.5, 0.1875),
        "neighbours": draw_neighbours(jax.random.fold_in(splits[7], 71), part),
        "rotations": with_ends(jax.random.randint(splits[5], (COLS,), 0, 6), jax.random.fold_in(splits[5], 1), 0, 5).astype(jnp.int32),
        "pentagons": with_ends((jax.random.randint(splits[6], (COLS,), 0, 16) < 1).astype(jnp.int32), jax.random.fold_in(splits[6], 1), 0, 1),
    }


def tap_sources(neighbours, rotations, pentagons, index_tap):
    if index_tap == 0:
        slot_index = jnp.zeros_like(rotations)
    else:
        slot_index = 1 + (index_tap - 1 - rotations) % 6
    source = jnp.take_along_axis(neighbours, slot_index[:, None], axis=1)[:, 0]
    keep_mask = 1 - pentagons * (slot_index == 6).astype(jnp.int32)
    return (source, keep_mask)

def reference(columns_in, cotangent, conv_weight, mix_weight, neighbours, rotations, pentagons):
    preact = jnp.zeros((COLS, LEV, C), jnp.float32)
    for index_tap in range(TAPS):
        source, keep_mask = tap_sources(neighbours, rotations, pentagons, index_tap)
        tap_rows = jnp.take(columns_in, source, axis=0) * keep_mask.astype(jnp.bfloat16)[:, None]
        preact = preact + jnp.einsum('nlc,cd->nld', tap_rows.reshape(COLS, LEV, C).astype(jnp.float32), conv_weight[index_tap].astype(jnp.float32))
    output, pullback = jax.vjp(jax.nn.gelu, preact)
    active = output.reshape(COLS, F).astype(jnp.bfloat16)
    upstream = jnp.dot(cotangent, mix_weight.T, preferred_element_type=jnp.float32)
    grad_pre = pullback(upstream.reshape(COLS, LEV, C))[0].astype(jnp.bfloat16)
    grad_mix = jnp.dot(active.T, cotangent, preferred_element_type=jnp.float32) / jnp.sqrt(jnp.float32(COLS))
    spread = cotangent.astype(jnp.float32)
    conv_terms = []
    for index_tap in range(TAPS):
        source, keep_mask = tap_sources(neighbours, rotations, pentagons, index_tap)
        tap_rows = jnp.take(columns_in, source, axis=0) * keep_mask.astype(jnp.bfloat16)[:, None]
        conv_terms.append(jnp.einsum('nlc,nld->cd', tap_rows.reshape(COLS, LEV, C).astype(jnp.float32), grad_pre.astype(jnp.float32)))
        tap_term = jnp.einsum('nld,cd->nlc', grad_pre.astype(jnp.float32), conv_weight[index_tap].astype(jnp.float32)).reshape(COLS, F)
        tap_term = tap_term * keep_mask.astype(jnp.float32)[:, None]
        spread = spread + jax.ops.segment_sum(tap_term, source, num_segments=COLS)
    grad_conv = jnp.stack(conv_terms) / jnp.sqrt(jnp.float32(COLS * LEV))
    return (spread.astype(jnp.bfloat16), grad_mix, grad_conv)
```

```python
import functools

import jax
import jax.numpy as jnp
from jax import lax
from jax.experimental import pallas as pl
from jax.experimental.pallas import tpu as pltpu
from jax.sharding import PartitionSpec as P

ROW = 256
WIDE = 256
TANH_SCALE = 0.7978845608028654
TANH_CUBE = 0.044715


f32 = jnp.float32
bf16 = jnp.bfloat16


def mm(a, b):
    return jnp.dot(a, b, preferred_element_type=f32)


def contract(a, b, dim_a, dim_b, **kw):
    return lax.dot_general(
        a, b, (((dim_a,), (dim_b,)), ((), ())), preferred_element_type=f32, **kw
    )


def iota(shape, dim):
    return lax.broadcasted_iota(jnp.int32, shape, dim)


def onehot(cond):
    return jnp.where(cond, 1.0, 0.0).astype(bf16)


def call(body, outs, cost, *args, scratch=(), scalars=0):
    in_specs = [pl.BlockSpec(memory_space=pltpu.SMEM)] * scalars
    in_specs += [pl.BlockSpec(memory_space=pltpu.VMEM)] * (len(args) - scalars)
    return pl.pallas_call(
        body,
        out_shape=[jax.ShapeDtypeStruct(s, d) for s, d in outs],
        in_specs=in_specs,
        out_specs=[pl.BlockSpec(memory_space=pltpu.VMEM)] * len(outs),
        scratch_shapes=list(scratch),
        cost_estimate=pl.CostEstimate(flops=cost, transcendentals=0, bytes_accessed=8 << 20),
        compiler_params=pltpu.CompilerParams(vmem_limit_bytes=32 << 20),
    )(*args)


def picked(meta, tap, dim):
    part = lambda k: lax.slice_in_dim(meta, k, k + 1, axis=dim)
    turn = tap - 1 - part(7)
    slot = 1 + jnp.where(turn < 0, turn + 6, turn)
    source = jnp.full_like(slot, -1)
    for k in range(1, 7):
        source = jnp.where(slot == k, part(k), source)
    return source


def spread_weights(rows):
    taps_c, c = rows.shape
    repeat = onehot(iota((c, WIDE), 1) % c == iota((c, WIDE), 0))
    down = onehot(iota((WIDE, c), 0) % c == iota((WIDE, c), 1))
    same = iota((WIDE, WIDE), 0) // c == iota((WIDE, WIDE), 1) // c
    wide = mm(rows, repeat).astype(bf16)
    out = []
    for tap in range(taps_c // c):
        block = mm(down, wide[tap * c : (tap + 1) * c])
        out.append(jnp.where(same, block, 0.0).astype(bf16))
    return out


def early_kernel(meta, meta_t, x, cot, conv, conv_t, mix, up, halo_sel, back_sel, own, pre, wk, wkt):
    n = x.shape[0]
    taps = wk.shape[0] // WIDE
    for tap, w in enumerate(spread_weights(conv[...])):
        wk[tap * WIDE : (tap + 1) * WIDE, :] = w
    for tap, w in enumerate(spread_weights(conv_t[...])):
        wkt[tap * WIDE : (tap + 1) * WIDE, :] = w
    m = meta[...]
    mt = meta_t[...]
    for tap in range(1, taps):
        at = (tap - 1) * n
        source = picked(m, tap, 1)
        halo_sel[at : at + n, :ROW] = onehot(iota((n, ROW), 1) == source)
        halo_sel[at : at + n, ROW:] = onehot(iota((n, ROW), 1) + (ROW + n) == source)
        mine = onehot(iota((n, n), 1) + ROW == source)
        own[at : at + n, :] = mm(mine, x[...]).astype(bf16)
        source_t = picked(mt, tap, 0)
        back_sel[:, at : at + n] = onehot(iota((n + 2 * ROW, n), 0) == source_t)
    for c in range(0, x.shape[1], WIDE):
        acc = mm(x[:, c : c + WIDE], wk[:WIDE, :])
        for tap in range(1, taps):
            acc += mm(own[(tap - 1) * n : tap * n, c : c + WIDE], wk[tap * WIDE : (tap + 1) * WIDE, :])
        pre[:, c : c + WIDE] = acc
    up[...] = contract(cot[...], mix[...], 1, 1)


def gelu_tanh(v):
    return jnp.tanh(TANH_SCALE * (v + TANH_CUBE * (v * v * v)))


def mix_rows(act_t, cot, bit, blocks, share, start):
    rows = [
        act_t[pl.ds(pl.multiple_of((2 * k + bit) * share, share), share), :] for k in range(blocks // 2)
    ]
    return mm(jnp.concatenate(rows, axis=0), cot[...])


def forward_kernel(blocks, me, low, high, halo_sel, pre_own, wk, cot, halo, pre, act_t, send):
    n, width = pre.shape
    taps = wk.shape[0] // WIDE
    for c in range(0, width, WIDE):
        rows = mm(halo_sel[:, :ROW], low[:, c : c + WIDE]) + mm(halo_sel[:, ROW:], high[:, c : c + WIDE])
        rows = rows.astype(bf16)
        halo[:, c : c + WIDE] = rows
        acc = pre_own[:, c : c + WIDE]
        for tap in range(1, taps):
            acc += mm(rows[(tap - 1) * n : tap * n], wk[tap * WIDE : (tap + 1) * WIDE, :])
        pre[:, c : c + WIDE] = acc
        active = (0.5 * acc) * (1.0 + gelu_tanh(acc))
        act_t[c : c + WIDE, :] = active.T.astype(bf16)
    share = width // blocks
    send[...] = mix_rows(act_t, cot, 1 - me[0], blocks, share, 0).astype(bf16)


def keep_kernel(blocks, me, act_t, cot, keep):
    keep[...] = mix_rows(act_t, cot, me[0], blocks, act_t.shape[0] // blocks, 0)


def backward_kernel(channels, scale, up, pre, x, own, halo, wkt, back_sel, grad, terms, low, high, conv):
    n, width = pre.shape
    taps = wkt.shape[0] // WIDE
    acc = [jnp.zeros((WIDE, WIDE), f32) for _ in range(taps)]
    for c in range(0, width, WIDE):
        v = pre[:, c : c + WIDE]
        t = gelu_tanh(v)
        slope = 0.5 * (1.0 + t) + (0.5 * TANH_SCALE) * v * (1.0 - t * t) * (1.0 + (3 * TANH_CUBE) * (v * v))
        g32 = up[:, c : c + WIDE] * slope
        g = g32.astype(bf16)
        grad[:, c : c + WIDE] = g
        g_t = g32.T.astype(bf16)
        for tap in range(taps):
            if tap == 0:
                rows = x[:, c : c + WIDE]
            else:
                rows = own[(tap - 1) * n : tap * n, c : c + WIDE] + halo[(tap - 1) * n : tap * n, c : c + WIDE]
                terms[(tap - 1) * n : tap * n, c : c + WIDE] = mm(
                    g, wkt[tap * WIDE : (tap + 1) * WIDE, :]
                ).astype(bf16)
            acc[tap] += mm(g_t, rows)
        low[:, c : c + WIDE] = mm(back_sel[:ROW, :], terms[:, c : c + WIDE]).astype(bf16)
        high[:, c : c + WIDE] = mm(back_sel[ROW + n :, :], terms[:, c : c + WIDE]).astype(bf16)
    same = iota((WIDE, WIDE), 0) // channels == iota((WIDE, WIDE), 1) // channels
    fold = jnp.where(iota((WIDE, channels), 0) % channels == iota((WIDE, channels), 1), 1.0, 0.0)
    for tap in range(taps):
        block = jnp.where(same, acc[tap], 0.0)
        block = jnp.sum(block.reshape(WIDE // channels, channels, WIDE), axis=0)
        conv[:, tap * channels : (tap + 1) * channels] = (
            contract(block, fold, 1, 0, precision=lax.Precision.HIGHEST) * scale
        )


def inner_kernel(grad, terms, wkt, back_sel, cot, inner):
    n, width = grad.shape
    for c in range(0, width, WIDE):
        acc = mm(grad[:, c : c + WIDE], wkt[:WIDE, :]) + cot[:, c : c + WIDE].astype(f32)
        inner[:, c : c + WIDE] = acc + mm(back_sel[ROW : ROW + n, :], terms[:, c : c + WIDE])


def shards(columns_in, cotangent, conv_weight, mix_weight, neighbours, rotations, pentagons):
    n, width = columns_in.shape
    taps, channels = conv_weight.shape[:2]
    devices = lax.axis_size("space")
    place = lax.axis_index("space")
    total_cols = n * devices
    levels = width // channels
    bits = devices.bit_length() - 1

    def ring(value, by):
        return lax.ppermute(value, "space", [(i, (i + by) % devices) for i in range(devices)])

    def swap(value, bit):
        return lax.ppermute(value, "space", [(i, i ^ (1 << bit)) for i in range(devices)])

    below = ring(columns_in, 1)
    above = ring(columns_in, -1)
    local = (neighbours - place * n + ROW) % total_cols
    void = (pentagons[:, None] == 1) & (jnp.arange(taps)[None, :] == 6)
    meta = jnp.concatenate([jnp.where(void, -1, local), rotations[:, None]], axis=1)
    pairs = (taps - 1) * n
    up, halo_sel, back_sel, own, pre_own, wk, wkt = call(
        early_kernel,
        [
            ((n, width), f32),
            ((pairs, 2 * ROW), bf16),
            ((n + 2 * ROW, pairs), bf16),
            ((pairs, width), bf16),
            ((n, width), f32),
            ((taps * WIDE, WIDE), bf16),
            ((taps * WIDE, WIDE), bf16),
        ],
        3 << 30,
        meta,
        meta.T,
        columns_in,
        cotangent,
        conv_weight.reshape(taps * channels, channels),
        conv_weight.transpose(0, 2, 1).reshape(taps * channels, channels),
        mix_weight,
    )
    core = (place & 1).astype(jnp.int32).reshape(1)
    halo, pre, act_t, send = call(
        functools.partial(forward_kernel, devices),
        [
            ((pairs, width), bf16),
            ((n, width), f32),
            ((width, n), bf16),
            ((width // 2, width), bf16),
        ],
        3 << 30,
        core,
        below,
        above,
        halo_sel,
        pre_own,
        wk,
        cotangent,
        scalars=1,
    )
    got = swap(send, 0)
    (keep,) = call(
        functools.partial(keep_kernel, devices),
        [((width // 2, width), f32)],
        1 << 29,
        core,
        act_t,
        cotangent,
        scalars=1,
    )
    grad, terms, to_low, to_high, conv = call(
        functools.partial(backward_kernel, channels, 1.0 / float(total_cols * levels) ** 0.5),
        [
            ((n, width), bf16),
            ((pairs, width), bf16),
            ((ROW, width), bf16),
            ((ROW, width), bf16),
            ((channels, taps * channels), f32),
        ],
        4 << 30,
        up,
        pre,
        columns_in,
        own,
        halo,
        wkt,
        back_sel,
    )
    share = width // devices
    half = width // 2
    parts = []
    for first in (0, 1):
        order = list(range(1, bits))
        if first and len(order) > 1:
            order[0], order[1] = order[1], order[0]
        left = list(range(bits - 1, 0, -1))
        cols = slice(first * half, (first + 1) * half)
        shape = (2,) * len(left) + (share, half)
        parts.append([(keep[:, cols] + got[:, cols].astype(f32)).reshape(shape), left, order])
    for stage in range(bits - 1):
        moved = []
        for value, left, order in parts:
            bit = order[stage]
            axis = left.index(bit)
            mine = (place >> bit) & 1
            sent = lax.dynamic_index_in_dim(value, 1 - mine, axis, keepdims=False).astype(bf16)
            moved.append(swap(sent, bit))
        for k, (value, left, order) in enumerate(parts):
            bit = order[stage]
            axis = left.index(bit)
            mine = (place >> bit) & 1
            kept = lax.dynamic_index_in_dim(value, mine, axis, keepdims=False)
            parts[k] = [kept + moved[k].astype(f32), [b for b in left if b != bit], order]
    grad_mix = jnp.concatenate([p[0] for p in parts], axis=1) / jnp.sqrt(f32(total_cols))

    from_below = ring(to_high, 1)
    from_above = ring(to_low, -1)
    for bit in range(bits):
        conv = conv + swap(conv, bit)
    grad_conv = conv.reshape(channels, taps, channels).transpose(1, 2, 0)
    (inner,) = call(
        inner_kernel, [((n, width), f32)], 1 << 30, grad, terms, wkt, back_sel, cotangent
    )
    grad_input = (inner + from_below.astype(f32) + from_above.astype(f32)).astype(bf16)
    return grad_input, grad_mix, grad_conv


def solution(mesh):
    return jax.shard_map(
        shards,
        mesh=mesh,
        in_specs=(
            P(("group", "space"), None),
            P(("group", "space"), None),
            P(),
            P(),
            P("space", None),
            P("space"),
            P("space"),
        ),
        out_specs=(P(("group", "space"), None), P("space", "group"), P("group", None, None)),
        check_vma=False,
    )
```

```python
import functools

import jax
import jax.numpy as jnp
from jax import lax
from jax.experimental import pallas as pl
from jax.experimental.pallas import tpu as pltpu
from jax.sharding import PartitionSpec as P


ROW = 256
WIDE = 256
TANH_SCALE = 0.7978845608028654
TANH_CUBE = 0.044715


f32 = jnp.float32
bf16 = jnp.bfloat16


def mm(a, b):
    return jnp.dot(a, b, preferred_element_type=f32)


def contract(a, b, dim_a, dim_b, **kw):
    return lax.dot_general(
        a, b, (((dim_a,), (dim_b,)), ((), ())), preferred_element_type=f32, **kw
    )


def iota(shape, dim):
    return lax.broadcasted_iota(jnp.int32, shape, dim)


def onehot(cond):
    return jnp.where(cond, 1.0, 0.0).astype(bf16)


def call(body, outs, cost, *args, scratch=(), scalars=0, far=()):
    space = lambda k: pltpu.SMEM if k < scalars else pltpu.HBM if k in far else pltpu.VMEM
    return pl.pallas_call(
        body,
        out_shape=[jax.ShapeDtypeStruct(s, d) for s, d in outs],
        in_specs=[pl.BlockSpec(memory_space=space(k)) for k in range(len(args))],
        out_specs=[pl.BlockSpec(memory_space=pltpu.VMEM)] * len(outs),
        scratch_shapes=list(scratch),
        cost_estimate=pl.CostEstimate(flops=cost, transcendentals=0, bytes_accessed=8 << 20),
        compiler_params=pltpu.CompilerParams(vmem_limit_bytes=12 << 20),
    )(*args)


def picked(local_t, turns, tap):
    turn = tap - 1 - turns
    slot = 1 + jnp.where(turn < 0, turn + 6, turn)
    source = jnp.full_like(slot, -1)
    for k in range(1, 7):
        source = jnp.where(slot == k, local_t[k : k + 1, :], source)
    return source


def early_kernel(
    place, near, turns, void, x_hbm, cot_hbm, conv_hbm, mix_hbm, up, halo_sel, back_sel, own, pre, wk, wkt, x, cot, conv, mix, sems
):
    copies = [
        pltpu.make_async_copy(src, dst, sems.at[k])
        for k, (src, dst) in enumerate(((conv_hbm, conv), (x_hbm, x), (cot_hbm, cot), (mix_hbm, mix)))
    ]
    for copy in copies:
        copy.start()
    n = x.shape[0]
    taps, c = conv.shape[:2]
    offset, total = place[0], place[1]
    moved = near[...] - offset + ROW
    moved = jnp.where(moved < 0, moved + total, moved)
    moved = jnp.where(moved >= total, moved - total, moved)
    dropped = (void[...] == 1) & (iota((taps, n), 0) == 6)
    local_t = jnp.where(dropped, -1, moved)
    sources = [picked(local_t, turns[...], tap) for tap in range(1, taps)]
    sources_t = jnp.concatenate(sources + [sources[0]] * (8 - len(sources)), axis=0)
    eye = jnp.where(iota((n, n), 0) == iota((n, n), 1), 1.0, 0.0)
    columns = contract(eye, sources_t.astype(f32), 1, 1, precision=lax.Precision.HIGHEST)
    columns = columns.astype(jnp.int32)

    copies[0].wait()
    repeat = onehot(iota((c, WIDE), 1) % c == iota((c, WIDE), 0))
    down = onehot(iota((WIDE, c), 0) % c == iota((WIDE, c), 1))
    same = iota((WIDE, WIDE), 0) // c == iota((WIDE, WIDE), 1) // c
    for tap in range(taps):
        for dim, out in ((1, wk), (0, wkt)):
            wide = contract(conv[tap], repeat, dim, 0).astype(bf16)
            out[tap * WIDE : (tap + 1) * WIDE, :] = jnp.where(same, mm(down, wide), 0.0).astype(bf16)
    copies[1].wait()
    for tap in range(1, taps):
        at = (tap - 1) * n
        source = columns[:, tap - 1 : tap]
        halo_sel[at : at + n, :ROW] = onehot(iota((n, ROW), 1) == source)
        halo_sel[at : at + n, ROW:] = onehot(iota((n, ROW), 1) + (ROW + n) == source)
        mine = onehot(iota((n, n), 1) + ROW == source)
        own[at : at + n, :] = mm(mine, x[...]).astype(bf16)
        back_sel[:, at : at + n] = onehot(iota((n + 2 * ROW, n), 0) == sources[tap - 1])
    for c in range(0, x.shape[1], WIDE):
        acc = mm(x[:, c : c + WIDE], wk[:WIDE, :])
        for tap in range(1, taps):
            acc += mm(own[(tap - 1) * n : tap * n, c : c + WIDE], wk[tap * WIDE : (tap + 1) * WIDE, :])
        pre[:, c : c + WIDE] = acc
    copies[2].wait()
    copies[3].wait()
    up[...] = contract(cot[...], mix[...], 1, 1)


def gelu_tanh(v):
    return jnp.tanh(TANH_SCALE * (v + TANH_CUBE * (v * v * v)))


def mix_rows(act_t, cot, bit, blocks, share):
    rows = [
        act_t[pl.ds(pl.multiple_of((2 * k + bit) * share, share), share), :] for k in range(blocks // 2)
    ]
    return mm(jnp.concatenate(rows, axis=0), cot[...])


def forward_kernel(blocks, me, low, high, halo_sel, pre_own, wk, cot, halo, pre, act_t, send):
    n, width = pre.shape
    taps = wk.shape[0] // WIDE
    for c in range(0, width, WIDE):
        both = jnp.concatenate([low[:, c : c + WIDE], high[:, c : c + WIDE]], axis=0)
        rows = mm(halo_sel[...], both).astype(bf16)
        halo[:, c : c + WIDE] = rows
        acc = pre_own[:, c : c + WIDE]
        for tap in range(1, taps):
            acc += mm(rows[(tap - 1) * n : tap * n], wk[tap * WIDE : (tap + 1) * WIDE, :])
        pre[:, c : c + WIDE] = acc
        active = (0.5 * acc) * (1.0 + gelu_tanh(acc))
        act_t[c : c + WIDE, :] = active.T.astype(bf16)
    share = width // blocks
    send[...] = mix_rows(act_t, cot, 1 - me[0], blocks, share).astype(bf16)


def keep_kernel(blocks, me, act_t, cot, keep):
    keep[...] = mix_rows(act_t, cot, me[0], blocks, act_t.shape[0] // blocks)


def merge_kernel(blocks, me, keep, got, send_a, keep_a, send_b, keep_b):
    share = keep.shape[0] * 2 // blocks
    half = keep.shape[1] // 2
    for first, send, kept in ((0, send_a, keep_a), (1, send_b, keep_b)):
        bit = me[1 + first]
        cols = slice(first * half, (first + 1) * half)
        for q in range(blocks // 4):
            base = (q >> first) * (2 << first) + (q & first)
            for value, out in ((1 - bit, send), (bit, kept)):
                at = pl.ds(pl.multiple_of((base + (value << first)) * share, share), share)
                out[q * share : (q + 1) * share, :] = (keep[at, cols] + got[at, cols].astype(f32)).astype(out.dtype)


def backward_kernel(channels, scale, up, pre, x, own, halo, wkt, back_sel, grad, terms, low, high, conv):
    n, width = pre.shape
    taps = wkt.shape[0] // WIDE
    acc = [jnp.zeros((WIDE, WIDE), f32) for _ in range(taps)]
    for c in range(0, width, WIDE):
        v = pre[:, c : c + WIDE]
        t = gelu_tanh(v)
        slope = 0.5 * (1.0 + t) + (0.5 * TANH_SCALE) * v * (1.0 - t * t) * (1.0 + (3 * TANH_CUBE) * (v * v))
        g32 = up[:, c : c + WIDE] * slope
        g = g32.astype(bf16)
        grad[:, c : c + WIDE] = g
        g_t = g32.T.astype(bf16)
        for tap in range(taps):
            if tap == 0:
                rows = x[:, c : c + WIDE]
            else:
                rows = own[(tap - 1) * n : tap * n, c : c + WIDE] + halo[(tap - 1) * n : tap * n, c : c + WIDE]
                terms[(tap - 1) * n : tap * n, c : c + WIDE] = mm(
                    g, wkt[tap * WIDE : (tap + 1) * WIDE, :]
                ).astype(bf16)
            acc[tap] += mm(g_t, rows)
        low[:, c : c + WIDE] = mm(back_sel[:ROW, :], terms[:, c : c + WIDE]).astype(bf16)
        high[:, c : c + WIDE] = mm(back_sel[ROW + n :, :], terms[:, c : c + WIDE]).astype(bf16)
    same = iota((WIDE, WIDE), 0) // channels == iota((WIDE, WIDE), 1) // channels
    fold = jnp.where(iota((WIDE, channels), 0) % channels == iota((WIDE, channels), 1), 1.0, 0.0)
    for tap in range(taps):
        block = jnp.where(same, acc[tap], 0.0)
        block = jnp.sum(block.reshape(WIDE // channels, channels, WIDE), axis=0)
        conv[:, tap * channels : (tap + 1) * channels] = (
            contract(block, fold, 1, 0, precision=lax.Precision.HIGHEST) * scale
        )


def inner_kernel(grad, terms, wkt, back_sel, cot, inner):
    n, width = grad.shape
    for c in range(0, width, WIDE):
        acc = mm(grad[:, c : c + WIDE], wkt[:WIDE, :]) + cot[:, c : c + WIDE].astype(f32)
        inner[:, c : c + WIDE] = acc + mm(back_sel[ROW : ROW + n, :], terms[:, c : c + WIDE])


def shards(columns_in, cotangent, conv_weight, mix_weight, neighbours, rotations, pentagons):
    n, width = columns_in.shape
    taps, channels = conv_weight.shape[:2]
    devices = lax.axis_size("space")
    place = lax.axis_index("space").astype(jnp.int32)
    total_cols = n * devices
    levels = width // channels
    bits = devices.bit_length() - 1

    def ring(value, by):
        return lax.ppermute(value, "space", [(i, (i + by) % devices) for i in range(devices)])

    def swap(value, bit):
        return lax.ppermute(value, "space", [(i, i ^ (1 << bit)) for i in range(devices)])

    below = ring(columns_in, 1)
    above = ring(columns_in, -1)
    pairs = (taps - 1) * n
    up, halo_sel, back_sel, own, pre_own, wk, wkt = call(
        early_kernel,
        [
            ((n, width), f32),
            ((pairs, 2 * ROW), bf16),
            ((n + 2 * ROW, pairs), bf16),
            ((pairs, width), bf16),
            ((n, width), f32),
            ((taps * WIDE, WIDE), bf16),
            ((taps * WIDE, WIDE), bf16),
        ],
        3 << 30,
        jnp.stack([place * n, jnp.int32(total_cols)]),
        neighbours.T,
        rotations[None, :],
        pentagons[None, :],
        columns_in,
        cotangent,
        conv_weight,
        mix_weight,
        scalars=1,
        far=(4, 5, 6, 7),
        scratch=[
            pltpu.VMEM(columns_in.shape, bf16),
            pltpu.VMEM(cotangent.shape, bf16),
            pltpu.VMEM(conv_weight.shape, bf16),
            pltpu.VMEM(mix_weight.shape, bf16),
            pltpu.SemaphoreType.DMA((4,)),
        ],
    )
    mine = jnp.stack([(place >> b) & 1 for b in range(3)])
    halo, pre, act_t, send = call(
        functools.partial(forward_kernel, devices),
        [
            ((pairs, width), bf16),
            ((n, width), f32),
            ((width, n), bf16),
            ((width // 2, width), bf16),
        ],
        3 << 30,
        mine,
        below,
        above,
        halo_sel,
        pre_own,
        wk,
        cotangent,
        scalars=1,
    )
    got = swap(send, 0)
    (keep,) = call(
        functools.partial(keep_kernel, devices),
        [((width // 2, width), f32)],
        1 << 29,
        mine,
        act_t,
        cotangent,
        scalars=1,
    )
    half = width // 2
    merged = call(
        functools.partial(merge_kernel, devices),
        [((width // 4, half), bf16), ((width // 4, half), f32)] * 2,
        1 << 20,
        mine,
        keep,
        got,
        scalars=1,
    )
    grad, terms, to_low, to_high, conv = call(
        functools.partial(backward_kernel, channels, 1.0 / float(total_cols * levels) ** 0.5),
        [
            ((n, width), bf16),
            ((pairs, width), bf16),
            ((ROW, width), bf16),
            ((ROW, width), bf16),
            ((channels, taps * channels), f32),
        ],
        4 << 30,
        up,
        pre,
        columns_in,
        own,
        halo,
        wkt,
        back_sel,
    )
    share = width // devices
    parts = []
    for first in (0, 1):
        order = list(range(1, bits))
        if first:
            order[0], order[1] = order[1], order[0]
        got = swap(merged[2 * first], order[0])
        left = [b for b in range(bits - 1, 0, -1) if b != order[0]]
        parts.append([merged[2 * first + 1], got, left, order])
    for stage in range(2, bits):
        for k, (kept, got, left, order) in enumerate(parts):
            bit = order[stage - 1]
            axis = left.index(bit)
            at = (place >> bit) & 1
            value = (kept + got.astype(f32)).reshape((2,) * len(left) + (share, half))
            sent = lax.dynamic_index_in_dim(value, 1 - at, axis, keepdims=False)
            kept = lax.dynamic_index_in_dim(value, at, axis, keepdims=False)
            flat = (share << (len(left) - 1), half)
            got = swap(sent.astype(bf16).reshape(flat), bit)
            parts[k] = [kept.reshape(flat), got, [b for b in left if b != bit], order]
    grad_mix = jnp.concatenate([p[0] + p[1].astype(f32) for p in parts], axis=1)
    grad_mix = grad_mix / jnp.sqrt(f32(total_cols))

    from_below = ring(to_high, 1)
    from_above = ring(to_low, -1)
    for bit in range(bits):
        conv = conv + swap(conv, bit)
    grad_conv = conv.reshape(channels, taps, channels).transpose(1, 2, 0)
    (inner,) = call(
        inner_kernel, [((n, width), f32)], 1 << 30, grad, terms, wkt, back_sel, cotangent
    )
    grad_input = (inner + from_below.astype(f32) + from_above.astype(f32)).astype(bf16)
    return grad_input, grad_mix, grad_conv


def solution(mesh):
    return jax.shard_map(
        shards,
        mesh=mesh,
        in_specs=(
            P(("group", "space"), None),
            P(("group", "space"), None),
            P(),
            P(),
            P("space", None),
            P("space"),
            P("space"),
        ),
        out_specs=(P(("group", "space"), None), P("space", "group"), P("group", None, None)),
        check_vma=False,
    )
```

```python
import functools

import jax
import jax.numpy as jnp
from jax import lax
from jax.experimental import pallas as pl
from jax.experimental.pallas import tpu as pltpu
from jax.sharding import PartitionSpec as P


ROW = 256
WIDE = 256
TANH_SCALE = 0.7978845608028654
TANH_CUBE = 0.044715


f32 = jnp.float32
bf16 = jnp.bfloat16


def mm(a, b):
    return jnp.dot(a, b, preferred_element_type=f32)


def contract(a, b, dim_a, dim_b, **kw):
    return lax.dot_general(
        a, b, (((dim_a,), (dim_b,)), ((), ())), preferred_element_type=f32, **kw
    )


def iota(shape, dim):
    return lax.broadcasted_iota(jnp.int32, shape, dim)


def onehot(cond):
    return jnp.where(cond, 1.0, 0.0).astype(bf16)


def call(body, outs, cost, *args, scratch=(), scalars=0, far=()):
    space = lambda k: pltpu.SMEM if k < scalars else pltpu.HBM if k in far else pltpu.VMEM
    return pl.pallas_call(
        body,
        out_shape=[jax.ShapeDtypeStruct(s, d) for s, d in outs],
        in_specs=[pl.BlockSpec(memory_space=space(k)) for k in range(len(args))],
        out_specs=[pl.BlockSpec(memory_space=pltpu.VMEM)] * len(outs),
        scratch_shapes=list(scratch),
        cost_estimate=pl.CostEstimate(flops=cost, transcendentals=0, bytes_accessed=8 << 20),
        compiler_params=pltpu.CompilerParams(vmem_limit_bytes=12 << 20),
    )(*args)


def picked(local_t, turns, tap):
    turn = tap - 1 - turns
    slot = 1 + jnp.where(turn < 0, turn + 6, turn)
    source = jnp.full_like(slot, -1)
    for k in range(1, 7):
        source = jnp.where(slot == k, local_t[k : k + 1, :], source)
    return source


def early_kernel(place, near, turns, void, x_hbm, conv_hbm, halo_sel, sources_out, own, wk, x, conv, sems):
    copies = [
        pltpu.make_async_copy(src, dst, sems.at[k])
        for k, (src, dst) in enumerate(((conv_hbm, conv), (x_hbm, x)))
    ]
    for copy in copies:
        copy.start()
    n = x.shape[0]
    taps, c = conv.shape[:2]
    offset, total = place[0], place[1]
    moved = near[...] - offset + ROW
    moved = jnp.where(moved < 0, moved + total, moved)
    moved = jnp.where(moved >= total, moved - total, moved)
    dropped = (void[...] == 1) & (iota((taps, n), 0) == 6)
    local_t = jnp.where(dropped, -1, moved)
    sources = [picked(local_t, turns[...], tap) for tap in range(1, taps)]
    sources_t = jnp.concatenate(sources + [sources[0]] * (8 - len(sources)), axis=0)
    sources_out[...] = sources_t
    eye = jnp.where(iota((n, n), 0) == iota((n, n), 1), 1.0, 0.0)
    columns = contract(eye, sources_t.astype(f32), 1, 1, precision=lax.Precision.HIGHEST)
    columns = columns.astype(jnp.int32)

    copies[0].wait()
    repeat = onehot(iota((c, WIDE), 1) % c == iota((c, WIDE), 0))
    down = onehot(iota((WIDE, c), 0) % c == iota((WIDE, c), 1))
    same = iota((WIDE, WIDE), 0) // c == iota((WIDE, WIDE), 1) // c
    for tap in range(taps):
        wide = mm(conv[tap], repeat).astype(bf16)
        wk[tap * WIDE : (tap + 1) * WIDE, :] = jnp.where(same, mm(down, wide), 0.0).astype(bf16)
    copies[1].wait()
    for tap in range(1, taps):
        at = (tap - 1) * n
        source = columns[:, tap - 1 : tap]
        halo_sel[at : at + n, :ROW] = onehot(iota((n, ROW), 1) == source)
        halo_sel[at : at + n, ROW:] = onehot(iota((n, ROW), 1) + (ROW + n) == source)
        mine = onehot(iota((n, n), 1) + ROW == source)
        own[at : at + n, :] = mm(mine, x[...]).astype(bf16)


def gelu_tanh(v):
    return jnp.tanh(TANH_SCALE * (v + TANH_CUBE * (v * v * v)))


def mix_rows(act_t, cot, bit, share):
    blocks = act_t.shape[0] // share
    rows = [
        act_t[pl.ds(pl.multiple_of((2 * k + bit) * share, share), share), :] for k in range(blocks // 2)
    ]
    return mm(jnp.concatenate(rows, axis=0), cot[...])


def front_kernel(share, me, low, high, halo_sel, own, wk, x, cot, rows_out, pre, act_t, send):
    n, width = pre.shape
    taps = wk.shape[0] // WIDE
    for c in range(0, width, WIDE):
        both = jnp.concatenate([low[:, c : c + WIDE], high[:, c : c + WIDE]], axis=0)
        rows = mm(halo_sel[...], both).astype(bf16) + own[:, c : c + WIDE]
        rows_out[:, c : c + WIDE] = rows
        acc = mm(x[:, c : c + WIDE], wk[:WIDE, :])
        for tap in range(1, taps):
            acc += mm(rows[(tap - 1) * n : tap * n], wk[tap * WIDE : (tap + 1) * WIDE, :])
        pre[:, c : c + WIDE] = acc
        active = (0.5 * acc) * (1.0 + gelu_tanh(acc))
        act_t[c : c + WIDE, :] = active.T.astype(bf16)
    send[...] = mix_rows(act_t, cot, 1 - me[0], share).astype(bf16)


def keep_kernel(share, me, act_t, cot, mix_hbm, keep, up, mix, sem):
    copy = pltpu.make_async_copy(mix_hbm, mix, sem.at[0])
    copy.start()
    keep[...] = mix_rows(act_t, cot, me[0], share)
    copy.wait()
    up[...] = contract(cot[...], mix[...], 1, 1)


def select_rows(sources, start, count, taps):
    n = sources.shape[1]
    return jnp.concatenate(
        [onehot(iota((count, n), 0) + start == sources[tap : tap + 1, :]) for tap in range(taps - 1)], axis=1
    )


def terms_kernel(up, pre, wk, sources, grad, terms, low, high, back_sel):
    n, width = pre.shape
    taps = wk.shape[0] // WIDE
    back_sel[:ROW, :] = select_rows(sources, 0, ROW, taps)
    back_sel[ROW:, :] = select_rows(sources, ROW + n, ROW, taps)
    for c in range(0, width, WIDE):
        v = pre[:, c : c + WIDE]
        t = gelu_tanh(v)
        slope = 0.5 * (1.0 + t) + (0.5 * TANH_SCALE) * v * (1.0 - t * t) * (1.0 + (3 * TANH_CUBE) * (v * v))
        g = (up[:, c : c + WIDE] * slope).astype(bf16)
        grad[:, c : c + WIDE] = g
        for tap in range(1, taps):
            terms[(tap - 1) * n : tap * n, c : c + WIDE] = contract(
                g, wk[tap * WIDE : (tap + 1) * WIDE, :], 1, 1
            ).astype(bf16)
        both = mm(back_sel[...], terms[:, c : c + WIDE]).astype(bf16)
        low[:, c : c + WIDE] = both[:ROW]
        high[:, c : c + WIDE] = both[ROW:]


def weights_kernel(channels, scale, grad, x, rows, conv):
    n, width = grad.shape
    taps = rows.shape[0] // n + 1
    acc = [jnp.zeros((WIDE, WIDE), f32) for _ in range(taps)]
    for c in range(0, width, WIDE):
        g_t = grad[:, c : c + WIDE].astype(f32).T.astype(bf16)
        acc[0] += mm(g_t, x[:, c : c + WIDE])
        for tap in range(1, taps):
            acc[tap] += mm(g_t, rows[(tap - 1) * n : tap * n, c : c + WIDE])
    same = iota((WIDE, WIDE), 0) // channels == iota((WIDE, WIDE), 1) // channels
    fold = jnp.where(iota((channels, WIDE), 1) % channels == iota((channels, WIDE), 0), 1.0, 0.0)
    for tap in range(taps):
        block = jnp.where(same, acc[tap], 0.0)
        block = jnp.sum(block.reshape(WIDE // channels, channels, WIDE), axis=0)
        conv[:, tap * channels : (tap + 1) * channels] = (
            contract(fold, block, 1, 1, precision=lax.Precision.HIGHEST) * scale
        )


def inner_kernel(grad, terms, wk, sources, cot, inner):
    n, width = grad.shape
    taps = wk.shape[0] // WIDE
    sel = select_rows(sources, ROW, n, taps)
    for c in range(0, width, WIDE):
        acc = contract(grad[:, c : c + WIDE], wk[:WIDE, :], 1, 1) + cot[:, c : c + WIDE].astype(f32)
        inner[:, c : c + WIDE] = acc + mm(sel, terms[:, c : c + WIDE])


def halve(share, bit, skip, kept, got, send, keep):
    for q in range(kept.shape[0] // share // 2):
        base = ((q >> skip) << (skip + 1)) | (q & ((1 << skip) - 1))
        for value, out in ((1 - bit, send), (bit, keep)):
            at = pl.ds(pl.multiple_of((base + (value << skip)) * share, share), share)
            out[q * share : (q + 1) * share, :] = (kept[at, :] + got[at, :].astype(f32)).astype(out.dtype)


def split_kernel(share, where, me, keep, got, *outs):
    half = keep.shape[1] // 2
    for k, (bit, skip) in enumerate(where):
        cols = slice(k * half, (k + 1) * half)
        halve(share, me[bit], skip, keep.at[:, cols], got.at[:, cols], outs[2 * k], outs[2 * k + 1])


def merge_kernel(share, where, me, *refs):
    for k, (bit, skip) in enumerate(where):
        halve(share, me[bit], skip, refs[2 * k], refs[2 * k + 1], refs[4 + 2 * k], refs[5 + 2 * k])


def finish_kernel(scale, kept_a, got_a, kept_b, got_b, out):
    half = kept_a.shape[1]
    out[:, :half] = (kept_a[...] + got_a[...].astype(f32)) * scale
    out[:, half:] = (kept_b[...] + got_b[...].astype(f32)) * scale


def total_kernel(inner, first, second, out):
    out[...] = (inner[...] + first[...].astype(f32) + second[...].astype(f32)).astype(bf16)


def shards(columns_in, cotangent, conv_weight, mix_weight, neighbours, rotations, pentagons):
    n, width = columns_in.shape
    taps, channels = conv_weight.shape[:2]
    devices = lax.axis_size("space")
    place = lax.axis_index("space").astype(jnp.int32)
    total_cols = n * devices
    levels = width // channels
    bits = devices.bit_length() - 1

    def ring(value, by):
        return lax.ppermute(value, "space", [(i, (i + by) % devices) for i in range(devices)])

    def swap(value, bit):
        return lax.ppermute(value, "space", [(i, i ^ (1 << bit)) for i in range(devices)])

    below = ring(columns_in, 1)
    above = ring(columns_in, -1)
    pairs = (taps - 1) * n
    share = width // devices
    half = width // 2
    mine = jnp.stack([(place >> b) & 1 for b in range(bits)])
    halo_sel, sources, own, wk = call(
        early_kernel,
        [((pairs, 2 * ROW), bf16), ((8, n), jnp.int32), ((pairs, width), bf16), ((taps * WIDE, WIDE), bf16)],
        1 << 30,
        jnp.stack([place * n, jnp.int32(total_cols)]),
        neighbours.T,
        rotations[None, :],
        pentagons[None, :],
        columns_in,
        conv_weight,
        scalars=1,
        far=(4, 5),
        scratch=[
            pltpu.VMEM(columns_in.shape, bf16),
            pltpu.VMEM(conv_weight.shape, bf16),
            pltpu.SemaphoreType.DMA((2,)),
        ],
    )
    rows, pre, act_t, send = call(
        functools.partial(front_kernel, share),
        [((pairs, width), bf16), ((n, width), f32), ((width, n), bf16), ((half, width), bf16)],
        3 << 30,
        mine,
        below,
        above,
        halo_sel,
        own,
        wk,
        columns_in,
        cotangent,
        scalars=1,
    )
    got = swap(send, 0)
    keep, up = call(
        functools.partial(keep_kernel, share),
        [((half, width), f32), ((n, width), f32)],
        1 << 30,
        mine,
        act_t,
        cotangent,
        mix_weight,
        scalars=1,
        far=(3,),
        scratch=[pltpu.VMEM(mix_weight.shape, bf16), pltpu.SemaphoreType.DMA((1,))],
    )
    orders = [list(range(1, bits)), list(range(2, bits)) + [1]]
    lefts = [list(range(bits - 1, 0, -1)) for _ in orders]

    def places(stage):
        where = []
        for order, left in zip(orders, lefts):
            bit = order[stage]
            where.append((bit, len(left) - 1 - left.index(bit)))
            left.remove(bit)
        return tuple(where)

    rows_left = half // 2
    parts = call(
        functools.partial(split_kernel, share, places(0)),
        [((rows_left, half), bf16), ((rows_left, half), f32)] * 2,
        1 << 20,
        mine,
        keep,
        got,
        scalars=1,
    )
    for stage in range(1, bits):
        gots = []
        for k in (0, 1):
            gots.append(swap(parts[2 * k], orders[k][stage - 1]))
        state = [parts[1], gots[0], parts[3], gots[1]]
        if stage < bits - 1:
            rows_left //= 2
            parts = call(
                functools.partial(merge_kernel, share, places(stage)),
                [((rows_left, half), bf16), ((rows_left, half), f32)] * 2,
                1 << 20,
                mine,
                *state,
                scalars=1,
            )
    (grad_mix,) = call(
        functools.partial(finish_kernel, 1.0 / float(total_cols) ** 0.5),
        [((share, width), f32)],
        1 << 20,
        *state,
    )
    grad, terms, to_low, to_high = call(
        terms_kernel,
        [((n, width), bf16), ((pairs, width), bf16), ((ROW, width), bf16), ((ROW, width), bf16)],
        3 << 30,
        up,
        pre,
        wk,
        sources,
        scratch=[pltpu.VMEM((2 * ROW, pairs), bf16)],
    )
    from_below = ring(to_high, 1)
    from_above = ring(to_low, -1)
    (conv,) = call(
        functools.partial(weights_kernel, channels, 1.0 / float(total_cols * levels) ** 0.5),
        [((channels, taps * channels), f32)],
        1 << 30,
        grad,
        columns_in,
        rows,
    )
    for bit in [0] + orders[1]:
        conv = conv + swap(conv, bit)
    grad_conv = conv.reshape(channels, taps, channels).transpose(1, 0, 2)
    (inner,) = call(inner_kernel, [((n, width), f32)], 1 << 30, grad, terms, wk, sources, cotangent)
    (grad_input,) = call(total_kernel, [((n, width), bf16)], 1 << 20, inner, from_below, from_above)
    return grad_input, grad_mix, grad_conv


def solution(mesh):
    return jax.shard_map(
        shards,
        mesh=mesh,
        in_specs=(
            P(("group", "space"), None),
            P(("group", "space"), None),
            P(),
            P(),
            P("space", None),
            P("space"),
            P("space"),
        ),
        out_specs=(P(("group", "space"), None), P("space", "group"), P("group", None, None)),
        check_vma=False,
    )
```

```python
import functools

import jax
import jax.numpy as jnp
from jax import lax
from jax.experimental import pallas as pl
from jax.experimental.pallas import tpu as pltpu
from jax.sharding import PartitionSpec as P


ROW = 256
WIDE = 256
TANH_SCALE = 0.7978845608028654
TANH_CUBE = 0.044715


f32 = jnp.float32
bf16 = jnp.bfloat16


def mm(a, b):
    return jnp.dot(a, b, preferred_element_type=f32)


def contract(a, b, dim_a, dim_b, **kw):
    return lax.dot_general(
        a, b, (((dim_a,), (dim_b,)), ((), ())), preferred_element_type=f32, **kw
    )


def iota(shape, dim):
    return lax.broadcasted_iota(jnp.int32, shape, dim)


def onehot(cond):
    return jnp.where(cond, 1.0, 0.0).astype(bf16)


def call(body, outs, cost, *args, scratch=(), scalars=0, far=()):
    space = lambda k: pltpu.SMEM if k < scalars else pltpu.HBM if k in far else pltpu.VMEM
    return pl.pallas_call(
        body,
        out_shape=[jax.ShapeDtypeStruct(s, d) for s, d in outs],
        in_specs=[pl.BlockSpec(memory_space=space(k)) for k in range(len(args))],
        out_specs=[pl.BlockSpec(memory_space=pltpu.VMEM)] * len(outs),
        scratch_shapes=list(scratch),
        cost_estimate=pl.CostEstimate(flops=cost, transcendentals=0, bytes_accessed=8 << 20),
        compiler_params=pltpu.CompilerParams(vmem_limit_bytes=12 << 20),
    )(*args)


def picked(local_t, turns, tap):
    turn = tap - 1 - turns
    slot = 1 + jnp.where(turn < 0, turn + 6, turn)
    source = jnp.full_like(slot, -1)
    for k in range(1, 7):
        source = jnp.where(slot == k, local_t[k : k + 1, :], source)
    return source


def early_kernel(place, near, turns, void, x_hbm, conv_hbm, halo_sel, sources_out, own, wk, x, conv, sems):
    copies = [
        pltpu.make_async_copy(src, dst, sems.at[k])
        for k, (src, dst) in enumerate(((conv_hbm, conv), (x_hbm, x)))
    ]
    for copy in copies:
        copy.start()
    n = x.shape[0]
    taps, c = conv.shape[:2]
    offset, total = place[0], place[1]
    moved = near[...] - offset + ROW
    moved = jnp.where(moved < 0, moved + total, moved)
    moved = jnp.where(moved >= total, moved - total, moved)
    dropped = (void[...] == 1) & (iota((taps, n), 0) == 6)
    local_t = jnp.where(dropped, -1, moved)
    sources = [picked(local_t, turns[...], tap) for tap in range(1, taps)]
    sources_t = jnp.concatenate(sources + [sources[0]] * (8 - len(sources)), axis=0)
    sources_out[...] = sources_t
    eye = jnp.where(iota((n, n), 0) == iota((n, n), 1), 1.0, 0.0)
    columns = contract(eye, sources_t.astype(f32), 1, 1, precision=lax.Precision.HIGHEST)
    columns = columns.astype(jnp.int32)

    copies[0].wait()
    repeat = onehot(iota((c, WIDE), 1) % c == iota((c, WIDE), 0))
    down = onehot(iota((WIDE, c), 0) % c == iota((WIDE, c), 1))
    same = iota((WIDE, WIDE), 0) // c == iota((WIDE, WIDE), 1) // c
    for tap in range(taps):
        wide = mm(conv[tap], repeat).astype(bf16)
        wk[tap * WIDE : (tap + 1) * WIDE, :] = jnp.where(same, mm(down, wide), 0.0).astype(bf16)
    copies[1].wait()
    for tap in range(1, taps):
        at = (tap - 1) * n
        source = columns[:, tap - 1 : tap]
        halo_sel[at : at + n, :ROW] = onehot(iota((n, ROW), 1) == source)
        halo_sel[at : at + n, ROW:] = onehot(iota((n, ROW), 1) + (ROW + n) == source)
        mine = onehot(iota((n, n), 1) + ROW == source)
        own[at : at + n, :] = mm(mine, x[...]).astype(bf16)


def gelu_tanh(v):
    return jnp.tanh(TANH_SCALE * (v + TANH_CUBE * (v * v * v)))


def mix_rows(act_t, cot, bit, share):
    blocks = act_t.shape[0] // share
    rows = [
        act_t[pl.ds(pl.multiple_of((2 * k + bit) * share, share), share), :] for k in range(blocks // 2)
    ]
    return mm(jnp.concatenate(rows, axis=0), cot[...])


def front_kernel(share, me, low, high, halo_sel, own, wk, x, cot, rows_out, pre, act_t, send):
    n, width = pre.shape
    taps = wk.shape[0] // WIDE
    for c in range(0, width, WIDE):
        both = jnp.concatenate([low[:, c : c + WIDE], high[:, c : c + WIDE]], axis=0)
        rows = mm(halo_sel[...], both).astype(bf16) + own[:, c : c + WIDE]
        rows_out[:, c : c + WIDE] = rows
        acc = mm(x[:, c : c + WIDE], wk[:WIDE, :])
        for tap in range(1, taps):
            acc += mm(rows[(tap - 1) * n : tap * n], wk[tap * WIDE : (tap + 1) * WIDE, :])
        pre[:, c : c + WIDE] = acc
        active = (0.5 * acc) * (1.0 + gelu_tanh(acc))
        act_t[c : c + WIDE, :] = active.T.astype(bf16)
    send[...] = mix_rows(act_t, cot, 1 - me[0], share).astype(bf16)


def keep_kernel(share, me, act_t, cot, mix_hbm, keep, up, mix, sem):
    copy = pltpu.make_async_copy(mix_hbm, mix, sem.at[0])
    copy.start()
    keep[...] = mix_rows(act_t, cot, me[0], share)
    copy.wait()
    up[...] = contract(cot[...], mix[...], 1, 1)


def select_rows(sources, start, count, taps):
    n = sources.shape[1]
    return jnp.concatenate(
        [onehot(iota((count, n), 0) + start == sources[tap : tap + 1, :]) for tap in range(taps - 1)], axis=1
    )


def weights_kernel(channels, scale, up, pre, x, rows, grad, conv):
    n, width = grad.shape
    taps = rows.shape[0] // n + 1
    acc = [jnp.zeros((WIDE, WIDE), f32) for _ in range(taps)]
    for c in range(0, width, WIDE):
        v = pre[:, c : c + WIDE]
        t = gelu_tanh(v)
        slope = 0.5 * (1.0 + t) + (0.5 * TANH_SCALE) * v * (1.0 - t * t) * (1.0 + (3 * TANH_CUBE) * (v * v))
        g = up[:, c : c + WIDE] * slope
        grad[:, c : c + WIDE] = g.astype(bf16)
        g_t = g.T.astype(bf16)
        acc[0] += mm(g_t, x[:, c : c + WIDE])
        for tap in range(1, taps):
            acc[tap] += mm(g_t, rows[(tap - 1) * n : tap * n, c : c + WIDE])
    same = iota((WIDE, WIDE), 0) // channels == iota((WIDE, WIDE), 1) // channels
    conv[...] = jnp.zeros(conv.shape, f32)
    fold = jnp.where(iota((channels, WIDE), 1) % channels == iota((channels, WIDE), 0), 1.0, 0.0)
    for tap in range(taps):
        block = jnp.where(same, acc[tap], 0.0)
        block = jnp.sum(block.reshape(WIDE // channels, channels, WIDE), axis=0)
        conv[:, tap * channels : (tap + 1) * channels] = (
            contract(fold, block, 1, 1, precision=lax.Precision.HIGHEST) * scale
        )


def terms_kernel(grad, wk, sources, terms, low, high, back_sel):
    n, width = grad.shape
    taps = wk.shape[0] // WIDE
    back_sel[:ROW, :] = select_rows(sources, 0, ROW, taps)
    back_sel[ROW:, :] = select_rows(sources, ROW + n, ROW, taps)
    for c in range(0, width, WIDE):
        g = grad[:, c : c + WIDE]
        for tap in range(1, taps):
            terms[(tap - 1) * n : tap * n, c : c + WIDE] = contract(
                g, wk[tap * WIDE : (tap + 1) * WIDE, :], 1, 1
            ).astype(bf16)
        both = mm(back_sel[...], terms[:, c : c + WIDE]).astype(bf16)
        low[:, c : c + WIDE] = both[:ROW]
        high[:, c : c + WIDE] = both[ROW:]


def inner_kernel(grad, terms, wk, sources, cot, inner):
    n, width = grad.shape
    taps = wk.shape[0] // WIDE
    sel = select_rows(sources, ROW, n, taps)
    for c in range(0, width, WIDE):
        acc = contract(grad[:, c : c + WIDE], wk[:WIDE, :], 1, 1) + cot[:, c : c + WIDE].astype(f32)
        inner[:, c : c + WIDE] = acc + mm(sel, terms[:, c : c + WIDE])


def halve(share, bit, skip, kept, got, got_at, send, send_at, keep):
    for q in range(kept.shape[0] // share // 2):
        base = ((q >> skip) << (skip + 1)) | (q & ((1 << skip) - 1))
        for value, out, out_at in ((1 - bit, send, send_at), (bit, keep, 0)):
            at = pl.multiple_of((base + (value << skip)) * share, share)
            came = got[pl.ds(pl.multiple_of(at + got_at, 16), share), :].astype(f32)
            out[out_at + q * share : out_at + (q + 1) * share, :] = (
                kept[pl.ds(at, share), :] + came
            ).astype(out.dtype)


def split_kernel(share, where, me, keep, got, *outs):
    half = keep.shape[1] // 2
    for k, (bit, skip) in enumerate(where):
        cols = slice(k * half, (k + 1) * half)
        halve(share, me[bit], skip, keep.at[:, cols], got.at[:, cols], 0, outs[2 * k], 0, outs[2 * k + 1])


def parcel(ref):
    return ref[:16, :128].astype(f32) + ref[:16, 128:256].astype(f32)


def merge_kernel(share, where, first, me, kept_a, got_a, kept_b, got_b, conv, conv_got, send_a, keep_a, send_b, keep_b, conv_out):
    whole = conv[...] + (conv_got[...] if first else parcel(got_a))
    high = whole.astype(bf16)
    low = (whole - high.astype(f32)).astype(bf16)
    conv_out[...] = high.astype(f32) + low.astype(f32)
    send_a[:16, :] = jnp.zeros((16, send_a.shape[1]), bf16)
    send_a[:16, :128] = high
    send_a[:16, 128:256] = low
    (bit_a, skip_a), (bit_b, skip_b) = where
    halve(share, me[bit_a], skip_a, kept_a, got_a, 0 if first else 16, send_a, 16, keep_a)
    halve(share, me[bit_b], skip_b, kept_b, got_b, 0, send_b, 0, keep_b)


def last_kernel(scale, channels, kept_a, got_a, kept_b, got_b, conv, inner, first, second, mix_out, conv_out, grad_out):
    half = kept_a.shape[1]
    mix_out[:, :half] = (kept_a[...] + got_a[16:, :].astype(f32)) * scale
    mix_out[:, half:] = (kept_b[...] + got_b[...].astype(f32)) * scale
    whole = conv[...] + parcel(got_a)
    for tap in range(conv_out.shape[0]):
        conv_out[tap] = whole[:, tap * channels : (tap + 1) * channels]
    grad_out[...] = (inner[...] + first[...].astype(f32) + second[...].astype(f32)).astype(bf16)


def shards(columns_in, cotangent, conv_weight, mix_weight, neighbours, rotations, pentagons):
    n, width = columns_in.shape
    taps, channels = conv_weight.shape[:2]
    devices = lax.axis_size("space")
    place = lax.axis_index("space").astype(jnp.int32)
    total_cols = n * devices
    levels = width // channels
    bits = devices.bit_length() - 1

    def ring(value, by):
        return lax.ppermute(value, "space", [(i, (i + by) % devices) for i in range(devices)])

    def swap(value, bit):
        return lax.ppermute(value, "space", [(i, i ^ (1 << bit)) for i in range(devices)])

    below = ring(columns_in, 1)
    above = ring(columns_in, -1)
    pairs = (taps - 1) * n
    share = width // devices
    half = width // 2
    mine = jnp.stack([(place >> b) & 1 for b in range(bits)])
    halo_sel, sources, own, wk = call(
        early_kernel,
        [((pairs, 2 * ROW), bf16), ((8, n), jnp.int32), ((pairs, width), bf16), ((taps * WIDE, WIDE), bf16)],
        1 << 30,
        jnp.stack([place * n, jnp.int32(total_cols)]),
        neighbours.T,
        rotations[None, :],
        pentagons[None, :],
        columns_in,
        conv_weight,
        scalars=1,
        far=(4, 5),
        scratch=[
            pltpu.VMEM(columns_in.shape, bf16),
            pltpu.VMEM(conv_weight.shape, bf16),
            pltpu.SemaphoreType.DMA((2,)),
        ],
    )
    rows, pre, act_t, send = call(
        functools.partial(front_kernel, share),
        [((pairs, width), bf16), ((n, width), f32), ((width, n), bf16), ((half, width), bf16)],
        3 << 30,
        mine,
        below,
        above,
        halo_sel,
        own,
        wk,
        columns_in,
        cotangent,
        scalars=1,
    )
    got = swap(send, 0)
    keep, up = call(
        functools.partial(keep_kernel, share),
        [((half, width), f32), ((n, width), f32)],
        1 << 30,
        mine,
        act_t,
        cotangent,
        mix_weight,
        scalars=1,
        far=(3,),
        scratch=[pltpu.VMEM(mix_weight.shape, bf16), pltpu.SemaphoreType.DMA((1,))],
    )
    orders = [list(range(1, bits)), list(range(2, bits)) + [1]]
    lefts = [list(range(bits - 1, 0, -1)) for _ in orders]

    def places(stage):
        where = []
        for order, left in zip(orders, lefts):
            bit = order[stage]
            where.append((bit, len(left) - 1 - left.index(bit)))
            left.remove(bit)
        return tuple(where)

    rows_left = half // 2
    parts = call(
        functools.partial(split_kernel, share, places(0)),
        [((rows_left, half), bf16), ((rows_left, half), f32)] * 2,
        1 << 20,
        mine,
        keep,
        got,
        scalars=1,
    )
    grad, conv = call(
        functools.partial(weights_kernel, channels, 1.0 / float(total_cols * levels) ** 0.5),
        [((n, width), bf16), ((channels, 128), f32)],
        2 << 30,
        up,
        pre,
        columns_in,
        rows,
    )
    terms, to_low, to_high = call(
        terms_kernel,
        [((pairs, width), bf16), ((ROW, width), bf16), ((ROW, width), bf16)],
        3 << 30,
        grad,
        wk,
        sources,
        scratch=[pltpu.VMEM((2 * ROW, pairs), bf16)],
    )
    conv = conv + swap(conv, 0)
    conv_got = swap(conv, 1)
    from_below = ring(to_high, 1)
    from_above = ring(to_low, -1)
    for stage in range(1, bits):
        gots = []
        for k in (0, 1):
            gots.append(swap(parts[2 * k], orders[k][stage - 1]))
        state = [parts[1], gots[0], parts[3], gots[1]]
        if stage < bits - 1:
            rows_left //= 2
            *parts, conv = call(
                functools.partial(merge_kernel, share, places(stage), stage == 1),
                [
                    ((rows_left + 16, half), bf16),
                    ((rows_left, half), f32),
                    ((rows_left, half), bf16),
                    ((rows_left, half), f32),
                    ((channels, 128), f32),
                ],
                1 << 20,
                mine,
                *state,
                conv,
                conv_got,
                scalars=1,
            )
    (inner,) = call(
        inner_kernel, [((n, width), f32)], 1 << 30, grad, terms, wk, sources, cotangent
    )
    grad_mix, grad_conv, grad_input = call(
        functools.partial(last_kernel, 1.0 / float(total_cols) ** 0.5, channels),
        [((share, width), f32), ((taps, channels, channels), f32), ((n, width), bf16)],
        1 << 20,
        *state,
        conv,
        inner,
        from_below,
        from_above,
    )
    return grad_input, grad_mix, grad_conv


def solution(mesh):
    return jax.shard_map(
        shards,
        mesh=mesh,
        in_specs=(
            P(("group", "space"), None),
            P(("group", "space"), None),
            P(),
            P(),
            P("space", None),
            P("space"),
            P("space"),
        ),
        out_specs=(P(("group", "space"), None), P("space", "group"), P("group", None, None)),
        check_vma=False,
    )
```

```python
import functools

import jax
import jax.numpy as jnp
from jax import lax
from jax.experimental import pallas as pl
from jax.experimental.pallas import tpu as pltpu
from jax.sharding import PartitionSpec as P


ROW = 256
WIDE = 256
TANH_SCALE = 0.7978845608028654
TANH_CUBE = 0.044715


f32 = jnp.float32
bf16 = jnp.bfloat16


def mm(a, b):
    return jnp.dot(a, b, preferred_element_type=f32)


def contract(a, b, dim_a, dim_b, **kw):
    return lax.dot_general(
        a, b, (((dim_a,), (dim_b,)), ((), ())), preferred_element_type=f32, **kw
    )


def iota(shape, dim):
    return lax.broadcasted_iota(jnp.int32, shape, dim)


def onehot(cond):
    return jnp.where(cond, 1.0, 0.0).astype(bf16)


def call(body, outs, cost, *args, scratch=(), scalars=0, far=()):
    space = lambda k: pltpu.SMEM if k < scalars else pltpu.HBM if k in far else pltpu.VMEM
    return pl.pallas_call(
        body,
        out_shape=[jax.ShapeDtypeStruct(s, d) for s, d in outs],
        in_specs=[pl.BlockSpec(memory_space=space(k)) for k in range(len(args))],
        out_specs=[pl.BlockSpec(memory_space=pltpu.VMEM)] * len(outs),
        scratch_shapes=list(scratch),
        cost_estimate=pl.CostEstimate(flops=cost, transcendentals=0, bytes_accessed=8 << 20),
        compiler_params=pltpu.CompilerParams(vmem_limit_bytes=12 << 20),
    )(*args)


def picked(local_t, turns, tap):
    turn = tap - 1 - turns
    slot = 1 + jnp.where(turn < 0, turn + 6, turn)
    source = jnp.full_like(slot, -1)
    for k in range(1, 7):
        source = jnp.where(slot == k, local_t[k : k + 1, :], source)
    return source


def early_kernel(place, near, turns, void, x_hbm, conv_hbm, halo_sel, sources_out, own, wk, x, conv, sems):
    copies = [
        pltpu.make_async_copy(src, dst, sems.at[k])
        for k, (src, dst) in enumerate(((conv_hbm, conv), (x_hbm, x)))
    ]
    for copy in copies:
        copy.start()
    n = x.shape[0]
    taps, c = conv.shape[:2]
    offset, total = place[0], place[1]
    moved = near[...] - offset + ROW
    moved = jnp.where(moved < 0, moved + total, moved)
    moved = jnp.where(moved >= total, moved - total, moved)
    dropped = (void[...] == 1) & (iota((taps, n), 0) == 6)
    local_t = jnp.where(dropped, -1, moved)
    sources = [picked(local_t, turns[...], tap) for tap in range(1, taps)]
    sources_t = jnp.concatenate(sources + [sources[0]] * (8 - len(sources)), axis=0)
    sources_out[...] = sources_t
    eye = jnp.where(iota((n, n), 0) == iota((n, n), 1), 1.0, 0.0)
    columns = contract(eye, sources_t.astype(f32), 1, 1, precision=lax.Precision.HIGHEST)
    columns = columns.astype(jnp.int32)

    copies[0].wait()
    repeat = onehot(iota((c, WIDE), 1) % c == iota((c, WIDE), 0))
    down = onehot(iota((WIDE, c), 0) % c == iota((WIDE, c), 1))
    same = iota((WIDE, WIDE), 0) // c == iota((WIDE, WIDE), 1) // c
    for tap in range(taps):
        wide = mm(conv[tap], repeat).astype(bf16)
        wk[tap * WIDE : (tap + 1) * WIDE, :] = jnp.where(same, mm(down, wide), 0.0).astype(bf16)
    copies[1].wait()
    for tap in range(1, taps):
        at = (tap - 1) * n
        source = columns[:, tap - 1 : tap]
        halo_sel[at : at + n, :ROW] = onehot(iota((n, ROW), 1) == source)
        halo_sel[at : at + n, ROW:] = onehot(iota((n, ROW), 1) + (ROW + n) == source)
        mine = onehot(iota((n, n), 1) + ROW == source)
        own[at : at + n, :] = mm(mine, x[...]).astype(bf16)


def gelu_tanh(v):
    return jnp.tanh(TANH_SCALE * (v + TANH_CUBE * (v * v * v)))


def mix_rows(act_t, cot, bit, share):
    blocks = act_t.shape[0] // share
    rows = [
        act_t[pl.ds(pl.multiple_of((2 * k + bit) * share, share), share), :] for k in range(blocks // 2)
    ]
    return mm(jnp.concatenate(rows, axis=0), cot[...])


def front_kernel(share, me, low, high, halo_sel, own, wk, x, cot, rows_out, pre, act_t, send):
    n, width = pre.shape
    taps = wk.shape[0] // WIDE
    for c in range(0, width, WIDE):
        both = jnp.concatenate([low[:, c : c + WIDE], high[:, c : c + WIDE]], axis=0)
        rows = mm(halo_sel[...], both).astype(bf16) + own[:, c : c + WIDE]
        rows_out[:, c : c + WIDE] = rows
        acc = mm(x[:, c : c + WIDE], wk[:WIDE, :])
        for tap in range(1, taps):
            acc += mm(rows[(tap - 1) * n : tap * n], wk[tap * WIDE : (tap + 1) * WIDE, :])
        pre[:, c : c + WIDE] = acc
        active = (0.5 * acc) * (1.0 + gelu_tanh(acc))
        act_t[c : c + WIDE, :] = active.T.astype(bf16)
    send[...] = mix_rows(act_t, cot, 1 - me[0], share).astype(bf16)


def keep_kernel(share, me, act_t, cot, mix_hbm, keep, up, mix, sem):
    copy = pltpu.make_async_copy(mix_hbm, mix, sem.at[0])
    copy.start()
    keep[...] = mix_rows(act_t, cot, me[0], share)
    copy.wait()
    up[...] = contract(cot[...], mix[...], 1, 1)


def select_rows(sources, start, count, taps):
    n = sources.shape[1]
    return jnp.concatenate(
        [onehot(iota((count, n), 0) + start == sources[tap : tap + 1, :]) for tap in range(taps - 1)], axis=1
    )


def weights_kernel(channels, scale, up, pre, x, rows, grad, conv):
    n, width = grad.shape
    taps = rows.shape[0] // n + 1
    acc = [jnp.zeros((WIDE, WIDE), f32) for _ in range(taps)]
    for c in range(0, width, WIDE):
        v = pre[:, c : c + WIDE]
        t = gelu_tanh(v)
        slope = 0.5 * (1.0 + t) + (0.5 * TANH_SCALE) * v * (1.0 - t * t) * (1.0 + (3 * TANH_CUBE) * (v * v))
        g = up[:, c : c + WIDE] * slope
        grad[:, c : c + WIDE] = g.astype(bf16)
        g_t = g.T.astype(bf16)
        acc[0] += mm(g_t, x[:, c : c + WIDE])
        for tap in range(1, taps):
            acc[tap] += mm(g_t, rows[(tap - 1) * n : tap * n, c : c + WIDE])
    same = iota((WIDE, WIDE), 0) // channels == iota((WIDE, WIDE), 1) // channels
    conv[...] = jnp.zeros(conv.shape, f32)
    fold = jnp.where(iota((channels, WIDE), 1) % channels == iota((channels, WIDE), 0), 1.0, 0.0)
    for tap in range(taps):
        block = jnp.where(same, acc[tap], 0.0)
        block = jnp.sum(block.reshape(WIDE // channels, channels, WIDE), axis=0)
        conv[:, tap * channels : (tap + 1) * channels] = (
            contract(fold, block, 1, 1, precision=lax.Precision.HIGHEST) * scale
        )


def terms_kernel(grad, wk, sources, terms, low, high, back_sel):
    n, width = grad.shape
    taps = wk.shape[0] // WIDE
    back_sel[:ROW, :] = select_rows(sources, 0, ROW, taps)
    back_sel[ROW:, :] = select_rows(sources, ROW + n, ROW, taps)
    for c in range(0, width, WIDE):
        g = grad[:, c : c + WIDE]
        for tap in range(1, taps):
            terms[(tap - 1) * n : tap * n, c : c + WIDE] = contract(
                g, wk[tap * WIDE : (tap + 1) * WIDE, :], 1, 1
            ).astype(bf16)
        both = mm(back_sel[...], terms[:, c : c + WIDE]).astype(bf16)
        low[:, c : c + WIDE] = both[:ROW]
        high[:, c : c + WIDE] = both[ROW:]


def inner_kernel(grad, terms, wk, sources, cot, inner):
    n, width = grad.shape
    taps = wk.shape[0] // WIDE
    sel = select_rows(sources, ROW, n, taps)
    for c in range(0, width, WIDE):
        acc = contract(grad[:, c : c + WIDE], wk[:WIDE, :], 1, 1) + cot[:, c : c + WIDE].astype(f32)
        inner[:, c : c + WIDE] = acc + mm(sel, terms[:, c : c + WIDE])


def halve(share, bit, skip, kept, got, got_at, send, send_at, keep):
    for q in range(kept.shape[0] // share // 2):
        base = ((q >> skip) << (skip + 1)) | (q & ((1 << skip) - 1))
        for value, out, out_at in ((1 - bit, send, send_at), (bit, keep, 0)):
            at = pl.multiple_of((base + (value << skip)) * share, share)
            came = got[pl.ds(pl.multiple_of(at + got_at, 16), share), :].astype(f32)
            out[out_at + q * share : out_at + (q + 1) * share, :] = (
                kept[pl.ds(at, share), :] + came
            ).astype(out.dtype)


def split_kernel(share, where, me, keep, got, *outs):
    half = keep.shape[1] // 2
    for k, (bit, skip) in enumerate(where):
        cols = slice(k * half, (k + 1) * half)
        halve(share, me[bit], skip, keep.at[:, cols], got.at[:, cols], 0, outs[2 * k], 0, outs[2 * k + 1])


def parcel(ref):
    return ref[:16, :128].astype(f32) + ref[:16, 128:256].astype(f32)


def conv_sum(conv, gots):
    one, two, three = [parcel(got) for got in gots]
    return (conv[...] + one) + (two + three)


def quarter(share, bits, skips, kept, gots, got_at, sends, send_at, keep):
    (lo, hi), (bit_lo, bit_hi) = skips, bits
    small, large = min(lo, hi), max(lo, hi)
    for q in range(kept.shape[0] // share // 4):
        base = ((q >> small) << (small + 1)) | (q & ((1 << small) - 1))
        base = ((base >> large) << (large + 1)) | (base & ((1 << large) - 1))
        for delta in range(4):
            out, out_at = (keep, 0) if delta == 0 else (sends[delta - 1], send_at)
            want_lo = 1 - bit_lo if delta & 1 else bit_lo
            want_hi = 1 - bit_hi if delta & 2 else bit_hi
            at = pl.multiple_of((base + (want_lo << lo) + (want_hi << hi)) * share, share)
            value = kept[pl.ds(at, share), :]
            for got in gots:
                value += got[pl.ds(pl.multiple_of(at + got_at, 16), share), :].astype(f32)
            out[out_at + q * share : out_at + (q + 1) * share, :] = value.astype(out.dtype)


def quad_kernel(share, where, came, me, *refs):
    first = came == 1
    kept_a, gots_a, kept_b, gots_b = refs[0], refs[1 : 1 + came], refs[1 + came], refs[2 + came : 2 + 2 * came]
    rest = refs[2 + 2 * came :]
    if first:
        whole = rest[0][...] + rest[1][...]
        rest = rest[2:]
    else:
        whole = conv_sum(rest[0], gots_a)
        rest = rest[1:]
    sends_a, keep_a, sends_b, keep_b, conv_out = rest[:3], rest[3], rest[4:7], rest[7], rest[8]
    high = whole.astype(bf16)
    low = (whole - high.astype(f32)).astype(bf16)
    conv_out[...] = high.astype(f32) + low.astype(f32)
    for send in sends_a:
        send[:16, :] = jnp.zeros((16, send.shape[1]), bf16)
        send[:16, :128] = high
        send[:16, 128:256] = low
    (bits_a, skips_a), (bits_b, skips_b) = where
    chosen = lambda bits: (me[bits[0]], me[bits[1]])
    quarter(share, chosen(bits_a), skips_a, kept_a, gots_a, 0 if first else 16, sends_a, 16, keep_a)
    quarter(share, chosen(bits_b), skips_b, kept_b, gots_b, 0, sends_b, 0, keep_b)


def last_kernel(scale, channels, *refs):
    kept_a, gots_a, kept_b, gots_b = refs[0], refs[1:4], refs[4], refs[5:8]
    conv, inner, first, second, mix_out, conv_out, grad_out = refs[8:]
    half = kept_a.shape[1]
    total = kept_a[...]
    for got in gots_a:
        total += got[16:, :].astype(f32)
    mix_out[:, :half] = total * scale
    total = kept_b[...]
    for got in gots_b:
        total += got[...].astype(f32)
    mix_out[:, half:] = total * scale
    whole = conv_sum(conv, gots_a)
    for tap in range(conv_out.shape[0]):
        conv_out[tap] = whole[:, tap * channels : (tap + 1) * channels]
    grad_out[...] = (inner[...] + first[...].astype(f32) + second[...].astype(f32)).astype(bf16)


def shards(columns_in, cotangent, conv_weight, mix_weight, neighbours, rotations, pentagons):
    n, width = columns_in.shape
    taps, channels = conv_weight.shape[:2]
    devices = lax.axis_size("space")
    place = lax.axis_index("space").astype(jnp.int32)
    total_cols = n * devices
    levels = width // channels
    bits = devices.bit_length() - 1

    def ring(value, by):
        return lax.ppermute(value, "space", [(i, (i + by) % devices) for i in range(devices)])

    def swap_by(value, mask):
        return lax.ppermute(value, "space", [(i, i ^ mask) for i in range(devices)])

    def swap(value, bit):
        return swap_by(value, 1 << bit)

    below = ring(columns_in, 1)
    above = ring(columns_in, -1)
    pairs = (taps - 1) * n
    share = width // devices
    half = width // 2
    mine = jnp.stack([(place >> b) & 1 for b in range(bits)])
    halo_sel, sources, own, wk = call(
        early_kernel,
        [((pairs, 2 * ROW), bf16), ((8, n), jnp.int32), ((pairs, width), bf16), ((taps * WIDE, WIDE), bf16)],
        1 << 30,
        jnp.stack([place * n, jnp.int32(total_cols)]),
        neighbours.T,
        rotations[None, :],
        pentagons[None, :],
        columns_in,
        conv_weight,
        scalars=1,
        far=(4, 5),
        scratch=[
            pltpu.VMEM(columns_in.shape, bf16),
            pltpu.VMEM(conv_weight.shape, bf16),
            pltpu.SemaphoreType.DMA((2,)),
        ],
    )
    rows, pre, act_t, send = call(
        functools.partial(front_kernel, share),
        [((pairs, width), bf16), ((n, width), f32), ((width, n), bf16), ((half, width), bf16)],
        3 << 30,
        mine,
        below,
        above,
        halo_sel,
        own,
        wk,
        columns_in,
        cotangent,
        scalars=1,
    )
    got = swap(send, 0)
    keep, up = call(
        functools.partial(keep_kernel, share),
        [((half, width), f32), ((n, width), f32)],
        1 << 30,
        mine,
        act_t,
        cotangent,
        mix_weight,
        scalars=1,
        far=(3,),
        scratch=[pltpu.VMEM(mix_weight.shape, bf16), pltpu.SemaphoreType.DMA((1,))],
    )
    orders = [list(range(1, bits)), list(range(2, bits)) + [1]]
    lefts = [list(range(bits - 1, 0, -1)) for _ in orders]

    def position(k, bit):
        return len(lefts[k]) - 1 - lefts[k].index(bit)

    def drop(k, *gone):
        lefts[k] = [b for b in lefts[k] if b not in gone]

    rows_left = half // 2
    parts = call(
        functools.partial(
            split_kernel, share, tuple((order[0], position(k, order[0])) for k, order in enumerate(orders))
        ),
        [((rows_left, half), bf16), ((rows_left, half), f32)] * 2,
        1 << 20,
        mine,
        keep,
        got,
        scalars=1,
    )
    kept, gots = [parts[1], parts[3]], []
    for k in (0, 1):
        gots.append([swap(parts[2 * k], orders[k][0])])
        drop(k, orders[k][0])
    grad, conv = call(
        functools.partial(weights_kernel, channels, 1.0 / float(total_cols * levels) ** 0.5),
        [((n, width), bf16), ((channels, 128), f32)],
        2 << 30,
        up,
        pre,
        columns_in,
        rows,
    )
    terms, to_low, to_high = call(
        terms_kernel,
        [((pairs, width), bf16), ((ROW, width), bf16), ((ROW, width), bf16)],
        3 << 30,
        grad,
        wk,
        sources,
        scratch=[pltpu.VMEM((2 * ROW, pairs), bf16)],
    )
    conv = conv + swap(conv, 0)
    conv_got = swap(conv, 1)
    from_below = ring(to_high, 1)
    from_above = ring(to_low, -1)
    for stage in range(1, bits - 1, 2):
        rows_left //= 4
        pair = [order[stage : stage + 2] for order in orders]
        where = tuple((tuple(p), tuple(position(k, b) for b in p)) for k, p in enumerate(pair))
        outs = call(
            functools.partial(quad_kernel, share, where, len(gots[0])),
            [((rows_left + 16, half), bf16)] * 3
            + [((rows_left, half), f32)]
            + [((rows_left, half), bf16)] * 3
            + [((rows_left, half), f32), ((channels, 128), f32)],
            1 << 20,
            mine,
            kept[0],
            *gots[0],
            kept[1],
            *gots[1],
            conv,
            *([conv_got] if stage == 1 else []),
            scalars=1,
        )
        kept, conv = [outs[3], outs[7]], outs[8]
        gots = []
        for k in (0, 1):
            came = []
            for delta in (1, 2, 3):
                came.append(swap_by(outs[4 * k + delta - 1], ((delta & 1) << pair[k][0]) | ((delta >> 1) << pair[k][1])))
            gots.append(came)
            drop(k, *pair[k])
    (inner,) = call(
        inner_kernel, [((n, width), f32)], 1 << 30, grad, terms, wk, sources, cotangent
    )
    grad_mix, grad_conv, grad_input = call(
        functools.partial(last_kernel, 1.0 / float(total_cols) ** 0.5, channels),
        [((share, width), f32), ((taps, channels, channels), f32), ((n, width), bf16)],
        1 << 20,
        kept[0],
        *gots[0],
        kept[1],
        *gots[1],
        conv,
        inner,
        from_below,
        from_above,
    )
    return grad_input, grad_mix, grad_conv


def solution(mesh):
    return jax.shard_map(
        shards,
        mesh=mesh,
        in_specs=(
            P(("group", "space"), None),
            P(("group", "space"), None),
            P(),
            P(),
            P("space", None),
            P("space"),
            P("space"),
        ),
        out_specs=(P(("group", "space"), None), P("space", "group"), P("group", None, None)),
        check_vma=False,
    )
```

```python
import functools

import jax
import jax.numpy as jnp
from jax import lax
from jax.experimental import pallas as pl
from jax.experimental.pallas import tpu as pltpu
from jax.sharding import PartitionSpec as P


ROW = 256
WIDE = 256
TANH_SCALE = 0.7978845608028654
TANH_CUBE = 0.044715


f32 = jnp.float32
bf16 = jnp.bfloat16


def mm(a, b):
    return jnp.dot(a, b, preferred_element_type=f32)


def contract(a, b, dim_a, dim_b, **kw):
    return lax.dot_general(
        a, b, (((dim_a,), (dim_b,)), ((), ())), preferred_element_type=f32, **kw
    )


def iota(shape, dim):
    return lax.broadcasted_iota(jnp.int32, shape, dim)


def onehot(cond):
    return jnp.where(cond, 1.0, 0.0).astype(bf16)


def call(body, outs, cost, *args, scratch=(), scalars=0, far=()):
    space = lambda k: pltpu.SMEM if k < scalars else pltpu.HBM if k in far else pltpu.VMEM
    return pl.pallas_call(
        body,
        out_shape=[jax.ShapeDtypeStruct(s, d) for s, d in outs],
        in_specs=[pl.BlockSpec(memory_space=space(k)) for k in range(len(args))],
        out_specs=[pl.BlockSpec(memory_space=pltpu.VMEM)] * len(outs),
        scratch_shapes=list(scratch),
        cost_estimate=pl.CostEstimate(flops=cost, transcendentals=0, bytes_accessed=8 << 20),
        compiler_params=pltpu.CompilerParams(vmem_limit_bytes=12 << 20),
    )(*args)


def picked(local_t, turns, tap):
    turn = tap - 1 - turns
    slot = 1 + jnp.where(turn < 0, turn + 6, turn)
    source = jnp.full_like(slot, -1)
    for k in range(1, 7):
        source = jnp.where(slot == k, local_t[k : k + 1, :], source)
    return source


def early_kernel(place, near, turns, void, x_hbm, conv_hbm, halo_sel, sources_out, own, wk, x, conv, sems):
    copies = [
        pltpu.make_async_copy(src, dst, sems.at[k])
        for k, (src, dst) in enumerate(((conv_hbm, conv), (x_hbm, x)))
    ]
    for copy in copies:
        copy.start()
    n = x.shape[0]
    taps, c = conv.shape[:2]
    offset, total = place[0], place[1]
    moved = near[...] - offset + ROW
    moved = jnp.where(moved < 0, moved + total, moved)
    moved = jnp.where(moved >= total, moved - total, moved)
    dropped = (void[...] == 1) & (iota((taps, n), 0) == 6)
    local_t = jnp.where(dropped, -1, moved)
    sources = [picked(local_t, turns[...], tap) for tap in range(1, taps)]
    sources_t = jnp.concatenate(sources + [sources[0]] * (8 - len(sources)), axis=0)
    sources_out[...] = sources_t
    eye = jnp.where(iota((n, n), 0) == iota((n, n), 1), 1.0, 0.0)
    columns = contract(eye, sources_t.astype(f32), 1, 1, precision=lax.Precision.HIGHEST)
    columns = columns.astype(jnp.int32)

    copies[0].wait()
    repeat = onehot(iota((c, WIDE), 1) % c == iota((c, WIDE), 0))
    down = onehot(iota((WIDE, c), 0) % c == iota((WIDE, c), 1))
    same = iota((WIDE, WIDE), 0) // c == iota((WIDE, WIDE), 1) // c
    for tap in range(taps):
        wide = mm(conv[tap], repeat).astype(bf16)
        wk[tap * WIDE : (tap + 1) * WIDE, :] = jnp.where(same, mm(down, wide), 0.0).astype(bf16)
    copies[1].wait()
    for tap in range(1, taps):
        at = (tap - 1) * n
        source = columns[:, tap - 1 : tap]
        halo_sel[at : at + n, :ROW] = onehot(iota((n, ROW), 1) == source)
        halo_sel[at : at + n, ROW:] = onehot(iota((n, ROW), 1) + (ROW + n) == source)
        mine = onehot(iota((n, n), 1) + ROW == source)
        own[at : at + n, :] = mm(mine, x[...]).astype(bf16)


def gelu_tanh(v):
    return jnp.tanh(TANH_SCALE * (v + TANH_CUBE * (v * v * v)))


def front_kernel(share, me, low, high, halo_sel, own, wk, x, rows_out, pre, act_keep, act_send, act_t):
    n, width = pre.shape
    taps = wk.shape[0] // WIDE
    for c in range(0, width, WIDE):
        both = jnp.concatenate([low[:, c : c + WIDE], high[:, c : c + WIDE]], axis=0)
        rows = mm(halo_sel[...], both).astype(bf16) + own[:, c : c + WIDE]
        rows_out[:, c : c + WIDE] = rows
        acc = mm(x[:, c : c + WIDE], wk[:WIDE, :])
        for tap in range(1, taps):
            acc += mm(rows[(tap - 1) * n : tap * n], wk[tap * WIDE : (tap + 1) * WIDE, :])
        pre[:, c : c + WIDE] = acc
        active = (0.5 * acc) * (1.0 + gelu_tanh(acc))
        act_t[c : c + WIDE, :] = active.T.astype(bf16)
    for k in range(width // share // 2):
        for bit, out in ((me[0], act_keep), (1 - me[0], act_send)):
            at = pl.multiple_of((2 * k + bit) * share, share)
            out[k * share : (k + 1) * share, :] = act_t[pl.ds(at, share), :]


def up_kernel(cot, mix, up):
    up[...] = contract(cot[...], mix[...], 1, 1)


def mix_kernel(share, where, me, act, act_got, cot, cot_got, *outs):
    half = cot.shape[1] // 2
    blocks = act.shape[0] // share
    for k, (bit, skip) in enumerate(where):
        cols = slice(k * half, (k + 1) * half)
        both = jnp.concatenate([cot[:, cols], cot_got[:, cols]], axis=0)
        for want, out in ((1 - me[bit], outs[2 * k]), (me[bit], outs[2 * k + 1])):
            pieces = []
            for q in range(blocks // 2):
                base = ((q >> skip) << (skip + 1)) | (q & ((1 << skip) - 1))
                at = pl.ds(pl.multiple_of((base + (want << skip)) * share, share), share)
                pieces.append(jnp.concatenate([act[at, :], act_got[at, :]], axis=1))
            out[...] = mm(jnp.concatenate(pieces, axis=0), both).astype(out.dtype)


def select_rows(sources, start, count, taps):
    n = sources.shape[1]
    return jnp.concatenate(
        [onehot(iota((count, n), 0) + start == sources[tap : tap + 1, :]) for tap in range(taps - 1)], axis=1
    )


def weights_kernel(channels, scale, up, pre, x, rows, grad, conv):
    n, width = grad.shape
    taps = rows.shape[0] // n + 1
    acc = [jnp.zeros((WIDE, WIDE), f32) for _ in range(taps)]
    for c in range(0, width, WIDE):
        v = pre[:, c : c + WIDE]
        t = gelu_tanh(v)
        slope = 0.5 * (1.0 + t) + (0.5 * TANH_SCALE) * v * (1.0 - t * t) * (1.0 + (3 * TANH_CUBE) * (v * v))
        g = up[:, c : c + WIDE] * slope
        grad[:, c : c + WIDE] = g.astype(bf16)
        g_t = g.T.astype(bf16)
        acc[0] += mm(g_t, x[:, c : c + WIDE])
        for tap in range(1, taps):
            acc[tap] += mm(g_t, rows[(tap - 1) * n : tap * n, c : c + WIDE])
    same = iota((WIDE, WIDE), 0) // channels == iota((WIDE, WIDE), 1) // channels
    conv[...] = jnp.zeros(conv.shape, f32)
    fold = jnp.where(iota((channels, WIDE), 1) % channels == iota((channels, WIDE), 0), 1.0, 0.0)
    for tap in range(taps):
        block = jnp.where(same, acc[tap], 0.0)
        block = jnp.sum(block.reshape(WIDE // channels, channels, WIDE), axis=0)
        conv[:, tap * channels : (tap + 1) * channels] = (
            contract(fold, block, 1, 1, precision=lax.Precision.HIGHEST) * scale
        )


def terms_kernel(grad, wk, sources, terms, low, high, back_sel):
    n, width = grad.shape
    taps = wk.shape[0] // WIDE
    back_sel[:ROW, :] = select_rows(sources, 0, ROW, taps)
    back_sel[ROW:, :] = select_rows(sources, ROW + n, ROW, taps)
    for c in range(0, width, WIDE):
        g = grad[:, c : c + WIDE]
        for tap in range(1, taps):
            terms[(tap - 1) * n : tap * n, c : c + WIDE] = contract(
                g, wk[tap * WIDE : (tap + 1) * WIDE, :], 1, 1
            ).astype(bf16)
        both = mm(back_sel[...], terms[:, c : c + WIDE]).astype(bf16)
        low[:, c : c + WIDE] = both[:ROW]
        high[:, c : c + WIDE] = both[ROW:]


def inner_kernel(grad, terms, wk, sources, cot, inner):
    n, width = grad.shape
    taps = wk.shape[0] // WIDE
    sel = select_rows(sources, ROW, n, taps)
    for c in range(0, width, WIDE):
        acc = contract(grad[:, c : c + WIDE], wk[:WIDE, :], 1, 1) + cot[:, c : c + WIDE].astype(f32)
        inner[:, c : c + WIDE] = acc + mm(sel, terms[:, c : c + WIDE])


def parcel(ref):
    return ref[:16, :128].astype(f32) + ref[:16, 128:256].astype(f32)


def conv_sum(conv, gots):
    one, two, three = [parcel(got) for got in gots]
    return (conv[...] + one) + (two + three)


def quarter(share, bits, skips, kept, gots, got_at, sends, send_at, keep):
    (lo, hi), (bit_lo, bit_hi) = skips, bits
    small, large = min(lo, hi), max(lo, hi)
    for q in range(kept.shape[0] // share // 4):
        base = ((q >> small) << (small + 1)) | (q & ((1 << small) - 1))
        base = ((base >> large) << (large + 1)) | (base & ((1 << large) - 1))
        for delta in range(4):
            out, out_at = (keep, 0) if delta == 0 else (sends[delta - 1], send_at)
            want_lo = 1 - bit_lo if delta & 1 else bit_lo
            want_hi = 1 - bit_hi if delta & 2 else bit_hi
            at = pl.multiple_of((base + (want_lo << lo) + (want_hi << hi)) * share, share)
            value = kept[pl.ds(at, share), :]
            for got in gots:
                value += got[pl.ds(pl.multiple_of(at + got_at, 16), share), :].astype(f32)
            out[out_at + q * share : out_at + (q + 1) * share, :] = value.astype(out.dtype)


def quad_kernel(share, where, came, me, *refs):
    first = came == 1
    kept_a, gots_a, kept_b, gots_b = refs[0], refs[1 : 1 + came], refs[1 + came], refs[2 + came : 2 + 2 * came]
    rest = refs[2 + 2 * came :]
    if first:
        whole = rest[0][...] + rest[1][...]
        rest = rest[2:]
    else:
        whole = conv_sum(rest[0], gots_a)
        rest = rest[1:]
    sends_a, keep_a, sends_b, keep_b, conv_out = rest[:3], rest[3], rest[4:7], rest[7], rest[8]
    high = whole.astype(bf16)
    low = (whole - high.astype(f32)).astype(bf16)
    conv_out[...] = high.astype(f32) + low.astype(f32)
    for send in sends_a:
        send[:16, :] = jnp.zeros((16, send.shape[1]), bf16)
        send[:16, :128] = high
        send[:16, 128:256] = low
    (bits_a, skips_a), (bits_b, skips_b) = where
    chosen = lambda bits: (me[bits[0]], me[bits[1]])
    quarter(share, chosen(bits_a), skips_a, kept_a, gots_a, 0 if first else 16, sends_a, 16, keep_a)
    quarter(share, chosen(bits_b), skips_b, kept_b, gots_b, 0, sends_b, 0, keep_b)


def last_kernel(scale, channels, *refs):
    kept_a, gots_a, kept_b, gots_b = refs[0], refs[1:4], refs[4], refs[5:8]
    conv, inner, first, second, mix_out, conv_out, grad_out = refs[8:]
    half = kept_a.shape[1]
    total = kept_a[...]
    for got in gots_a:
        total += got[16:, :].astype(f32)
    mix_out[:, :half] = total * scale
    total = kept_b[...]
    for got in gots_b:
        total += got[...].astype(f32)
    mix_out[:, half:] = total * scale
    whole = conv_sum(conv, gots_a)
    for tap in range(conv_out.shape[0]):
        conv_out[tap] = whole[:, tap * channels : (tap + 1) * channels]
    grad_out[...] = (inner[...] + first[...].astype(f32) + second[...].astype(f32)).astype(bf16)


def shards(columns_in, cotangent, conv_weight, mix_weight, neighbours, rotations, pentagons):
    n, width = columns_in.shape
    taps, channels = conv_weight.shape[:2]
    devices = lax.axis_size("space")
    place = lax.axis_index("space").astype(jnp.int32)
    total_cols = n * devices
    levels = width // channels
    bits = devices.bit_length() - 1

    def ring(value, by):
        return lax.ppermute(value, "space", [(i, (i + by) % devices) for i in range(devices)])

    def swap_by(value, mask):
        return lax.ppermute(value, "space", [(i, i ^ mask) for i in range(devices)])

    def swap(value, bit):
        return swap_by(value, 1 << bit)

    below = ring(columns_in, 1)
    above = ring(columns_in, -1)
    cot_got = swap(cotangent, 0)
    pairs = (taps - 1) * n
    share = width // devices
    half = width // 2
    mine = jnp.stack([(place >> b) & 1 for b in range(bits)])
    halo_sel, sources, own, wk = call(
        early_kernel,
        [((pairs, 2 * ROW), bf16), ((8, n), jnp.int32), ((pairs, width), bf16), ((taps * WIDE, WIDE), bf16)],
        1 << 30,
        jnp.stack([place * n, jnp.int32(total_cols)]),
        neighbours.T,
        rotations[None, :],
        pentagons[None, :],
        columns_in,
        conv_weight,
        scalars=1,
        far=(4, 5),
        scratch=[
            pltpu.VMEM(columns_in.shape, bf16),
            pltpu.VMEM(conv_weight.shape, bf16),
            pltpu.SemaphoreType.DMA((2,)),
        ],
    )
    (up,) = call(up_kernel, [((n, width), f32)], 1 << 29, cotangent, mix_weight)
    rows, pre, act, act_send = call(
        functools.partial(front_kernel, share),
        [((pairs, width), bf16), ((n, width), f32), ((half, n), bf16), ((half, n), bf16)],
        3 << 30,
        mine,
        below,
        above,
        halo_sel,
        own,
        wk,
        columns_in,
        scalars=1,
        scratch=[pltpu.VMEM((width, n), bf16)],
    )
    act_got = swap(act_send, 0)
    orders = [list(range(1, bits)), list(range(2, bits)) + [1]]
    lefts = [list(range(bits - 1, 0, -1)) for _ in orders]

    def position(k, bit):
        return len(lefts[k]) - 1 - lefts[k].index(bit)

    def drop(k, *gone):
        lefts[k] = [b for b in lefts[k] if b not in gone]

    rows_left = half // 2
    parts = call(
        functools.partial(
            mix_kernel, share, tuple((order[0], position(k, order[0])) for k, order in enumerate(orders))
        ),
        [((rows_left, half), bf16), ((rows_left, half), f32)] * 2,
        1 << 30,
        mine,
        act,
        act_got,
        cotangent,
        cot_got,
        scalars=1,
    )
    kept, gots = [parts[1], parts[3]], []
    for k in (0, 1):
        gots.append([swap(parts[2 * k], orders[k][0])])
        drop(k, orders[k][0])
    grad, conv = call(
        functools.partial(weights_kernel, channels, 1.0 / float(total_cols * levels) ** 0.5),
        [((n, width), bf16), ((channels, 128), f32)],
        2 << 30,
        up,
        pre,
        columns_in,
        rows,
    )
    terms, to_low, to_high = call(
        terms_kernel,
        [((pairs, width), bf16), ((ROW, width), bf16), ((ROW, width), bf16)],
        3 << 30,
        grad,
        wk,
        sources,
        scratch=[pltpu.VMEM((2 * ROW, pairs), bf16)],
    )
    conv = conv + swap(conv, 0)
    conv_got = swap(conv, 1)
    from_below = ring(to_high, 1)
    from_above = ring(to_low, -1)
    for stage in range(1, bits - 1, 2):
        rows_left //= 4
        pair = [order[stage : stage + 2] for order in orders]
        where = tuple((tuple(p), tuple(position(k, b) for b in p)) for k, p in enumerate(pair))
        outs = call(
            functools.partial(quad_kernel, share, where, len(gots[0])),
            [((rows_left + 16, half), bf16)] * 3
            + [((rows_left, half), f32)]
            + [((rows_left, half), bf16)] * 3
            + [((rows_left, half), f32), ((channels, 128), f32)],
            1 << 20,
            mine,
            kept[0],
            *gots[0],
            kept[1],
            *gots[1],
            conv,
            *([conv_got] if stage == 1 else []),
            scalars=1,
        )
        kept, conv = [outs[3], outs[7]], outs[8]
        gots = []
        for k in (0, 1):
            came = []
            for delta in (1, 2, 3):
                came.append(swap_by(outs[4 * k + delta - 1], ((delta & 1) << pair[k][0]) | ((delta >> 1) << pair[k][1])))
            gots.append(came)
            drop(k, *pair[k])
    (inner,) = call(
        inner_kernel, [((n, width), f32)], 1 << 30, grad, terms, wk, sources, cotangent
    )
    grad_mix, grad_conv, grad_input = call(
        functools.partial(last_kernel, 1.0 / float(total_cols) ** 0.5, channels),
        [((share, width), f32), ((taps, channels, channels), f32), ((n, width), bf16)],
        1 << 20,
        kept[0],
        *gots[0],
        kept[1],
        *gots[1],
        conv,
        inner,
        from_below,
        from_above,
    )
    return grad_input, grad_mix, grad_conv


def solution(mesh):
    return jax.shard_map(
        shards,
        mesh=mesh,
        in_specs=(
            P(("group", "space"), None),
            P(("group", "space"), None),
            P(),
            P(),
            P("space", None),
            P("space"),
            P("space"),
        ),
        out_specs=(P(("group", "space"), None), P("space", "group"), P("group", None, None)),
        check_vma=False,
    )
```

```python
import functools

import jax
import jax.numpy as jnp
from jax import lax
from jax.experimental import pallas as pl
from jax.experimental.pallas import tpu as pltpu
from jax.sharding import PartitionSpec as P


ROW = 256
WIDE = 256
TANH_SCALE = 0.7978845608028654
TANH_CUBE = 0.044715


f32 = jnp.float32
bf16 = jnp.bfloat16


def mm(a, b):
    return jnp.dot(a, b, preferred_element_type=f32)


def contract(a, b, dim_a, dim_b, **kw):
    return lax.dot_general(
        a, b, (((dim_a,), (dim_b,)), ((), ())), preferred_element_type=f32, **kw
    )


def iota(shape, dim):
    return lax.broadcasted_iota(jnp.int32, shape, dim)


def onehot(cond):
    return jnp.where(cond, 1.0, 0.0).astype(bf16)


def call(body, outs, cost, *args, scratch=(), scalars=0, far=()):
    space = lambda k: pltpu.SMEM if k < scalars else pltpu.HBM if k in far else pltpu.VMEM
    return pl.pallas_call(
        body,
        out_shape=[jax.ShapeDtypeStruct(s, d) for s, d in outs],
        in_specs=[pl.BlockSpec(memory_space=space(k)) for k in range(len(args))],
        out_specs=[pl.BlockSpec(memory_space=pltpu.VMEM)] * len(outs),
        scratch_shapes=list(scratch),
        cost_estimate=pl.CostEstimate(flops=cost, transcendentals=0, bytes_accessed=8 << 20),
        compiler_params=pltpu.CompilerParams(vmem_limit_bytes=12 << 20),
    )(*args)


def picked(local_t, turns, tap):
    turn = tap - 1 - turns
    slot = 1 + jnp.where(turn < 0, turn + 6, turn)
    source = jnp.full_like(slot, -1)
    for k in range(1, 7):
        source = jnp.where(slot == k, local_t[k : k + 1, :], source)
    return source


def early_kernel(place, near, turns, void, x_hbm, conv_hbm, halo_sel, sources_out, own, wk, x, conv, sems):
    copies = [
        pltpu.make_async_copy(src, dst, sems.at[k])
        for k, (src, dst) in enumerate(((conv_hbm, conv), (x_hbm, x)))
    ]
    for copy in copies:
        copy.start()
    n = x.shape[0]
    taps, c = conv.shape[:2]
    offset, total = place[0], place[1]
    base_far, base_near = place[2], place[3]
    moved = near[...] - offset + ROW
    moved = jnp.where(moved < 0, moved + total, moved)
    moved = jnp.where(moved >= total, moved - total, moved)
    dropped = (void[...] == 1) & (iota((taps, n), 0) == 6)
    local_t = jnp.where(dropped, -1, moved)
    sources = [picked(local_t, turns[...], tap) for tap in range(1, taps)]
    sources_t = jnp.concatenate(sources + [sources[0]] * (8 - len(sources)), axis=0)
    sources_out[...] = sources_t
    eye = jnp.where(iota((n, n), 0) == iota((n, n), 1), 1.0, 0.0)
    columns = contract(eye, sources_t.astype(f32), 1, 1, precision=lax.Precision.HIGHEST)
    columns = columns.astype(jnp.int32)

    copies[0].wait()
    repeat = onehot(iota((c, WIDE), 1) % c == iota((c, WIDE), 0))
    down = onehot(iota((WIDE, c), 0) % c == iota((WIDE, c), 1))
    same = iota((WIDE, WIDE), 0) // c == iota((WIDE, WIDE), 1) // c
    for tap in range(taps):
        wide = mm(conv[tap], repeat).astype(bf16)
        wk[tap * WIDE : (tap + 1) * WIDE, :] = jnp.where(same, mm(down, wide), 0.0).astype(bf16)
    copies[1].wait()
    for tap in range(1, taps):
        at = (tap - 1) * n
        source = columns[:, tap - 1 : tap]
        halo_sel[at : at + n, :ROW] = onehot(iota((n, ROW), 1) == source - base_far)
        halo_sel[at : at + n, ROW:] = onehot(iota((n, ROW), 1) == source - base_near)
        mine = onehot(iota((n, n), 1) + ROW == source)
        own[at : at + n, :] = mm(mine, x[...]).astype(bf16)


def gelu_tanh(v):
    return jnp.tanh(TANH_SCALE * (v + TANH_CUBE * (v * v * v)))


def front_kernel(share, me, far, near, halo_sel, own, wk, x, rows_out, pre, act_keep, act_send, act_t):
    n, width = pre.shape
    taps = wk.shape[0] // WIDE
    for c in range(0, width, WIDE):
        both = jnp.concatenate([far[:, c : c + WIDE], near[:, c : c + WIDE]], axis=0)
        rows = mm(halo_sel[...], both).astype(bf16) + own[:, c : c + WIDE]
        rows_out[:, c : c + WIDE] = rows
        acc = mm(x[:, c : c + WIDE], wk[:WIDE, :])
        for tap in range(1, taps):
            acc += mm(rows[(tap - 1) * n : tap * n], wk[tap * WIDE : (tap + 1) * WIDE, :])
        pre[:, c : c + WIDE] = acc
        active = (0.5 * acc) * (1.0 + gelu_tanh(acc))
        act_t[c : c + WIDE, :] = active.T.astype(bf16)
    for k in range(width // share // 2):
        for bit, out in ((me[0], act_keep), (1 - me[0], act_send)):
            at = pl.multiple_of((2 * k + bit) * share, share)
            out[k * share : (k + 1) * share, :] = act_t[pl.ds(at, share), :]


def up_kernel(cot, mix, up):
    up[...] = contract(cot[...], mix[...], 1, 1)


def mix_kernel(share, where, me, act, act_got, cot, cot_got, *outs):
    half = cot.shape[1] // 2
    blocks = act.shape[0] // share
    for k, (bit, skip) in enumerate(where):
        cols = slice(k * half, (k + 1) * half)
        both = jnp.concatenate([cot[:, cols], cot_got[:, cols]], axis=0)
        for want, out in ((1 - me[bit], outs[2 * k]), (me[bit], outs[2 * k + 1])):
            pieces = []
            for q in range(blocks // 2):
                base = ((q >> skip) << (skip + 1)) | (q & ((1 << skip) - 1))
                at = pl.ds(pl.multiple_of((base + (want << skip)) * share, share), share)
                pieces.append(jnp.concatenate([act[at, :], act_got[at, :]], axis=1))
            out[...] = mm(jnp.concatenate(pieces, axis=0), both).astype(out.dtype)


def select_rows(sources, start, count, taps):
    n = sources.shape[1]
    return jnp.concatenate(
        [onehot(iota((count, n), 0) == sources[tap : tap + 1, :] - start) for tap in range(taps - 1)], axis=1
    )


def weights_kernel(channels, scale, up, pre, x, rows, grad, conv):
    n, width = grad.shape
    taps = rows.shape[0] // n + 1
    acc = [jnp.zeros((WIDE, WIDE), f32) for _ in range(taps)]
    for c in range(0, width, WIDE):
        v = pre[:, c : c + WIDE]
        t = gelu_tanh(v)
        slope = 0.5 * (1.0 + t) + (0.5 * TANH_SCALE) * v * (1.0 - t * t) * (1.0 + (3 * TANH_CUBE) * (v * v))
        g = up[:, c : c + WIDE] * slope
        grad[:, c : c + WIDE] = g.astype(bf16)
        g_t = g.T.astype(bf16)
        acc[0] += mm(g_t, x[:, c : c + WIDE])
        for tap in range(1, taps):
            acc[tap] += mm(g_t, rows[(tap - 1) * n : tap * n, c : c + WIDE])
    same = iota((WIDE, WIDE), 0) // channels == iota((WIDE, WIDE), 1) // channels
    conv[...] = jnp.zeros(conv.shape, f32)
    fold = jnp.where(iota((channels, WIDE), 1) % channels == iota((channels, WIDE), 0), 1.0, 0.0)
    for tap in range(taps):
        block = jnp.where(same, acc[tap], 0.0)
        block = jnp.sum(block.reshape(WIDE // channels, channels, WIDE), axis=0)
        conv[:, tap * channels : (tap + 1) * channels] = (
            contract(fold, block, 1, 1, precision=lax.Precision.HIGHEST) * scale
        )


def terms_kernel(place, grad, wk, sources, terms, far, near, back_sel):
    n, width = grad.shape
    taps = wk.shape[0] // WIDE
    back_sel[:ROW, :] = select_rows(sources, place[2], ROW, taps)
    back_sel[ROW:, :] = select_rows(sources, place[3], ROW, taps)
    for c in range(0, width, WIDE):
        g = grad[:, c : c + WIDE]
        for tap in range(1, taps):
            terms[(tap - 1) * n : tap * n, c : c + WIDE] = contract(
                g, wk[tap * WIDE : (tap + 1) * WIDE, :], 1, 1
            ).astype(bf16)
        both = mm(back_sel[...], terms[:, c : c + WIDE]).astype(bf16)
        far[:, c : c + WIDE] = both[:ROW]
        near[:, c : c + WIDE] = both[ROW:]


def inner_kernel(grad, terms, wk, sources, cot, inner):
    n, width = grad.shape
    taps = wk.shape[0] // WIDE
    sel = select_rows(sources, ROW, n, taps)
    for c in range(0, width, WIDE):
        acc = contract(grad[:, c : c + WIDE], wk[:WIDE, :], 1, 1) + cot[:, c : c + WIDE].astype(f32)
        inner[:, c : c + WIDE] = acc + mm(sel, terms[:, c : c + WIDE])


def parcel(ref):
    return ref[:16, :128].astype(f32) + ref[:16, 128:256].astype(f32)


def conv_sum(conv, gots):
    one, two, three = [parcel(got) for got in gots]
    return (conv[...] + one) + (two + three)


def quarter(share, bits, skips, kept, gots, got_at, sends, send_at, keep):
    (lo, hi), (bit_lo, bit_hi) = skips, bits
    small, large = min(lo, hi), max(lo, hi)
    for q in range(kept.shape[0] // share // 4):
        base = ((q >> small) << (small + 1)) | (q & ((1 << small) - 1))
        base = ((base >> large) << (large + 1)) | (base & ((1 << large) - 1))
        for delta in range(4):
            out, out_at = (keep, 0) if delta == 0 else (sends[delta - 1], send_at)
            want_lo = 1 - bit_lo if delta & 1 else bit_lo
            want_hi = 1 - bit_hi if delta & 2 else bit_hi
            at = pl.multiple_of((base + (want_lo << lo) + (want_hi << hi)) * share, share)
            value = kept[pl.ds(at, share), :]
            for got in gots:
                value += got[pl.ds(pl.multiple_of(at + got_at, 16), share), :].astype(f32)
            out[out_at + q * share : out_at + (q + 1) * share, :] = value.astype(out.dtype)


def quad_kernel(share, where, came, me, *refs):
    first = came == 1
    kept_a, gots_a, kept_b, gots_b = refs[0], refs[1 : 1 + came], refs[1 + came], refs[2 + came : 2 + 2 * came]
    rest = refs[2 + 2 * came :]
    if first:
        whole = rest[0][...] + rest[1][...]
        rest = rest[2:]
    else:
        whole = conv_sum(rest[0], gots_a)
        rest = rest[1:]
    sends_a, keep_a, sends_b, keep_b, conv_out = rest[:3], rest[3], rest[4:7], rest[7], rest[8]
    high = whole.astype(bf16)
    low = (whole - high.astype(f32)).astype(bf16)
    conv_out[...] = high.astype(f32) + low.astype(f32)
    for send in sends_a:
        send[:16, :] = jnp.zeros((16, send.shape[1]), bf16)
        send[:16, :128] = high
        send[:16, 128:256] = low
    (bits_a, skips_a), (bits_b, skips_b) = where
    chosen = lambda bits: (me[bits[0]], me[bits[1]])
    quarter(share, chosen(bits_a), skips_a, kept_a, gots_a, 0 if first else 16, sends_a, 16, keep_a)
    quarter(share, chosen(bits_b), skips_b, kept_b, gots_b, 0, sends_b, 0, keep_b)


def last_kernel(scale, channels, *refs):
    kept_a, gots_a, kept_b, gots_b = refs[0], refs[1:4], refs[4], refs[5:8]
    conv, inner, first, second, mix_out, conv_out, grad_out = refs[8:]
    half = kept_a.shape[1]
    total = kept_a[...]
    for got in gots_a:
        total += got[16:, :].astype(f32)
    mix_out[:, :half] = total * scale
    total = kept_b[...]
    for got in gots_b:
        total += got[...].astype(f32)
    mix_out[:, half:] = total * scale
    whole = conv_sum(conv, gots_a)
    for tap in range(conv_out.shape[0]):
        conv_out[tap] = whole[:, tap * channels : (tap + 1) * channels]
    grad_out[...] = (inner[...] + first[...].astype(f32) + second[...].astype(f32)).astype(bf16)


def shards(columns_in, cotangent, conv_weight, mix_weight, neighbours, rotations, pentagons):
    n, width = columns_in.shape
    taps, channels = conv_weight.shape[:2]
    devices = lax.axis_size("space")
    place = lax.axis_index("space").astype(jnp.int32)
    total_cols = n * devices
    levels = width // channels
    bits = devices.bit_length() - 1

    def near_swap(value):
        return lax.ppermute(value, "space", [(i, i ^ 1) for i in range(devices)])

    def far_swap(value):
        other = lambda i: (i + 1 if i % 2 else i - 1) % devices
        return lax.ppermute(value, "space", [(i, other(i)) for i in range(devices)])

    def swap_by(value, mask):
        return lax.ppermute(value, "space", [(i, i ^ mask) for i in range(devices)])

    def swap(value, bit):
        return swap_by(value, 1 << bit)

    far = far_swap(columns_in)
    near = near_swap(columns_in)
    odd = place & 1
    spots = jnp.stack([place * n, jnp.int32(total_cols), odd * (ROW + n), (1 - odd) * (ROW + n)])
    cot_got = swap(cotangent, 0)
    pairs = (taps - 1) * n
    share = width // devices
    half = width // 2
    mine = jnp.stack([(place >> b) & 1 for b in range(bits)])
    halo_sel, sources, own, wk = call(
        early_kernel,
        [((pairs, 2 * ROW), bf16), ((8, n), jnp.int32), ((pairs, width), bf16), ((taps * WIDE, WIDE), bf16)],
        1 << 30,
        spots,
        neighbours.T,
        rotations[None, :],
        pentagons[None, :],
        columns_in,
        conv_weight,
        scalars=1,
        far=(4, 5),
        scratch=[
            pltpu.VMEM(columns_in.shape, bf16),
            pltpu.VMEM(conv_weight.shape, bf16),
            pltpu.SemaphoreType.DMA((2,)),
        ],
    )
    (up,) = call(up_kernel, [((n, width), f32)], 1 << 29, cotangent, mix_weight)
    rows, pre, act, act_send = call(
        functools.partial(front_kernel, share),
        [((pairs, width), bf16), ((n, width), f32), ((half, n), bf16), ((half, n), bf16)],
        3 << 30,
        mine,
        far,
        near,
        halo_sel,
        own,
        wk,
        columns_in,
        scalars=1,
        scratch=[pltpu.VMEM((width, n), bf16)],
    )
    act_got = swap(act_send, 0)
    orders = [list(range(1, bits)), list(range(2, bits)) + [1]]
    lefts = [list(range(bits - 1, 0, -1)) for _ in orders]

    def position(k, bit):
        return len(lefts[k]) - 1 - lefts[k].index(bit)

    def drop(k, *gone):
        lefts[k] = [b for b in lefts[k] if b not in gone]

    rows_left = half // 2
    parts = call(
        functools.partial(
            mix_kernel, share, tuple((order[0], position(k, order[0])) for k, order in enumerate(orders))
        ),
        [((rows_left, half), bf16), ((rows_left, half), f32)] * 2,
        1 << 30,
        mine,
        act,
        act_got,
        cotangent,
        cot_got,
        scalars=1,
    )
    kept, gots = [parts[1], parts[3]], []
    for k in (0, 1):
        gots.append([swap(parts[2 * k], orders[k][0])])
        drop(k, orders[k][0])
    grad, conv = call(
        functools.partial(weights_kernel, channels, 1.0 / float(total_cols * levels) ** 0.5),
        [((n, width), bf16), ((channels, 128), f32)],
        2 << 30,
        up,
        pre,
        columns_in,
        rows,
    )
    terms, to_far, to_near = call(
        terms_kernel,
        [((pairs, width), bf16), ((ROW, width), bf16), ((ROW, width), bf16)],
        3 << 30,
        spots,
        grad,
        wk,
        sources,
        scalars=1,
        scratch=[pltpu.VMEM((2 * ROW, pairs), bf16)],
    )
    conv = conv + swap(conv, 0)
    conv_got = swap(conv, 1)
    from_far = far_swap(to_far)
    from_near = near_swap(to_near)
    for stage in range(1, bits - 1, 2):
        rows_left //= 4
        pair = [order[stage : stage + 2] for order in orders]
        where = tuple((tuple(p), tuple(position(k, b) for b in p)) for k, p in enumerate(pair))
        outs = call(
            functools.partial(quad_kernel, share, where, len(gots[0])),
            [((rows_left + 16, half), bf16)] * 3
            + [((rows_left, half), f32)]
            + [((rows_left, half), bf16)] * 3
            + [((rows_left, half), f32), ((channels, 128), f32)],
            1 << 20,
            mine,
            kept[0],
            *gots[0],
            kept[1],
            *gots[1],
            conv,
            *([conv_got] if stage == 1 else []),
            scalars=1,
        )
        kept, conv = [outs[3], outs[7]], outs[8]
        gots = []
        for k in (0, 1):
            came = []
            for delta in (1, 2, 3):
                came.append(swap_by(outs[4 * k + delta - 1], ((delta & 1) << pair[k][0]) | ((delta >> 1) << pair[k][1])))
            gots.append(came)
            drop(k, *pair[k])
    (inner,) = call(
        inner_kernel, [((n, width), f32)], 1 << 30, grad, terms, wk, sources, cotangent
    )
    grad_mix, grad_conv, grad_input = call(
        functools.partial(last_kernel, 1.0 / float(total_cols) ** 0.5, channels),
        [((share, width), f32), ((taps, channels, channels), f32), ((n, width), bf16)],
        1 << 20,
        kept[0],
        *gots[0],
        kept[1],
        *gots[1],
        conv,
        inner,
        from_far,
        from_near,
    )
    return grad_input, grad_mix, grad_conv


def solution(mesh):
    return jax.shard_map(
        shards,
        mesh=mesh,
        in_specs=(
            P(("group", "space"), None),
            P(("group", "space"), None),
            P(),
            P(),
            P("space", None),
            P("space"),
            P("space"),
        ),
        out_specs=(P(("group", "space"), None), P("space", "group"), P("group", None, None)),
        check_vma=False,
    )
```

```python
import functools

import jax
import jax.numpy as jnp
from jax import lax
from jax.experimental import pallas as pl
from jax.experimental.pallas import tpu as pltpu
from jax.sharding import PartitionSpec as P


ROW = 256
WIDE = 256
TANH_SCALE = 0.7978845608028654
TANH_CUBE = 0.044715


f32 = jnp.float32
bf16 = jnp.bfloat16


def mm(a, b):
    return jnp.dot(a, b, preferred_element_type=f32)


def contract(a, b, dim_a, dim_b, **kw):
    return lax.dot_general(
        a, b, (((dim_a,), (dim_b,)), ((), ())), preferred_element_type=f32, **kw
    )


def iota(shape, dim):
    return lax.broadcasted_iota(jnp.int32, shape, dim)


def onehot(cond):
    return jnp.where(cond, 1.0, 0.0).astype(bf16)


def call(body, outs, cost, *args, scratch=(), scalars=0, far=()):
    space = lambda k: pltpu.SMEM if k < scalars else pltpu.HBM if k in far else pltpu.VMEM
    return pl.pallas_call(
        body,
        out_shape=[jax.ShapeDtypeStruct(s, d) for s, d in outs],
        in_specs=[pl.BlockSpec(memory_space=space(k)) for k in range(len(args))],
        out_specs=[pl.BlockSpec(memory_space=pltpu.VMEM)] * len(outs),
        scratch_shapes=list(scratch),
        cost_estimate=pl.CostEstimate(flops=cost, transcendentals=0, bytes_accessed=8 << 20),
        compiler_params=pltpu.CompilerParams(vmem_limit_bytes=12 << 20),
    )(*args)


def picked(local_t, turns, tap):
    turn = tap - 1 - turns
    slot = 1 + jnp.where(turn < 0, turn + 6, turn)
    source = jnp.full_like(slot, -1)
    for k in range(1, 7):
        source = jnp.where(slot == k, local_t[k : k + 1, :], source)
    return source


def early_kernel(place, near, turns, void, x_hbm, conv_hbm, halo_sel, sources_out, own, wk, x, conv, sems):
    copies = [
        pltpu.make_async_copy(src, dst, sems.at[k])
        for k, (src, dst) in enumerate(((conv_hbm, conv), (x_hbm, x)))
    ]
    for copy in copies:
        copy.start()
    n = x.shape[0]
    taps, c = conv.shape[:2]
    offset, total = place[0], place[1]
    base_far, base_near = place[2], place[3]
    moved = near[...] - offset + ROW
    moved = jnp.where(moved < 0, moved + total, moved)
    moved = jnp.where(moved >= total, moved - total, moved)
    dropped = (void[...] == 1) & (iota((taps, n), 0) == 6)
    local_t = jnp.where(dropped, -1, moved)
    sources = [picked(local_t, turns[...], tap) for tap in range(1, taps)]
    sources_t = jnp.concatenate(sources + [sources[0]] * (8 - len(sources)), axis=0)
    sources_out[...] = sources_t
    eye = jnp.where(iota((n, n), 0) == iota((n, n), 1), 1.0, 0.0)
    columns = contract(eye, sources_t.astype(f32), 1, 1, precision=lax.Precision.HIGHEST)
    columns = columns.astype(jnp.int32)

    copies[0].wait()
    repeat = onehot(iota((c, WIDE), 1) % c == iota((c, WIDE), 0))
    down = onehot(iota((WIDE, c), 0) % c == iota((WIDE, c), 1))
    same = iota((WIDE, WIDE), 0) // c == iota((WIDE, WIDE), 1) // c
    for tap in range(taps):
        wide = mm(conv[tap], repeat).astype(bf16)
        wk[tap * WIDE : (tap + 1) * WIDE, :] = jnp.where(same, mm(down, wide), 0.0).astype(bf16)
    copies[1].wait()
    for tap in range(1, taps):
        at = (tap - 1) * n
        source = columns[:, tap - 1 : tap]
        halo_sel[at : at + n, :ROW] = onehot(iota((n, ROW), 1) == source - base_far)
        halo_sel[at : at + n, ROW:] = onehot(iota((n, ROW), 1) == source - base_near)
        mine = onehot(iota((n, n), 1) + ROW == source)
        own[at : at + n, :] = mm(mine, x[...]).astype(bf16)


def gelu_tanh(v):
    return jnp.tanh(TANH_SCALE * (v + TANH_CUBE * (v * v * v)))


def front_kernel(share, me, far, near, halo_sel, own, wk, x, rows_out, pre, act_keep, act_send, act_t):
    n, width = pre.shape
    taps = wk.shape[0] // WIDE
    for c in range(0, width, WIDE):
        both = jnp.concatenate([far[:, c : c + WIDE], near[:, c : c + WIDE]], axis=0)
        rows = mm(halo_sel[...], both).astype(bf16) + own[:, c : c + WIDE]
        rows_out[:, c : c + WIDE] = rows
        acc = mm(x[:, c : c + WIDE], wk[:WIDE, :])
        for tap in range(1, taps):
            acc += mm(rows[(tap - 1) * n : tap * n], wk[tap * WIDE : (tap + 1) * WIDE, :])
        pre[:, c : c + WIDE] = acc
        active = (0.5 * acc) * (1.0 + gelu_tanh(acc))
        act_t[c : c + WIDE, :] = active.T.astype(bf16)
    for k in range(width // share // 2):
        for bit, out in ((me[0], act_keep), (1 - me[0], act_send)):
            at = pl.multiple_of((2 * k + bit) * share, share)
            out[k * share : (k + 1) * share, :] = act_t[pl.ds(at, share), :]


def up_kernel(cot, mix, up):
    up[...] = contract(cot[...], mix[...], 1, 1)


def blocks_of(count, bits, skips, me):
    groups = []
    for delta in range(1 << len(bits)):
        offset = 0
        for k, (bit, skip) in enumerate(zip(bits, skips)):
            offset += ((1 - me[bit]) if (delta >> k) & 1 else me[bit]) << skip
        group = []
        for q in range(count >> len(bits)):
            base = q
            for skip in sorted(skips):
                base = ((base >> skip) << (skip + 1)) | (base & ((1 << skip) - 1))
            group.append(base + offset)
        groups.append(group)
    return groups


def parcel(ref):
    return ref[:16, :128].astype(f32) + ref[:16, 128:256].astype(f32)


def pack(whole, sends, kept):
    high = whole.astype(bf16)
    low = (whole - high.astype(f32)).astype(bf16)
    kept[...] = high.astype(f32) + low.astype(f32)
    for send in sends:
        send[:16, :] = jnp.zeros((16, send.shape[1]), bf16)
        send[:16, :128] = high
        send[:16, 128:256] = low


def conv_sum(conv, gots):
    if len(gots) == 1:
        return conv[...] + parcel(gots[0])
    one, two, three = [parcel(got) for got in gots]
    return (conv[...] + one) + (two + three)


def mix_kernel(share, bits, skips, me, act, act_got, cot, cot_got, conv, conv_got, *outs):
    *sends, keep, conv_out = outs
    pack(conv[...] + conv_got[...], sends, conv_out)
    groups = blocks_of(act.shape[0] // share, bits, skips, me)
    both = jnp.concatenate([cot[...], cot_got[...]], axis=0)
    pieces = []
    for group in groups:
        for block in group:
            at = pl.ds(pl.multiple_of(block * share, share), share)
            pieces.append(jnp.concatenate([act[at, :], act_got[at, :]], axis=1))
    total = mm(jnp.concatenate(pieces, axis=0), both)
    rows = keep.shape[0]
    keep[...] = total[:rows]
    for k, send in enumerate(sends):
        send[16:, :] = total[(k + 1) * rows : (k + 2) * rows].astype(bf16)


def stage_kernel(share, bits, skips, came, me, kept, *refs):
    gots, conv, (*sends, keep, conv_out) = refs[:came], refs[came], refs[came + 1 :]
    pack(conv_sum(conv, gots), sends, conv_out)
    groups = blocks_of(kept.shape[0] // share, bits, skips, me)
    for group, out, out_at in zip(groups, [keep] + sends, [0] + [16] * len(sends)):
        for q, block in enumerate(group):
            at = pl.multiple_of(block * share, share)
            value = kept[pl.ds(at, share), :]
            for got in gots:
                value += got[pl.ds(pl.multiple_of(at + 16, 16), share), :].astype(f32)
            out[out_at + q * share : out_at + (q + 1) * share, :] = value.astype(out.dtype)


def last_kernel(scale, channels, came, kept, *refs):
    gots, (conv, inner, first, second, mix_out, conv_out, grad_out) = refs[:came], refs[came:]
    total = kept[...]
    for got in gots:
        total += got[16:, :].astype(f32)
    mix_out[...] = total * scale
    whole = conv_sum(conv, gots)
    for tap in range(conv_out.shape[0]):
        conv_out[tap] = whole[:, tap * channels : (tap + 1) * channels]
    grad_out[...] = (inner[...] + first[...].astype(f32) + second[...].astype(f32)).astype(bf16)


def select_rows(sources, start, count, taps):
    n = sources.shape[1]
    return jnp.concatenate(
        [onehot(iota((count, n), 0) == sources[tap : tap + 1, :] - start) for tap in range(taps - 1)], axis=1
    )


def weights_kernel(channels, scale, up, pre, x, rows, grad, conv):
    n, width = grad.shape
    taps = rows.shape[0] // n + 1
    acc = [jnp.zeros((WIDE, WIDE), f32) for _ in range(taps)]
    for c in range(0, width, WIDE):
        v = pre[:, c : c + WIDE]
        t = gelu_tanh(v)
        slope = 0.5 * (1.0 + t) + (0.5 * TANH_SCALE) * v * (1.0 - t * t) * (1.0 + (3 * TANH_CUBE) * (v * v))
        g = up[:, c : c + WIDE] * slope
        grad[:, c : c + WIDE] = g.astype(bf16)
        g_t = g.T.astype(bf16)
        acc[0] += mm(g_t, x[:, c : c + WIDE])
        for tap in range(1, taps):
            acc[tap] += mm(g_t, rows[(tap - 1) * n : tap * n, c : c + WIDE])
    same = iota((WIDE, WIDE), 0) // channels == iota((WIDE, WIDE), 1) // channels
    conv[...] = jnp.zeros(conv.shape, f32)
    fold = jnp.where(iota((channels, WIDE), 1) % channels == iota((channels, WIDE), 0), 1.0, 0.0)
    for tap in range(taps):
        block = jnp.where(same, acc[tap], 0.0)
        block = jnp.sum(block.reshape(WIDE // channels, channels, WIDE), axis=0)
        conv[:, tap * channels : (tap + 1) * channels] = (
            contract(fold, block, 1, 1, precision=lax.Precision.HIGHEST) * scale
        )


def pick_kernel(place, sources, back_sel):
    taps = back_sel.shape[1] // sources.shape[1] + 1
    back_sel[:ROW, :] = select_rows(sources, place[2], ROW, taps)
    back_sel[ROW:, :] = select_rows(sources, place[3], ROW, taps)


def terms_kernel(grad, wk, back_sel, terms, far, near):
    n, width = grad.shape
    taps = wk.shape[0] // WIDE
    for c in range(0, width, WIDE):
        g = grad[:, c : c + WIDE]
        for tap in range(1, taps):
            terms[(tap - 1) * n : tap * n, c : c + WIDE] = contract(
                g, wk[tap * WIDE : (tap + 1) * WIDE, :], 1, 1
            ).astype(bf16)
        both = mm(back_sel[...], terms[:, c : c + WIDE]).astype(bf16)
        far[:, c : c + WIDE] = both[:ROW]
        near[:, c : c + WIDE] = both[ROW:]


def inner_kernel(grad, terms, wk, sources, cot, inner):
    n, width = grad.shape
    taps = wk.shape[0] // WIDE
    sel = select_rows(sources, ROW, n, taps)
    for c in range(0, width, WIDE):
        acc = contract(grad[:, c : c + WIDE], wk[:WIDE, :], 1, 1) + cot[:, c : c + WIDE].astype(f32)
        inner[:, c : c + WIDE] = acc + mm(sel, terms[:, c : c + WIDE])


def shards(columns_in, cotangent, conv_weight, mix_weight, neighbours, rotations, pentagons):
    n, width = columns_in.shape
    taps, channels = conv_weight.shape[:2]
    devices = lax.axis_size("space")
    place = lax.axis_index("space").astype(jnp.int32)
    total_cols = n * devices
    levels = width // channels
    bits = devices.bit_length() - 1

    def near_swap(value):
        return lax.ppermute(value, "space", [(i, i ^ 1) for i in range(devices)])

    def far_swap(value):
        other = lambda i: (i + 1 if i % 2 else i - 1) % devices
        return lax.ppermute(value, "space", [(i, other(i)) for i in range(devices)])

    def swap_by(value, mask):
        return lax.ppermute(value, "space", [(i, i ^ mask) for i in range(devices)])

    def swap(value, bit):
        return swap_by(value, 1 << bit)

    far = far_swap(columns_in)
    near = near_swap(columns_in)
    odd = place & 1
    spots = jnp.stack([place * n, jnp.int32(total_cols), odd * (ROW + n), (1 - odd) * (ROW + n)])
    cot_got = swap(cotangent, 0)
    pairs = (taps - 1) * n
    share = width // devices
    half = width // 2
    mine = jnp.stack([(place >> b) & 1 for b in range(bits)])
    halo_sel, sources, own, wk = call(
        early_kernel,
        [((pairs, 2 * ROW), bf16), ((8, n), jnp.int32), ((pairs, width), bf16), ((taps * WIDE, WIDE), bf16)],
        1 << 30,
        spots,
        neighbours.T,
        rotations[None, :],
        pentagons[None, :],
        columns_in,
        conv_weight,
        scalars=1,
        far=(4, 5),
        scratch=[
            pltpu.VMEM(columns_in.shape, bf16),
            pltpu.VMEM(conv_weight.shape, bf16),
            pltpu.SemaphoreType.DMA((2,)),
        ],
    )
    (up,) = call(up_kernel, [((n, width), f32)], 1 << 29, cotangent, mix_weight)
    rows, pre, act, act_send = call(
        functools.partial(front_kernel, share),
        [((pairs, width), bf16), ((n, width), f32), ((half, n), bf16), ((half, n), bf16)],
        3 << 30,
        mine,
        far,
        near,
        halo_sel,
        own,
        wk,
        columns_in,
        scalars=1,
        scratch=[pltpu.VMEM((width, n), bf16)],
    )
    act_got = swap(act_send, 0)
    left = list(range(bits - 1, 0, -1))
    stages = [left[::-1][k : k + 2] for k in range(0, len(left), 2)]

    def skips_of(pair):
        return tuple(len(left) - 1 - left.index(b) for b in pair)

    grad, conv = call(
        functools.partial(weights_kernel, channels, 1.0 / float(total_cols * levels) ** 0.5),
        [((n, width), bf16), ((channels, 128), f32)],
        2 << 30,
        up,
        pre,
        columns_in,
        rows,
    )
    conv_got = swap(conv, 0)
    (back_sel,) = call(pick_kernel, [((2 * ROW, pairs), bf16)], 1 << 26, spots, sources, scalars=1)
    kept, gots = None, []
    rows_left = half
    for stage, pair in enumerate(stages):
        ways = 1 << len(pair)
        rows_left //= ways
        outs = [((rows_left + 16, width), bf16)] * (ways - 1) + [((rows_left, width), f32), ((channels, 128), f32)]
        if stage == 0:
            *sends, kept, conv = call(
                functools.partial(mix_kernel, share, tuple(pair), skips_of(pair)),
                outs,
                1 << 30,
                mine,
                act,
                act_got,
                cotangent,
                cot_got,
                conv,
                conv_got,
                scalars=1,
            )
        else:
            *sends, kept, conv = call(
                functools.partial(stage_kernel, share, tuple(pair), skips_of(pair), len(gots)),
                outs,
                1 << 20,
                mine,
                kept,
                *gots,
                conv,
                scalars=1,
            )
        gots = []
        for delta in range(ways - 1, 0, -1):
            mask = sum(1 << b for k, b in enumerate(pair) if (delta >> k) & 1)
            gots.insert(0, swap_by(sends[delta - 1], mask))
        left = [b for b in left if b not in pair]
    terms, to_far, to_near = call(
        terms_kernel,
        [((pairs, width), bf16), ((ROW, width), bf16), ((ROW, width), bf16)],
        3 << 30,
        grad,
        wk,
        back_sel,
    )
    from_far = far_swap(to_far)
    from_near = near_swap(to_near)
    (inner,) = call(inner_kernel, [((n, width), f32)], 1 << 30, grad, terms, wk, sources, cotangent)
    grad_mix, grad_conv, grad_input = call(
        functools.partial(last_kernel, 1.0 / float(total_cols) ** 0.5, channels, len(gots)),
        [((share, width), f32), ((taps, channels, channels), f32), ((n, width), bf16)],
        1 << 20,
        kept,
        *gots,
        conv,
        inner,
        from_far,
        from_near,
    )
    return grad_input, grad_mix, grad_conv


def solution(mesh):
    return jax.shard_map(
        shards,
        mesh=mesh,
        in_specs=(
            P(("group", "space"), None),
            P(("group", "space"), None),
            P(),
            P(),
            P("space", None),
            P("space"),
            P("space"),
        ),
        out_specs=(P(("group", "space"), None), P("space", "group"), P("group", None, None)),
        check_vma=False,
    )
```

```python
import functools

import jax
import jax.numpy as jnp
from jax import lax
from jax.experimental import pallas as pl
from jax.experimental.pallas import tpu as pltpu
from jax.sharding import PartitionSpec as P


ROW = 256
WIDE = 256
TANH_SCALE = 0.7978845608028654
TANH_CUBE = 0.044715


f32 = jnp.float32
bf16 = jnp.bfloat16


def mm(a, b):
    return jnp.dot(a, b, preferred_element_type=f32)


def contract(a, b, dim_a, dim_b, **kw):
    return lax.dot_general(
        a, b, (((dim_a,), (dim_b,)), ((), ())), preferred_element_type=f32, **kw
    )


def iota(shape, dim):
    return lax.broadcasted_iota(jnp.int32, shape, dim)


def onehot(cond):
    return jnp.where(cond, 1.0, 0.0).astype(bf16)


def call(body, outs, cost, *args, scratch=(), scalars=0, far=()):
    space = lambda k: pltpu.SMEM if k < scalars else pltpu.HBM if k in far else pltpu.VMEM
    return pl.pallas_call(
        body,
        out_shape=[jax.ShapeDtypeStruct(s, d) for s, d in outs],
        in_specs=[pl.BlockSpec(memory_space=space(k)) for k in range(len(args))],
        out_specs=[pl.BlockSpec(memory_space=pltpu.VMEM)] * len(outs),
        scratch_shapes=list(scratch),
        cost_estimate=pl.CostEstimate(flops=cost, transcendentals=0, bytes_accessed=8 << 20),
        compiler_params=pltpu.CompilerParams(vmem_limit_bytes=12 << 20),
    )(*args)


def picked(local_t, turns, tap):
    turn = tap - 1 - turns
    slot = 1 + jnp.where(turn < 0, turn + 6, turn)
    source = jnp.full_like(slot, -1)
    for k in range(1, 7):
        source = jnp.where(slot == k, local_t[k : k + 1, :], source)
    return source


def early_kernel(place, near, turns, void, x_hbm, conv_hbm, halo_sel, sources_out, own, wk, x, conv, sems):
    copies = [
        pltpu.make_async_copy(src, dst, sems.at[k])
        for k, (src, dst) in enumerate(((conv_hbm, conv), (x_hbm, x)))
    ]
    for copy in copies:
        copy.start()
    n = x.shape[0]
    taps, c = conv.shape[:2]
    offset, total = place[0], place[1]
    base_far, base_near = place[2], place[3]
    moved = near[...] - offset + ROW
    moved = jnp.where(moved < 0, moved + total, moved)
    moved = jnp.where(moved >= total, moved - total, moved)
    dropped = (void[...] == 1) & (iota((taps, n), 0) == 6)
    local_t = jnp.where(dropped, -1, moved)
    sources = [picked(local_t, turns[...], tap) for tap in range(1, taps)]
    sources_t = jnp.concatenate(sources + [sources[0]] * (8 - len(sources)), axis=0)
    sources_out[...] = sources_t
    eye = jnp.where(iota((n, n), 0) == iota((n, n), 1), 1.0, 0.0)
    columns = contract(eye, sources_t.astype(f32), 1, 1, precision=lax.Precision.HIGHEST)
    columns = columns.astype(jnp.int32)

    copies[0].wait()
    repeat = onehot(iota((c, WIDE), 1) % c == iota((c, WIDE), 0))
    down = onehot(iota((WIDE, c), 0) % c == iota((WIDE, c), 1))
    same = iota((WIDE, WIDE), 0) // c == iota((WIDE, WIDE), 1) // c
    for tap in range(taps):
        wide = mm(conv[tap], repeat).astype(bf16)
        wk[tap * WIDE : (tap + 1) * WIDE, :] = jnp.where(same, mm(down, wide), 0.0).astype(bf16)
    copies[1].wait()
    for tap in range(1, taps):
        at = (tap - 1) * n
        source = columns[:, tap - 1 : tap]
        halo_sel[at : at + n, :ROW] = onehot(iota((n, ROW), 1) == source - base_far)
        halo_sel[at : at + n, ROW:] = onehot(iota((n, ROW), 1) == source - base_near)
        mine = onehot(iota((n, n), 1) + ROW == source)
        own[at : at + n, :] = mm(mine, x[...]).astype(bf16)


def gelu_tanh(v):
    return jnp.tanh(TANH_SCALE * (v + TANH_CUBE * (v * v * v)))


def front_kernel(share, me, far, near, halo_sel, own, wk, x, rows_out, pre, act_keep, act_send, act_t):
    n, width = pre.shape
    taps = wk.shape[0] // WIDE
    for c in range(0, width, WIDE):
        both = jnp.concatenate([far[:, c : c + WIDE], near[:, c : c + WIDE]], axis=0)
        rows = mm(halo_sel[...], both).astype(bf16) + own[:, c : c + WIDE]
        rows_out[:, c : c + WIDE] = rows
        acc = mm(x[:, c : c + WIDE], wk[:WIDE, :])
        for tap in range(1, taps):
            acc += mm(rows[(tap - 1) * n : tap * n], wk[tap * WIDE : (tap + 1) * WIDE, :])
        pre[:, c : c + WIDE] = acc
        active = (0.5 * acc) * (1.0 + gelu_tanh(acc))
        act_t[c : c + WIDE, :] = active.T.astype(bf16)
    for k in range(width // share // 2):
        for bit, out in ((me[0], act_keep), (1 - me[0], act_send)):
            at = pl.multiple_of((2 * k + bit) * share, share)
            out[k * share : (k + 1) * share, :] = act_t[pl.ds(at, share), :]


def up_kernel(cot, mix, up):
    up[...] = contract(cot[...], mix[...], 1, 1)


def mix_kernel(share, where, me, act, act_got, cot, cot_got, *outs):
    half = cot.shape[1] // 2
    blocks = act.shape[0] // share
    for k, (bit, skip) in enumerate(where):
        cols = slice(k * half, (k + 1) * half)
        both = jnp.concatenate([cot[:, cols], cot_got[:, cols]], axis=0)
        for want, out in ((1 - me[bit], outs[2 * k]), (me[bit], outs[2 * k + 1])):
            pieces = []
            for q in range(blocks // 2):
                base = ((q >> skip) << (skip + 1)) | (q & ((1 << skip) - 1))
                at = pl.ds(pl.multiple_of((base + (want << skip)) * share, share), share)
                pieces.append(jnp.concatenate([act[at, :], act_got[at, :]], axis=1))
            out[...] = mm(jnp.concatenate(pieces, axis=0), both).astype(out.dtype)


def select_rows(sources, start, count, taps):
    n = sources.shape[1]
    return jnp.concatenate(
        [onehot(iota((count, n), 0) == sources[tap : tap + 1, :] - start) for tap in range(taps - 1)], axis=1
    )


def weights_kernel(channels, scale, up, pre, x, rows, grad, conv):
    n, width = grad.shape
    taps = rows.shape[0] // n + 1
    acc = [jnp.zeros((WIDE, WIDE), f32) for _ in range(taps)]
    for c in range(0, width, WIDE):
        v = pre[:, c : c + WIDE]
        t = gelu_tanh(v)
        slope = 0.5 * (1.0 + t) + (0.5 * TANH_SCALE) * v * (1.0 - t * t) * (1.0 + (3 * TANH_CUBE) * (v * v))
        g = up[:, c : c + WIDE] * slope
        grad[:, c : c + WIDE] = g.astype(bf16)
        g_t = g.T.astype(bf16)
        acc[0] += mm(g_t, x[:, c : c + WIDE])
        for tap in range(1, taps):
            acc[tap] += mm(g_t, rows[(tap - 1) * n : tap * n, c : c + WIDE])
    same = iota((WIDE, WIDE), 0) // channels == iota((WIDE, WIDE), 1) // channels
    conv[...] = jnp.zeros(conv.shape, f32)
    fold = jnp.where(iota((channels, WIDE), 1) % channels == iota((channels, WIDE), 0), 1.0, 0.0)
    for tap in range(taps):
        block = jnp.where(same, acc[tap], 0.0)
        block = jnp.sum(block.reshape(WIDE // channels, channels, WIDE), axis=0)
        conv[:, tap * channels : (tap + 1) * channels] = (
            contract(fold, block, 1, 1, precision=lax.Precision.HIGHEST) * scale
        )


def pick_kernel(place, sources, back_sel):
    taps = back_sel.shape[1] // sources.shape[1] + 1
    back_sel[:ROW, :] = select_rows(sources, place[2], ROW, taps)
    back_sel[ROW:, :] = select_rows(sources, place[3], ROW, taps)


def terms_kernel(grad, wk, back_sel, terms, far, near):
    n, width = grad.shape
    taps = wk.shape[0] // WIDE
    for c in range(0, width, WIDE):
        g = grad[:, c : c + WIDE]
        for tap in range(1, taps):
            terms[(tap - 1) * n : tap * n, c : c + WIDE] = contract(
                g, wk[tap * WIDE : (tap + 1) * WIDE, :], 1, 1
            ).astype(bf16)
        both = mm(back_sel[...], terms[:, c : c + WIDE]).astype(bf16)
        far[:, c : c + WIDE] = both[:ROW]
        near[:, c : c + WIDE] = both[ROW:]


def inner_kernel(grad, terms, wk, sources, cot, inner):
    n, width = grad.shape
    taps = wk.shape[0] // WIDE
    sel = select_rows(sources, ROW, n, taps)
    for c in range(0, width, WIDE):
        acc = contract(grad[:, c : c + WIDE], wk[:WIDE, :], 1, 1) + cot[:, c : c + WIDE].astype(f32)
        inner[:, c : c + WIDE] = acc + mm(sel, terms[:, c : c + WIDE])


def halve(share, bit, skip, kept, got, got_at, send, send_at, keep):
    for q in range(kept.shape[0] // share // 2):
        base = ((q >> skip) << (skip + 1)) | (q & ((1 << skip) - 1))
        for value, out, out_at in ((1 - bit, send, send_at), (bit, keep, 0)):
            at = pl.multiple_of((base + (value << skip)) * share, share)
            came = got[pl.ds(pl.multiple_of(at + got_at, 16), share), :].astype(f32)
            out[out_at + q * share : out_at + (q + 1) * share, :] = (
                kept[pl.ds(at, share), :] + came
            ).astype(out.dtype)


def parcel(ref):
    return ref[:16, :128].astype(f32) + ref[:16, 128:256].astype(f32)


def merge_kernel(share, where, first, me, kept_a, got_a, kept_b, got_b, conv, conv_got, send_a, keep_a, send_b, keep_b, conv_out):
    whole = conv[...] + (conv_got[...] if first else parcel(got_a))
    high = whole.astype(bf16)
    low = (whole - high.astype(f32)).astype(bf16)
    conv_out[...] = high.astype(f32) + low.astype(f32)
    send_a[:16, :] = jnp.zeros((16, send_a.shape[1]), bf16)
    send_a[:16, :128] = high
    send_a[:16, 128:256] = low
    (bit_a, skip_a), (bit_b, skip_b) = where
    halve(share, me[bit_a], skip_a, kept_a, got_a, 0 if first else 16, send_a, 16, keep_a)
    halve(share, me[bit_b], skip_b, kept_b, got_b, 0, send_b, 0, keep_b)


def last_kernel(scale, channels, kept_a, got_a, kept_b, got_b, conv, inner, first, second, mix_out, conv_out, grad_out):
    half = kept_a.shape[1]
    mix_out[:, :half] = (kept_a[...] + got_a[16:, :].astype(f32)) * scale
    mix_out[:, half:] = (kept_b[...] + got_b[...].astype(f32)) * scale
    whole = conv[...] + parcel(got_a)
    for tap in range(conv_out.shape[0]):
        conv_out[tap] = whole[:, tap * channels : (tap + 1) * channels]
    grad_out[...] = (inner[...] + first[...].astype(f32) + second[...].astype(f32)).astype(bf16)


def shards(columns_in, cotangent, conv_weight, mix_weight, neighbours, rotations, pentagons):
    n, width = columns_in.shape
    taps, channels = conv_weight.shape[:2]
    devices = lax.axis_size("space")
    place = lax.axis_index("space").astype(jnp.int32)
    total_cols = n * devices
    levels = width // channels
    bits = devices.bit_length() - 1

    def near_swap(value):
        return lax.ppermute(value, "space", [(i, i ^ 1) for i in range(devices)])

    def far_swap(value):
        other = lambda i: (i + 1 if i % 2 else i - 1) % devices
        return lax.ppermute(value, "space", [(i, other(i)) for i in range(devices)])

    def swap_by(value, mask):
        return lax.ppermute(value, "space", [(i, i ^ mask) for i in range(devices)])

    def swap(value, bit):
        return swap_by(value, 1 << bit)

    far = far_swap(columns_in)
    near = near_swap(columns_in)
    odd = place & 1
    spots = jnp.stack([place * n, jnp.int32(total_cols), odd * (ROW + n), (1 - odd) * (ROW + n)])
    cot_got = swap(cotangent, 0)
    pairs = (taps - 1) * n
    share = width // devices
    half = width // 2
    mine = jnp.stack([(place >> b) & 1 for b in range(bits)])
    halo_sel, sources, own, wk = call(
        early_kernel,
        [((pairs, 2 * ROW), bf16), ((8, n), jnp.int32), ((pairs, width), bf16), ((taps * WIDE, WIDE), bf16)],
        1 << 30,
        spots,
        neighbours.T,
        rotations[None, :],
        pentagons[None, :],
        columns_in,
        conv_weight,
        scalars=1,
        far=(4, 5),
        scratch=[
            pltpu.VMEM(columns_in.shape, bf16),
            pltpu.VMEM(conv_weight.shape, bf16),
            pltpu.SemaphoreType.DMA((2,)),
        ],
    )
    (up,) = call(up_kernel, [((n, width), f32)], 1 << 29, cotangent, mix_weight)
    (back_sel,) = call(pick_kernel, [((2 * ROW, pairs), bf16)], 1 << 26, spots, sources, scalars=1)
    rows, pre, act, act_send = call(
        functools.partial(front_kernel, share),
        [((pairs, width), bf16), ((n, width), f32), ((half, n), bf16), ((half, n), bf16)],
        3 << 30,
        mine,
        far,
        near,
        halo_sel,
        own,
        wk,
        columns_in,
        scalars=1,
        scratch=[pltpu.VMEM((width, n), bf16)],
    )
    act_got = swap(act_send, 0)
    orders = [list(range(1, bits)), list(range(2, bits)) + [1]]
    lefts = [list(range(bits - 1, 0, -1)) for _ in orders]

    def position(k, bit):
        return len(lefts[k]) - 1 - lefts[k].index(bit)

    def drop(k, *gone):
        lefts[k] = [b for b in lefts[k] if b not in gone]

    rows_left = half // 2
    parts = call(
        functools.partial(
            mix_kernel, share, tuple((order[0], position(k, order[0])) for k, order in enumerate(orders))
        ),
        [((rows_left, half), bf16), ((rows_left, half), f32)] * 2,
        1 << 30,
        mine,
        act,
        act_got,
        cotangent,
        cot_got,
        scalars=1,
    )
    kept, gots = [parts[1], parts[3]], []
    for k in (0, 1):
        gots.append([swap(parts[2 * k], orders[k][0])])
        drop(k, orders[k][0])
    grad, conv = call(
        functools.partial(weights_kernel, channels, 1.0 / float(total_cols * levels) ** 0.5),
        [((n, width), bf16), ((channels, 128), f32)],
        2 << 30,
        up,
        pre,
        columns_in,
        rows,
    )
    terms, to_far, to_near = call(
        terms_kernel,
        [((pairs, width), bf16), ((ROW, width), bf16), ((ROW, width), bf16)],
        3 << 30,
        grad,
        wk,
        back_sel,
    )
    conv = conv + swap(conv, 0)
    conv_got = swap(conv, 1)
    from_far = far_swap(to_far)
    from_near = near_swap(to_near)
    for stage in range(1, bits - 1):
        rows_left //= 2
        where = tuple((order[stage], position(k, order[stage])) for k, order in enumerate(orders))
        *outs, conv = call(
            functools.partial(merge_kernel, share, where, stage == 1),
            [
                ((rows_left + 16, half), bf16),
                ((rows_left, half), f32),
                ((rows_left, half), bf16),
                ((rows_left, half), f32),
                ((channels, 128), f32),
            ],
            1 << 20,
            mine,
            kept[0],
            *gots[0],
            kept[1],
            *gots[1],
            conv,
            conv_got,
            scalars=1,
        )
        kept, gots = [outs[1], outs[3]], []
        for k in (0, 1):
            gots.append([swap(outs[2 * k], orders[k][stage])])
            drop(k, orders[k][stage])
    (inner,) = call(
        inner_kernel, [((n, width), f32)], 1 << 30, grad, terms, wk, sources, cotangent
    )
    grad_mix, grad_conv, grad_input = call(
        functools.partial(last_kernel, 1.0 / float(total_cols) ** 0.5, channels),
        [((share, width), f32), ((taps, channels, channels), f32), ((n, width), bf16)],
        1 << 20,
        kept[0],
        *gots[0],
        kept[1],
        *gots[1],
        conv,
        inner,
        from_far,
        from_near,
    )
    return grad_input, grad_mix, grad_conv


def solution(mesh):
    return jax.shard_map(
        shards,
        mesh=mesh,
        in_specs=(
            P(("group", "space"), None),
            P(("group", "space"), None),
            P(),
            P(),
            P("space", None),
            P("space"),
            P("space"),
        ),
        out_specs=(P(("group", "space"), None), P("space", "group"), P("group", None, None)),
        check_vma=False,
    )
```

```python
import functools

import jax
import jax.numpy as jnp
from jax import lax
from jax.experimental import pallas as pl
from jax.experimental.pallas import tpu as pltpu
from jax.sharding import PartitionSpec as P


ROW = 256
WIDE = 256
TANH_SCALE = 0.7978845608028654
TANH_CUBE = 0.044715


f32 = jnp.float32
bf16 = jnp.bfloat16


def mm(a, b):
    return jnp.dot(a, b, preferred_element_type=f32)


def contract(a, b, dim_a, dim_b, **kw):
    return lax.dot_general(
        a, b, (((dim_a,), (dim_b,)), ((), ())), preferred_element_type=f32, **kw
    )


def iota(shape, dim):
    return lax.broadcasted_iota(jnp.int32, shape, dim)


def onehot(cond):
    return jnp.where(cond, 1.0, 0.0).astype(bf16)


def call(body, outs, cost, *args, scratch=(), scalars=0, far=()):
    space = lambda k: pltpu.SMEM if k < scalars else pltpu.HBM if k in far else pltpu.VMEM
    return pl.pallas_call(
        body,
        out_shape=[jax.ShapeDtypeStruct(s, d) for s, d in outs],
        in_specs=[pl.BlockSpec(memory_space=space(k)) for k in range(len(args))],
        out_specs=[pl.BlockSpec(memory_space=pltpu.VMEM)] * len(outs),
        scratch_shapes=list(scratch),
        cost_estimate=pl.CostEstimate(flops=cost, transcendentals=0, bytes_accessed=8 << 20),
        compiler_params=pltpu.CompilerParams(vmem_limit_bytes=12 << 20),
    )(*args)


def picked(local_t, turns, tap):
    turn = tap - 1 - turns
    slot = 1 + jnp.where(turn < 0, turn + 6, turn)
    source = jnp.full_like(slot, -1)
    for k in range(1, 7):
        source = jnp.where(slot == k, local_t[k : k + 1, :], source)
    return source


def early_kernel(place, near, turns, void, x_hbm, conv_hbm, halo_sel, sources_out, own, wk, x, conv, sems):
    copies = [
        pltpu.make_async_copy(src, dst, sems.at[k])
        for k, (src, dst) in enumerate(((conv_hbm, conv), (x_hbm, x)))
    ]
    for copy in copies:
        copy.start()
    n = x.shape[0]
    taps, c = conv.shape[:2]
    offset, total = place[0], place[1]
    base_far, base_near = place[2], place[3]
    moved = near[...] - offset + ROW
    moved = jnp.where(moved < 0, moved + total, moved)
    moved = jnp.where(moved >= total, moved - total, moved)
    dropped = (void[...] == 1) & (iota((taps, n), 0) == 6)
    local_t = jnp.where(dropped, -1, moved)
    sources = [picked(local_t, turns[...], tap) for tap in range(1, taps)]
    sources_t = jnp.concatenate(sources + [sources[0]] * (8 - len(sources)), axis=0)
    sources_out[...] = sources_t
    eye = jnp.where(iota((n, n), 0) == iota((n, n), 1), 1.0, 0.0)
    columns = contract(eye, sources_t.astype(f32), 1, 1, precision=lax.Precision.HIGHEST)
    columns = columns.astype(jnp.int32)

    copies[0].wait()
    repeat = onehot(iota((c, WIDE), 1) % c == iota((c, WIDE), 0))
    down = onehot(iota((WIDE, c), 0) % c == iota((WIDE, c), 1))
    same = iota((WIDE, WIDE), 0) // c == iota((WIDE, WIDE), 1) // c
    for tap in range(taps):
        wide = mm(conv[tap], repeat).astype(bf16)
        wk[tap * WIDE : (tap + 1) * WIDE, :] = jnp.where(same, mm(down, wide), 0.0).astype(bf16)
    copies[1].wait()
    for tap in range(1, taps):
        at = (tap - 1) * n
        source = columns[:, tap - 1 : tap]
        halo_sel[at : at + n, :ROW] = onehot(iota((n, ROW), 1) == source - base_far)
        halo_sel[at : at + n, ROW:] = onehot(iota((n, ROW), 1) == source - base_near)
        mine = onehot(iota((n, n), 1) + ROW == source)
        own[at : at + n, :] = mm(mine, x[...]).astype(bf16)


def gelu_tanh(v):
    return jnp.tanh(TANH_SCALE * (v + TANH_CUBE * (v * v * v)))


def front_kernel(share, me, far, near, halo_sel, own, wk, x, rows_out, pre, act_keep, act_send, act_t):
    n, width = pre.shape
    taps = wk.shape[0] // WIDE
    for c in range(0, width, WIDE):
        cols = slice(c, c + WIDE)
        both = jnp.concatenate([far[:, cols], near[:, cols]], axis=0)
        for tap in range(1, taps):
            at = slice((tap - 1) * n, tap * n)
            rows_out[at, cols] = mm(halo_sel[at, :], both).astype(bf16) + own[at, cols]
    for c in range(0, width, WIDE):
        cols = slice(c, c + WIDE)
        wide = [x[:, cols]] + [rows_out[(tap - 1) * n : tap * n, cols] for tap in range(1, taps)]
        acc = mm(jnp.concatenate(wide, axis=1), wk[...])
        pre[:, cols] = acc
        active = (0.5 * acc) * (1.0 + gelu_tanh(acc))
        act_t[cols, :] = active.T.astype(bf16)
    for k in range(width // share // 2):
        for bit, out in ((me[0], act_keep), (1 - me[0], act_send)):
            at = pl.multiple_of((2 * k + bit) * share, share)
            out[k * share : (k + 1) * share, :] = act_t[pl.ds(at, share), :]


def up_kernel(cot, mix, up):
    up[...] = contract(cot[...], mix[...], 1, 1)


def mix_kernel(share, where, me, act, act_got, cot, cot_got, *outs):
    half = cot.shape[1] // 2
    blocks = act.shape[0] // share
    for k, (bit, skip) in enumerate(where):
        cols = slice(k * half, (k + 1) * half)
        both = jnp.concatenate([cot[:, cols], cot_got[:, cols]], axis=0)
        pieces = []
        for want in (1 - me[bit], me[bit]):
            for q in range(blocks // 2):
                base = ((q >> skip) << (skip + 1)) | (q & ((1 << skip) - 1))
                at = pl.ds(pl.multiple_of((base + (want << skip)) * share, share), share)
                pieces.append(jnp.concatenate([act[at, :], act_got[at, :]], axis=1))
        total = mm(jnp.concatenate(pieces, axis=0), both)
        rows = total.shape[0] // 2
        outs[2 * k][...] = total[:rows].astype(bf16)
        outs[2 * k + 1][...] = total[rows:]


def select_rows(sources, start, count, taps):
    n = sources.shape[1]
    return jnp.concatenate(
        [onehot(iota((count, n), 0) == sources[tap : tap + 1, :] - start) for tap in range(taps - 1)], axis=1
    )


def weights_kernel(channels, scale, up, pre, x, rows, grad, conv):
    n, width = grad.shape
    taps = rows.shape[0] // n + 1
    turned = []
    for c in range(0, width, WIDE):
        v = pre[:, c : c + WIDE]
        t = gelu_tanh(v)
        slope = 0.5 * (1.0 + t) + (0.5 * TANH_SCALE) * v * (1.0 - t * t) * (1.0 + (3 * TANH_CUBE) * (v * v))
        g = up[:, c : c + WIDE] * slope
        grad[:, c : c + WIDE] = g.astype(bf16)
        turned.append(g.T.astype(bf16))
    turned = jnp.concatenate(turned, axis=1)
    acc = []
    for tap in range(taps):
        part = x[...] if tap == 0 else rows[(tap - 1) * n : tap * n, :]
        acc.append(mm(turned, jnp.concatenate([part[:, c : c + WIDE] for c in range(0, width, WIDE)], axis=0)))
    same = iota((WIDE, WIDE), 0) // channels == iota((WIDE, WIDE), 1) // channels
    conv[...] = jnp.zeros(conv.shape, f32)
    fold = jnp.where(iota((channels, WIDE), 1) % channels == iota((channels, WIDE), 0), 1.0, 0.0)
    for tap in range(taps):
        block = jnp.where(same, acc[tap], 0.0)
        block = jnp.sum(block.reshape(WIDE // channels, channels, WIDE), axis=0)
        conv[:, tap * channels : (tap + 1) * channels] = (
            contract(fold, block, 1, 1, precision=lax.Precision.HIGHEST) * scale
        )


def pick_kernel(place, sources, back_sel):
    taps = back_sel.shape[1] // sources.shape[1] + 1
    back_sel[:ROW, :] = select_rows(sources, place[2], ROW, taps)
    back_sel[ROW:, :] = select_rows(sources, place[3], ROW, taps)


def terms_kernel(grad, wk, back_sel, terms, far, near):
    n, width = grad.shape
    taps = wk.shape[0] // WIDE
    for c in range(0, width, WIDE):
        g = grad[:, c : c + WIDE]
        for tap in range(1, taps):
            terms[(tap - 1) * n : tap * n, c : c + WIDE] = contract(
                g, wk[tap * WIDE : (tap + 1) * WIDE, :], 1, 1
            ).astype(bf16)
        both = mm(back_sel[...], terms[:, c : c + WIDE]).astype(bf16)
        far[:, c : c + WIDE] = both[:ROW]
        near[:, c : c + WIDE] = both[ROW:]


def inner_kernel(grad, terms, wk, sources, cot, inner):
    n, width = grad.shape
    taps = wk.shape[0] // WIDE
    sel = select_rows(sources, ROW, n, taps)
    for c in range(0, width, WIDE):
        acc = contract(grad[:, c : c + WIDE], wk[:WIDE, :], 1, 1) + cot[:, c : c + WIDE].astype(f32)
        inner[:, c : c + WIDE] = acc + mm(sel, terms[:, c : c + WIDE])


def parcel(ref):
    return ref[:16, :128].astype(f32) + ref[:16, 128:256].astype(f32)


def conv_sum(conv, gots):
    one, two, three = [parcel(got) for got in gots]
    return (conv[...] + one) + (two + three)


def quarter(share, bits, skips, kept, gots, got_at, sends, send_at, keep):
    (lo, hi), (bit_lo, bit_hi) = skips, bits
    small, large = min(lo, hi), max(lo, hi)
    for q in range(kept.shape[0] // share // 4):
        base = ((q >> small) << (small + 1)) | (q & ((1 << small) - 1))
        base = ((base >> large) << (large + 1)) | (base & ((1 << large) - 1))
        for delta in range(4):
            out, out_at = (keep, 0) if delta == 0 else (sends[delta - 1], send_at)
            want_lo = 1 - bit_lo if delta & 1 else bit_lo
            want_hi = 1 - bit_hi if delta & 2 else bit_hi
            at = pl.multiple_of((base + (want_lo << lo) + (want_hi << hi)) * share, share)
            value = kept[pl.ds(at, share), :]
            for got in gots:
                value += got[pl.ds(pl.multiple_of(at + got_at, 16), share), :].astype(f32)
            out[out_at + q * share : out_at + (q + 1) * share, :] = value.astype(out.dtype)


def quad_kernel(share, where, came, me, *refs):
    first = came == 1
    kept_a, gots_a, kept_b, gots_b = refs[0], refs[1 : 1 + came], refs[1 + came], refs[2 + came : 2 + 2 * came]
    rest = refs[2 + 2 * came :]
    if first:
        whole = rest[0][...] + rest[1][...]
        rest = rest[2:]
    else:
        whole = conv_sum(rest[0], gots_a)
        rest = rest[1:]
    sends_a, keep_a, sends_b, keep_b, conv_out = rest[:3], rest[3], rest[4:7], rest[7], rest[8]
    high = whole.astype(bf16)
    low = (whole - high.astype(f32)).astype(bf16)
    conv_out[...] = high.astype(f32) + low.astype(f32)
    for send in sends_a:
        send[:16, :] = jnp.zeros((16, send.shape[1]), bf16)
        send[:16, :128] = high
        send[:16, 128:256] = low
    (bits_a, skips_a), (bits_b, skips_b) = where
    chosen = lambda bits: (me[bits[0]], me[bits[1]])
    quarter(share, chosen(bits_a), skips_a, kept_a, gots_a, 0 if first else 16, sends_a, 16, keep_a)
    quarter(share, chosen(bits_b), skips_b, kept_b, gots_b, 0, sends_b, 0, keep_b)


def last_kernel(scale, channels, *refs):
    kept_a, gots_a, kept_b, gots_b = refs[0], refs[1:4], refs[4], refs[5:8]
    conv, inner, first, second, mix_out, conv_out, grad_out = refs[8:]
    half = kept_a.shape[1]
    total = kept_a[...]
    for got in gots_a:
        total += got[16:, :].astype(f32)
    mix_out[:, :half] = total * scale
    total = kept_b[...]
    for got in gots_b:
        total += got[...].astype(f32)
    mix_out[:, half:] = total * scale
    whole = conv_sum(conv, gots_a)
    for tap in range(conv_out.shape[0]):
        conv_out[tap] = whole[:, tap * channels : (tap + 1) * channels]
    grad_out[...] = (inner[...] + first[...].astype(f32) + second[...].astype(f32)).astype(bf16)


def shards(columns_in, cotangent, conv_weight, mix_weight, neighbours, rotations, pentagons):
    n, width = columns_in.shape
    taps, channels = conv_weight.shape[:2]
    devices = lax.axis_size("space")
    place = lax.axis_index("space").astype(jnp.int32)
    total_cols = n * devices
    levels = width // channels
    bits = devices.bit_length() - 1

    def near_swap(value):
        return lax.ppermute(value, "space", [(i, i ^ 1) for i in range(devices)])

    def far_swap(value):
        other = lambda i: (i + 1 if i % 2 else i - 1) % devices
        return lax.ppermute(value, "space", [(i, other(i)) for i in range(devices)])

    def swap_by(value, mask):
        return lax.ppermute(value, "space", [(i, i ^ mask) for i in range(devices)])

    def swap(value, bit):
        return swap_by(value, 1 << bit)

    far = far_swap(columns_in)
    near = near_swap(columns_in)
    odd = place & 1
    spots = jnp.stack([place * n, jnp.int32(total_cols), odd * (ROW + n), (1 - odd) * (ROW + n)])
    cot_got = swap(cotangent, 0)
    pairs = (taps - 1) * n
    share = width // devices
    half = width // 2
    mine = jnp.stack([(place >> b) & 1 for b in range(bits)])
    halo_sel, sources, own, wk = call(
        early_kernel,
        [((pairs, 2 * ROW), bf16), ((8, n), jnp.int32), ((pairs, width), bf16), ((taps * WIDE, WIDE), bf16)],
        1 << 30,
        spots,
        neighbours.T,
        rotations[None, :],
        pentagons[None, :],
        columns_in,
        conv_weight,
        scalars=1,
        far=(4, 5),
        scratch=[
            pltpu.VMEM(columns_in.shape, bf16),
            pltpu.VMEM(conv_weight.shape, bf16),
            pltpu.SemaphoreType.DMA((2,)),
        ],
    )
    (up,) = call(up_kernel, [((n, width), f32)], 1 << 29, cotangent, mix_weight)
    (back_sel,) = call(pick_kernel, [((2 * ROW, pairs), bf16)], 1 << 26, spots, sources, scalars=1)
    rows, pre, act, act_send = call(
        functools.partial(front_kernel, share),
        [((pairs, width), bf16), ((n, width), f32), ((half, n), bf16), ((half, n), bf16)],
        3 << 30,
        mine,
        far,
        near,
        halo_sel,
        own,
        wk,
        columns_in,
        scalars=1,
        scratch=[pltpu.VMEM((width, n), bf16)],
    )
    act_got = swap(act_send, 0)
    orders = [list(range(1, bits)), list(range(2, bits)) + [1]]
    lefts = [list(range(bits - 1, 0, -1)) for _ in orders]

    def position(k, bit):
        return len(lefts[k]) - 1 - lefts[k].index(bit)

    def drop(k, *gone):
        lefts[k] = [b for b in lefts[k] if b not in gone]

    rows_left = half // 2
    parts = call(
        functools.partial(
            mix_kernel, share, tuple((order[0], position(k, order[0])) for k, order in enumerate(orders))
        ),
        [((rows_left, half), bf16), ((rows_left, half), f32)] * 2,
        1 << 30,
        mine,
        act,
        act_got,
        cotangent,
        cot_got,
        scalars=1,
    )
    kept, gots = [parts[1], parts[3]], []
    for k in (0, 1):
        gots.append([swap(parts[2 * k], orders[k][0])])
        drop(k, orders[k][0])
    grad, conv = call(
        functools.partial(weights_kernel, channels, 1.0 / float(total_cols * levels) ** 0.5),
        [((n, width), bf16), ((channels, 128), f32)],
        2 << 30,
        up,
        pre,
        columns_in,
        rows,
    )
    terms, to_far, to_near = call(
        terms_kernel,
        [((pairs, width), bf16), ((ROW, width), bf16), ((ROW, width), bf16)],
        3 << 30,
        grad,
        wk,
        back_sel,
    )
    conv = conv + swap(conv, 0)
    conv_got = swap(conv, 1)
    from_far = far_swap(to_far)
    from_near = near_swap(to_near)
    for stage in range(1, bits - 1, 2):
        rows_left //= 4
        pair = [order[stage : stage + 2] for order in orders]
        where = tuple((tuple(p), tuple(position(k, b) for b in p)) for k, p in enumerate(pair))
        outs = call(
            functools.partial(quad_kernel, share, where, len(gots[0])),
            [((rows_left + 16, half), bf16)] * 3
            + [((rows_left, half), f32)]
            + [((rows_left, half), bf16)] * 3
            + [((rows_left, half), f32), ((channels, 128), f32)],
            1 << 20,
            mine,
            kept[0],
            *gots[0],
            kept[1],
            *gots[1],
            conv,
            *([conv_got] if stage == 1 else []),
            scalars=1,
        )
        kept, conv = [outs[3], outs[7]], outs[8]
        gots = []
        for k in (0, 1):
            came = []
            for delta in (1, 2, 3):
                came.append(swap_by(outs[4 * k + delta - 1], ((delta & 1) << pair[k][0]) | ((delta >> 1) << pair[k][1])))
            gots.append(came)
            drop(k, *pair[k])
    (inner,) = call(
        inner_kernel, [((n, width), f32)], 1 << 30, grad, terms, wk, sources, cotangent
    )
    grad_mix, grad_conv, grad_input = call(
        functools.partial(last_kernel, 1.0 / float(total_cols) ** 0.5, channels),
        [((share, width), f32), ((taps, channels, channels), f32), ((n, width), bf16)],
        1 << 20,
        kept[0],
        *gots[0],
        kept[1],
        *gots[1],
        conv,
        inner,
        from_far,
        from_near,
    )
    return grad_input, grad_mix, grad_conv


def solution(mesh):
    return jax.shard_map(
        shards,
        mesh=mesh,
        in_specs=(
            P(("group", "space"), None),
            P(("group", "space"), None),
            P(),
            P(),
            P("space", None),
            P("space"),
            P("space"),
        ),
        out_specs=(P(("group", "space"), None), P("space", "group"), P("group", None, None)),
        check_vma=False,
    )
```

```python
import functools

import jax
import jax.numpy as jnp
from jax import lax
from jax.experimental import pallas as pl
from jax.experimental.pallas import tpu as pltpu
from jax.sharding import PartitionSpec as P


ROW = 256
WIDE = 256
TANH_SCALE = 0.7978845608028654
TANH_CUBE = 0.044715


f32 = jnp.float32
bf16 = jnp.bfloat16


def mm(a, b):
    return jnp.dot(a, b, preferred_element_type=f32)


def contract(a, b, dim_a, dim_b, **kw):
    return lax.dot_general(
        a, b, (((dim_a,), (dim_b,)), ((), ())), preferred_element_type=f32, **kw
    )


def iota(shape, dim):
    return lax.broadcasted_iota(jnp.int32, shape, dim)


def onehot(cond):
    return jnp.where(cond, 1.0, 0.0).astype(bf16)


def call(body, outs, cost, *args, scratch=(), scalars=0, far=()):
    space = lambda k: pltpu.SMEM if k < scalars else pltpu.HBM if k in far else pltpu.VMEM
    return pl.pallas_call(
        body,
        out_shape=[jax.ShapeDtypeStruct(s, d) for s, d in outs],
        in_specs=[pl.BlockSpec(memory_space=space(k)) for k in range(len(args))],
        out_specs=[pl.BlockSpec(memory_space=pltpu.VMEM)] * len(outs),
        scratch_shapes=list(scratch),
        cost_estimate=pl.CostEstimate(flops=cost, transcendentals=0, bytes_accessed=8 << 20),
        compiler_params=pltpu.CompilerParams(vmem_limit_bytes=12 << 20),
    )(*args)


def picked(local_t, turns, tap):
    turn = tap - 1 - turns
    slot = 1 + jnp.where(turn < 0, turn + 6, turn)
    source = jnp.full_like(slot, -1)
    for k in range(1, 7):
        source = jnp.where(slot == k, local_t[k : k + 1, :], source)
    return source


def early_kernel(place, near, turns, void, x_hbm, conv_hbm, halo_sel, sources_out, own, wk, x, conv, sems):
    copies = [
        pltpu.make_async_copy(src, dst, sems.at[k])
        for k, (src, dst) in enumerate(((conv_hbm, conv), (x_hbm, x)))
    ]
    for copy in copies:
        copy.start()
    n = x.shape[0]
    taps, c = conv.shape[:2]
    offset, total = place[0], place[1]
    base_far, base_near = place[2], place[3]
    moved = near[...] - offset + ROW
    moved = jnp.where(moved < 0, moved + total, moved)
    moved = jnp.where(moved >= total, moved - total, moved)
    dropped = (void[...] == 1) & (iota((taps, n), 0) == 6)
    local_t = jnp.where(dropped, -1, moved)
    sources = [picked(local_t, turns[...], tap) for tap in range(1, taps)]
    sources_t = jnp.concatenate(sources + [sources[0]] * (8 - len(sources)), axis=0)
    sources_out[...] = sources_t
    eye = jnp.where(iota((n, n), 0) == iota((n, n), 1), 1.0, 0.0)
    columns = contract(eye, sources_t.astype(f32), 1, 1, precision=lax.Precision.HIGHEST)
    columns = columns.astype(jnp.int32)

    copies[0].wait()
    repeat = onehot(iota((c, WIDE), 1) % c == iota((c, WIDE), 0))
    down = onehot(iota((WIDE, c), 0) % c == iota((WIDE, c), 1))
    same = iota((WIDE, WIDE), 0) // c == iota((WIDE, WIDE), 1) // c
    for tap in range(taps):
        wide = mm(conv[tap], repeat).astype(bf16)
        wk[tap * WIDE : (tap + 1) * WIDE, :] = jnp.where(same, mm(down, wide), 0.0).astype(bf16)
    copies[1].wait()
    for tap in range(1, taps):
        at = (tap - 1) * n
        source = columns[:, tap - 1 : tap]
        halo_sel[at : at + n, :ROW] = onehot(iota((n, ROW), 1) == source - base_far)
        halo_sel[at : at + n, ROW:] = onehot(iota((n, ROW), 1) == source - base_near)
        mine = onehot(iota((n, n), 1) + ROW == source)
        own[at : at + n, :] = mm(mine, x[...]).astype(bf16)


def gelu_tanh(v):
    return jnp.tanh(TANH_SCALE * (v + TANH_CUBE * (v * v * v)))


def front_kernel(share, me, far, near, halo_sel, own, wk, x, rows_out, pre, act_keep, act_send, act_t):
    n, width = pre.shape
    taps = wk.shape[0] // WIDE
    for c in range(0, width, WIDE):
        cols = slice(c, c + WIDE)
        both = jnp.concatenate([far[:, cols], near[:, cols]], axis=0)
        for tap in range(1, taps):
            at = slice((tap - 1) * n, tap * n)
            rows_out[at, cols] = mm(halo_sel[at, :], both).astype(bf16) + own[at, cols]
    for c in range(0, width, WIDE):
        cols = slice(c, c + WIDE)
        wide = [x[:, cols]] + [rows_out[(tap - 1) * n : tap * n, cols] for tap in range(1, taps)]
        acc = mm(jnp.concatenate(wide, axis=1), wk[...])
        pre[:, cols] = acc
        active = (0.5 * acc) * (1.0 + gelu_tanh(acc))
        act_t[cols, :] = active.T.astype(bf16)
    for k in range(width // share // 2):
        for bit, out in ((me[0], act_keep), (1 - me[0], act_send)):
            at = pl.multiple_of((2 * k + bit) * share, share)
            out[k * share : (k + 1) * share, :] = act_t[pl.ds(at, share), :]


def up_kernel(cot, mix, up):
    up[...] = contract(cot[...], mix[...], 1, 1)


def mix_kernel(share, where, me, act, act_got, cot, cot_got, *outs):
    half = cot.shape[1] // 2
    blocks = act.shape[0] // share
    for k, (bit, skip) in enumerate(where):
        cols = slice(k * half, (k + 1) * half)
        both = jnp.concatenate([cot[:, cols], cot_got[:, cols]], axis=0)
        pieces = []
        for want in (1 - me[bit], me[bit]):
            for q in range(blocks // 2):
                base = ((q >> skip) << (skip + 1)) | (q & ((1 << skip) - 1))
                at = pl.ds(pl.multiple_of((base + (want << skip)) * share, share), share)
                pieces.append(jnp.concatenate([act[at, :], act_got[at, :]], axis=1))
        total = mm(jnp.concatenate(pieces, axis=0), both)
        rows = total.shape[0] // 2
        outs[2 * k][...] = total[:rows].astype(bf16)
        outs[2 * k + 1][...] = total[rows:]


def select_rows(sources, start, count, taps):
    n = sources.shape[1]
    return jnp.concatenate(
        [onehot(iota((count, n), 0) == sources[tap : tap + 1, :] - start) for tap in range(taps - 1)], axis=1
    )


def weights_kernel(channels, scale, up, pre, x, rows, grad, conv):
    n, width = grad.shape
    taps = rows.shape[0] // n + 1
    turned = []
    for c in range(0, width, WIDE):
        v = pre[:, c : c + WIDE]
        t = gelu_tanh(v)
        slope = 0.5 * (1.0 + t) + (0.5 * TANH_SCALE) * v * (1.0 - t * t) * (1.0 + (3 * TANH_CUBE) * (v * v))
        g = up[:, c : c + WIDE] * slope
        grad[:, c : c + WIDE] = g.astype(bf16)
        turned.append(g.T.astype(bf16))
    turned = jnp.concatenate(turned, axis=1)
    acc = []
    for tap in range(taps):
        part = x[...] if tap == 0 else rows[(tap - 1) * n : tap * n, :]
        acc.append(mm(turned, jnp.concatenate([part[:, c : c + WIDE] for c in range(0, width, WIDE)], axis=0)))
    same = iota((WIDE, WIDE), 0) // channels == iota((WIDE, WIDE), 1) // channels
    conv[...] = jnp.zeros(conv.shape, f32)
    fold = jnp.where(iota((channels, WIDE), 1) % channels == iota((channels, WIDE), 0), 1.0, 0.0)
    for tap in range(taps):
        block = jnp.where(same, acc[tap], 0.0)
        block = jnp.sum(block.reshape(WIDE // channels, channels, WIDE), axis=0)
        conv[:, tap * channels : (tap + 1) * channels] = (
            contract(fold, block, 1, 1, precision=lax.Precision.HIGHEST) * scale
        )


def pick_kernel(place, sources, back_sel):
    taps = back_sel.shape[1] // sources.shape[1] + 1
    back_sel[:ROW, :] = select_rows(sources, place[2], ROW, taps)
    back_sel[ROW:, :] = select_rows(sources, place[3], ROW, taps)


def terms_kernel(grad, wk, back_sel, terms, far, near):
    n, width = grad.shape
    taps = wk.shape[0] // WIDE
    for c in range(0, width, WIDE):
        g = grad[:, c : c + WIDE]
        for tap in range(1, taps):
            terms[(tap - 1) * n : tap * n, c : c + WIDE] = contract(
                g, wk[tap * WIDE : (tap + 1) * WIDE, :], 1, 1
            ).astype(bf16)
        both = mm(back_sel[...], terms[:, c : c + WIDE]).astype(bf16)
        far[:, c : c + WIDE] = both[:ROW]
        near[:, c : c + WIDE] = both[ROW:]


def inner_kernel(grad, terms, wk, sources, cot, inner):
    n, width = grad.shape
    taps = wk.shape[0] // WIDE
    sel = select_rows(sources, ROW, n, taps)
    for c in range(0, width, WIDE):
        acc = contract(grad[:, c : c + WIDE], wk[:WIDE, :], 1, 1) + cot[:, c : c + WIDE].astype(f32)
        inner[:, c : c + WIDE] = acc + mm(sel, terms[:, c : c + WIDE])


def parcel(ref):
    return ref[:16, :128].astype(f32) + ref[:16, 128:256].astype(f32)


def conv_sum(conv, gots):
    one, two, three = [parcel(got) for got in gots]
    return (conv[...] + one) + (two + three)


def quarter(share, bits, skips, kept, gots, sends, keep):
    (lo, hi), (bit_lo, bit_hi) = skips, bits
    small, large = min(lo, hi), max(lo, hi)
    for q in range(kept.shape[0] // share // 4):
        base = ((q >> small) << (small + 1)) | (q & ((1 << small) - 1))
        base = ((base >> large) << (large + 1)) | (base & ((1 << large) - 1))
        for delta in range(4):
            out, out_at = (keep, 0) if delta == 0 else sends[delta - 1]
            want_lo = 1 - bit_lo if delta & 1 else bit_lo
            want_hi = 1 - bit_hi if delta & 2 else bit_hi
            at = pl.multiple_of((base + (want_lo << lo) + (want_hi << hi)) * share, share)
            value = kept[pl.ds(at, share), :]
            for got, got_at in gots:
                value += got[pl.ds(pl.multiple_of(at + got_at, 16), share), :].astype(f32)
            out[out_at + q * share : out_at + (q + 1) * share, :] = value.astype(out.dtype)


def quad_kernel(share, where, first, me, *refs):
    if first:
        kept_a, got_a, kept_b, got_b, conv, conv_got, *outs = refs
        gots_a, gots_b = [(got_a, 0)], [(got_b, 0)]
        whole = conv[...] + conv_got[...]
    else:
        kept_a, one, shared, three, kept_b, two_b, three_b, conv, *outs = refs
        gots_a = [(one, 16), (shared, 16), (three, 16)]
        gots_b = [(shared, 16 + kept_b.shape[0]), (two_b, 0), (three_b, 0)]
        whole = conv_sum(conv, (one, shared, three))
    send_one, send_shared, send_three, keep_a, send_two_b, send_three_b, keep_b, conv_out = outs
    high = whole.astype(bf16)
    low = (whole - high.astype(f32)).astype(bf16)
    conv_out[...] = high.astype(f32) + low.astype(f32)
    for send in (send_one, send_shared, send_three):
        send[:16, :] = jnp.zeros((16, send.shape[1]), bf16)
        send[:16, :128] = high
        send[:16, 128:256] = low
    (bits_a, skips_a), (bits_b, skips_b) = where
    chosen = lambda bits: (me[bits[0]], me[bits[1]])
    sends_a = [(send_one, 16), (send_shared, 16), (send_three, 16)]
    sends_b = [(send_shared, 16 + keep_b.shape[0]), (send_two_b, 0), (send_three_b, 0)]
    quarter(share, chosen(bits_a), skips_a, kept_a, gots_a, sends_a, keep_a)
    quarter(share, chosen(bits_b), skips_b, kept_b, gots_b, sends_b, keep_b)


def last_kernel(scale, channels, kept_a, one, shared, three, kept_b, two_b, three_b, conv, inner, first, second, mix_out, conv_out, grad_out):
    rows, half = kept_a.shape
    total = kept_a[...]
    for got in (one, shared, three):
        total += got[16 : 16 + rows, :].astype(f32)
    mix_out[:, :half] = total * scale
    total = kept_b[...] + shared[16 + rows :, :].astype(f32)
    for got in (two_b, three_b):
        total += got[...].astype(f32)
    mix_out[:, half:] = total * scale
    whole = conv_sum(conv, (one, shared, three))
    for tap in range(conv_out.shape[0]):
        conv_out[tap] = whole[:, tap * channels : (tap + 1) * channels]
    grad_out[...] = (inner[...] + first[...].astype(f32) + second[...].astype(f32)).astype(bf16)


def shards(columns_in, cotangent, conv_weight, mix_weight, neighbours, rotations, pentagons):
    n, width = columns_in.shape
    taps, channels = conv_weight.shape[:2]
    devices = lax.axis_size("space")
    place = lax.axis_index("space").astype(jnp.int32)
    total_cols = n * devices
    levels = width // channels
    bits = devices.bit_length() - 1

    def near_swap(value):
        return lax.ppermute(value, "space", [(i, i ^ 1) for i in range(devices)])

    def far_swap(value):
        other = lambda i: (i + 1 if i % 2 else i - 1) % devices
        return lax.ppermute(value, "space", [(i, other(i)) for i in range(devices)])

    def swap_by(value, mask):
        return lax.ppermute(value, "space", [(i, i ^ mask) for i in range(devices)])

    def swap(value, bit):
        return swap_by(value, 1 << bit)

    far = far_swap(columns_in)
    near = near_swap(columns_in)
    odd = place & 1
    spots = jnp.stack([place * n, jnp.int32(total_cols), odd * (ROW + n), (1 - odd) * (ROW + n)])
    cot_got = swap(cotangent, 0)
    pairs = (taps - 1) * n
    share = width // devices
    half = width // 2
    mine = jnp.stack([(place >> b) & 1 for b in range(bits)])
    halo_sel, sources, own, wk = call(
        early_kernel,
        [((pairs, 2 * ROW), bf16), ((8, n), jnp.int32), ((pairs, width), bf16), ((taps * WIDE, WIDE), bf16)],
        1 << 30,
        spots,
        neighbours.T,
        rotations[None, :],
        pentagons[None, :],
        columns_in,
        conv_weight,
        scalars=1,
        far=(4, 5),
        scratch=[
            pltpu.VMEM(columns_in.shape, bf16),
            pltpu.VMEM(conv_weight.shape, bf16),
            pltpu.SemaphoreType.DMA((2,)),
        ],
    )
    (up,) = call(up_kernel, [((n, width), f32)], 1 << 29, cotangent, mix_weight)
    (back_sel,) = call(pick_kernel, [((2 * ROW, pairs), bf16)], 1 << 26, spots, sources, scalars=1)
    rows, pre, act, act_send = call(
        functools.partial(front_kernel, share),
        [((pairs, width), bf16), ((n, width), f32), ((half, n), bf16), ((half, n), bf16)],
        3 << 30,
        mine,
        far,
        near,
        halo_sel,
        own,
        wk,
        columns_in,
        scalars=1,
        scratch=[pltpu.VMEM((width, n), bf16)],
    )
    act_got = swap(act_send, 0)
    orders = [list(range(1, bits)), list(range(2, bits)) + [1]]
    lefts = [list(range(bits - 1, 0, -1)) for _ in orders]

    def position(k, bit):
        return len(lefts[k]) - 1 - lefts[k].index(bit)

    def drop(k, *gone):
        lefts[k] = [b for b in lefts[k] if b not in gone]

    rows_left = half // 2
    parts = call(
        functools.partial(
            mix_kernel, share, tuple((order[0], position(k, order[0])) for k, order in enumerate(orders))
        ),
        [((rows_left, half), bf16), ((rows_left, half), f32)] * 2,
        1 << 30,
        mine,
        act,
        act_got,
        cotangent,
        cot_got,
        scalars=1,
    )
    kept, gots = [parts[1], parts[3]], []
    for k in (0, 1):
        gots.append([swap(parts[2 * k], orders[k][0])])
        drop(k, orders[k][0])
    grad, conv = call(
        functools.partial(weights_kernel, channels, 1.0 / float(total_cols * levels) ** 0.5),
        [((n, width), bf16), ((channels, 128), f32)],
        2 << 30,
        up,
        pre,
        columns_in,
        rows,
    )
    terms, to_far, to_near = call(
        terms_kernel,
        [((pairs, width), bf16), ((ROW, width), bf16), ((ROW, width), bf16)],
        3 << 30,
        grad,
        wk,
        back_sel,
    )
    conv = conv + swap(conv, 0)
    conv_got = swap(conv, 1)
    from_far = far_swap(to_far)
    from_near = near_swap(to_near)
    state = [kept[0], *gots[0], kept[1], *gots[1], conv, conv_got]
    for stage in range(1, bits - 1, 2):
        rows_left //= 4
        pair = [order[stage : stage + 2] for order in orders]
        where = tuple((tuple(p), tuple(position(k, b) for b in p)) for k, p in enumerate(pair))
        one, shared, three, keep_a, two_b, three_b, keep_b, conv = call(
            functools.partial(quad_kernel, share, where, stage == 1),
            [
                ((rows_left + 16, half), bf16),
                ((2 * rows_left + 16, half), bf16),
                ((rows_left + 16, half), bf16),
                ((rows_left, half), f32),
                ((rows_left, half), bf16),
                ((rows_left, half), bf16),
                ((rows_left, half), f32),
                ((channels, 128), f32),
            ],
            1 << 20,
            mine,
            *state,
            scalars=1,
        )
        (a_lo, both_bit), (_, b_hi) = pair
        shared = swap(shared, both_bit)
        three = swap_by(three, 1 << a_lo | 1 << both_bit)
        three_b = swap_by(three_b, 1 << both_bit | 1 << b_hi)
        two_b = swap(two_b, b_hi)
        one = swap(one, a_lo)
        state = [keep_a, one, shared, three, keep_b, two_b, three_b, conv]
        for k in (0, 1):
            drop(k, *pair[k])
    (inner,) = call(
        inner_kernel, [((n, width), f32)], 1 << 30, grad, terms, wk, sources, cotangent
    )
    grad_mix, grad_conv, grad_input = call(
        functools.partial(last_kernel, 1.0 / float(total_cols) ** 0.5, channels),
        [((share, width), f32), ((taps, channels, channels), f32), ((n, width), bf16)],
        1 << 20,
        *state,
        inner,
        from_far,
        from_near,
    )
    return grad_input, grad_mix, grad_conv


def solution(mesh):
    return jax.shard_map(
        shards,
        mesh=mesh,
        in_specs=(
            P(("group", "space"), None),
            P(("group", "space"), None),
            P(),
            P(),
            P("space", None),
            P("space"),
            P("space"),
        ),
        out_specs=(P(("group", "space"), None), P("space", "group"), P("group", None, None)),
        check_vma=False,
    )
```

```python
import functools

import jax
import jax.numpy as jnp
from jax import lax
from jax.experimental import pallas as pl
from jax.experimental.pallas import tpu as pltpu
from jax.sharding import PartitionSpec as P


ROW = 256
WIDE = 256
TANH_SCALE = 0.7978845608028654
TANH_CUBE = 0.044715


f32 = jnp.float32
bf16 = jnp.bfloat16


def mm(a, b):
    return jnp.dot(a, b, preferred_element_type=f32)


def contract(a, b, dim_a, dim_b, **kw):
    return lax.dot_general(
        a, b, (((dim_a,), (dim_b,)), ((), ())), preferred_element_type=f32, **kw
    )


def iota(shape, dim):
    return lax.broadcasted_iota(jnp.int32, shape, dim)


def onehot(cond):
    return jnp.where(cond, 1.0, 0.0).astype(bf16)


def call(body, outs, cost, *args, scratch=(), scalars=0, far=()):
    space = lambda k: pltpu.SMEM if k < scalars else pltpu.HBM if k in far else pltpu.VMEM
    return pl.pallas_call(
        body,
        out_shape=[jax.ShapeDtypeStruct(s, d) for s, d in outs],
        in_specs=[pl.BlockSpec(memory_space=space(k)) for k in range(len(args))],
        out_specs=[pl.BlockSpec(memory_space=pltpu.VMEM)] * len(outs),
        scratch_shapes=list(scratch),
        cost_estimate=pl.CostEstimate(flops=cost, transcendentals=0, bytes_accessed=8 << 20),
        compiler_params=pltpu.CompilerParams(vmem_limit_bytes=12 << 20),
    )(*args)


def picked(local_t, turns, tap):
    turn = tap - 1 - turns
    slot = 1 + jnp.where(turn < 0, turn + 6, turn)
    source = jnp.full_like(slot, -1)
    for k in range(1, 7):
        source = jnp.where(slot == k, local_t[k : k + 1, :], source)
    return source


def early_kernel(place, near, turns, void, x_hbm, conv_hbm, halo_sel, sources_out, own, wk, x, conv, sems):
    copies = [
        pltpu.make_async_copy(src, dst, sems.at[k])
        for k, (src, dst) in enumerate(((conv_hbm, conv), (x_hbm, x)))
    ]
    for copy in copies:
        copy.start()
    n = x.shape[0]
    taps, c = conv.shape[:2]
    offset, total = place[0], place[1]
    base_far, base_near = place[2], place[3]
    moved = near[...] - offset + ROW
    moved = jnp.where(moved < 0, moved + total, moved)
    moved = jnp.where(moved >= total, moved - total, moved)
    dropped = (void[...] == 1) & (iota((taps, n), 0) == 6)
    local_t = jnp.where(dropped, -1, moved)
    sources = [picked(local_t, turns[...], tap) for tap in range(1, taps)]
    sources_t = jnp.concatenate(sources + [sources[0]] * (8 - len(sources)), axis=0)
    sources_out[...] = sources_t
    eye = jnp.where(iota((n, n), 0) == iota((n, n), 1), 1.0, 0.0)
    columns = contract(eye, sources_t.astype(f32), 1, 1, precision=lax.Precision.HIGHEST)
    columns = columns.astype(jnp.int32)

    copies[0].wait()
    repeat = onehot(iota((c, WIDE), 1) % c == iota((c, WIDE), 0))
    down = onehot(iota((WIDE, c), 0) % c == iota((WIDE, c), 1))
    same = iota((WIDE, WIDE), 0) // c == iota((WIDE, WIDE), 1) // c
    for tap in range(taps):
        wide = mm(conv[tap], repeat).astype(bf16)
        wk[tap * WIDE : (tap + 1) * WIDE, :] = jnp.where(same, mm(down, wide), 0.0).astype(bf16)
    copies[1].wait()
    for tap in range(1, taps):
        at = (tap - 1) * n
        source = columns[:, tap - 1 : tap]
        halo_sel[at : at + n, :ROW] = onehot(iota((n, ROW), 1) == source - base_far)
        halo_sel[at : at + n, ROW:] = onehot(iota((n, ROW), 1) == source - base_near)
        mine = onehot(iota((n, n), 1) + ROW == source)
        own[at : at + n, :] = mm(mine, x[...]).astype(bf16)


def gelu_tanh(v):
    return jnp.tanh(TANH_SCALE * (v + TANH_CUBE * (v * v * v)))


def front_kernel(share, me, far, near, halo_sel, own, wk, x, rows_out, pre, act_keep, act_send, act_t):
    n, width = pre.shape
    taps = wk.shape[0] // WIDE
    for c in range(0, width, WIDE):
        cols = slice(c, c + WIDE)
        both = jnp.concatenate([far[:, cols], near[:, cols]], axis=0)
        for tap in range(1, taps):
            at = slice((tap - 1) * n, tap * n)
            rows_out[at, cols] = mm(halo_sel[at, :], both).astype(bf16) + own[at, cols]
    for c in range(0, width, WIDE):
        cols = slice(c, c + WIDE)
        wide = [x[:, cols]] + [rows_out[(tap - 1) * n : tap * n, cols] for tap in range(1, taps)]
        acc = mm(jnp.concatenate(wide, axis=1), wk[...])
        pre[:, cols] = acc
        active = (0.5 * acc) * (1.0 + gelu_tanh(acc))
        act_t[cols, :] = active.T.astype(bf16)
    for k in range(width // share // 2):
        for bit, out in ((me[0], act_keep), (1 - me[0], act_send)):
            at = pl.multiple_of((2 * k + bit) * share, share)
            out[k * share : (k + 1) * share, :] = act_t[pl.ds(at, share), :]


def up_kernel(cot, mix, up):
    up[...] = contract(cot[...], mix[...], 1, 1)


def mix_kernel(share, where, me, act, act_got, cot, cot_got, *outs):
    half = cot.shape[1] // 2
    blocks = act.shape[0] // share
    for k, (bit, skip) in enumerate(where):
        cols = slice(k * half, (k + 1) * half)
        both = jnp.concatenate([cot[:, cols], cot_got[:, cols]], axis=0)
        pieces = []
        for want in (1 - me[bit], me[bit]):
            for q in range(blocks // 2):
                base = ((q >> skip) << (skip + 1)) | (q & ((1 << skip) - 1))
                at = pl.ds(pl.multiple_of((base + (want << skip)) * share, share), share)
                pieces.append(jnp.concatenate([act[at, :], act_got[at, :]], axis=1))
        total = mm(jnp.concatenate(pieces, axis=0), both)
        rows = total.shape[0] // 2
        outs[2 * k][...] = total[:rows].astype(bf16)
        outs[2 * k + 1][...] = total[rows:]


def select_rows(sources, start, count, taps):
    n = sources.shape[1]
    return jnp.concatenate(
        [onehot(iota((count, n), 0) == sources[tap : tap + 1, :] - start) for tap in range(taps - 1)], axis=1
    )


def weights_kernel(channels, scale, up, pre, x, rows, grad, conv):
    n, width = grad.shape
    taps = rows.shape[0] // n + 1
    turned = []
    for c in range(0, width, WIDE):
        v = pre[:, c : c + WIDE]
        t = gelu_tanh(v)
        slope = 0.5 * (1.0 + t) + (0.5 * TANH_SCALE) * v * (1.0 - t * t) * (1.0 + (3 * TANH_CUBE) * (v * v))
        g = up[:, c : c + WIDE] * slope
        grad[:, c : c + WIDE] = g.astype(bf16)
        turned.append(g.T.astype(bf16))
    turned = jnp.concatenate(turned, axis=1)
    acc = []
    for tap in range(taps):
        part = x[...] if tap == 0 else rows[(tap - 1) * n : tap * n, :]
        acc.append(mm(turned, jnp.concatenate([part[:, c : c + WIDE] for c in range(0, width, WIDE)], axis=0)))
    same = iota((WIDE, WIDE), 0) // channels == iota((WIDE, WIDE), 1) // channels
    conv[...] = jnp.zeros(conv.shape, f32)
    fold = jnp.where(iota((channels, WIDE), 1) % channels == iota((channels, WIDE), 0), 1.0, 0.0)
    for tap in range(taps):
        block = jnp.where(same, acc[tap], 0.0)
        block = jnp.sum(block.reshape(WIDE // channels, channels, WIDE), axis=0)
        conv[:, tap * channels : (tap + 1) * channels] = (
            contract(fold, block, 1, 1, precision=lax.Precision.HIGHEST) * scale
        )


def pick_kernel(place, sources, back_sel):
    taps = back_sel.shape[1] // sources.shape[1] + 1
    back_sel[:ROW, :] = select_rows(sources, place[2], ROW, taps)
    back_sel[ROW:, :] = select_rows(sources, place[3], ROW, taps)


def terms_kernel(grad, wk, back_sel, terms, far, near):
    n, width = grad.shape
    taps = wk.shape[0] // WIDE
    for c in range(0, width, WIDE):
        g = grad[:, c : c + WIDE]
        for tap in range(1, taps):
            terms[(tap - 1) * n : tap * n, c : c + WIDE] = contract(
                g, wk[tap * WIDE : (tap + 1) * WIDE, :], 1, 1
            ).astype(bf16)
        both = mm(back_sel[...], terms[:, c : c + WIDE]).astype(bf16)
        far[:, c : c + WIDE] = both[:ROW]
        near[:, c : c + WIDE] = both[ROW:]


def inner_kernel(grad, terms, wk, sources, cot, inner):
    n, width = grad.shape
    taps = wk.shape[0] // WIDE
    sel = select_rows(sources, ROW, n, taps)
    for c in range(0, width, WIDE):
        acc = contract(grad[:, c : c + WIDE], wk[:WIDE, :], 1, 1) + cot[:, c : c + WIDE].astype(f32)
        inner[:, c : c + WIDE] = acc + mm(sel, terms[:, c : c + WIDE])


def parcel(ref):
    return ref[:16, :128].astype(f32) + ref[:16, 128:256].astype(f32)


def conv_sum(conv, gots):
    one, two, three = [parcel(got) for got in gots]
    return (conv[...] + one) + (two + three)


def quarter(share, bits, skips, kept, gots, sends, keep):
    (lo, hi), (bit_lo, bit_hi) = skips, bits
    small, large = min(lo, hi), max(lo, hi)
    for q in range(kept.shape[0] // share // 4):
        base = ((q >> small) << (small + 1)) | (q & ((1 << small) - 1))
        base = ((base >> large) << (large + 1)) | (base & ((1 << large) - 1))
        for delta in range(4):
            out, out_at = (keep, 0) if delta == 0 else sends[delta - 1]
            want_lo = 1 - bit_lo if delta & 1 else bit_lo
            want_hi = 1 - bit_hi if delta & 2 else bit_hi
            at = pl.multiple_of((base + (want_lo << lo) + (want_hi << hi)) * share, share)
            value = kept[pl.ds(at, share), :]
            for got, got_at in gots:
                value += got[pl.ds(pl.multiple_of(at + got_at, 16), share), :].astype(f32)
            out[out_at + q * share : out_at + (q + 1) * share, :] = value.astype(out.dtype)


def quad_kernel(share, where, first, me, *refs):
    if first:
        kept_a, got_a, kept_b, got_b, conv, conv_got, *outs = refs
        gots_a, gots_b = [(got_a, 0)], [(got_b, 0)]
        whole = conv[...] + conv_got[...]
    else:
        kept_a, one, shared, three, kept_b, two_b, three_b, conv, *outs = refs
        gots_a = [(one, 16), (shared, 16), (three, 16)]
        gots_b = [(shared, 16 + kept_b.shape[0]), (two_b, 0), (three_b, 0)]
        whole = conv_sum(conv, (one, shared, three))
    send_one, send_shared, send_three, keep_a, send_two_b, send_three_b, keep_b, conv_out = outs
    high = whole.astype(bf16)
    low = (whole - high.astype(f32)).astype(bf16)
    conv_out[...] = high.astype(f32) + low.astype(f32)
    for send in (send_one, send_shared, send_three):
        send[:16, :] = jnp.zeros((16, send.shape[1]), bf16)
        send[:16, :128] = high
        send[:16, 128:256] = low
    (bits_a, skips_a), (bits_b, skips_b) = where
    chosen = lambda bits: (me[bits[0]], me[bits[1]])
    sends_a = [(send_one, 16), (send_shared, 16), (send_three, 16)]
    sends_b = [(send_shared, 16 + keep_b.shape[0]), (send_two_b, 0), (send_three_b, 0)]
    quarter(share, chosen(bits_a), skips_a, kept_a, gots_a, sends_a, keep_a)
    quarter(share, chosen(bits_b), skips_b, kept_b, gots_b, sends_b, keep_b)


def last_kernel(scale, channels, kept_a, one, shared, three, kept_b, two_b, three_b, conv, mix_out, conv_out):
    rows, half = kept_a.shape
    total = kept_a[...]
    for got in (one, shared, three):
        total += got[16 : 16 + rows, :].astype(f32)
    mix_out[:, :half] = total * scale
    total = kept_b[...] + shared[16 + rows :, :].astype(f32)
    for got in (two_b, three_b):
        total += got[...].astype(f32)
    mix_out[:, half:] = total * scale
    whole = conv_sum(conv, (one, shared, three))
    for tap in range(conv_out.shape[0]):
        conv_out[tap] = whole[:, tap * channels : (tap + 1) * channels]


def total_kernel(inner, first, second, grad_out):
    grad_out[...] = (inner[...] + first[...].astype(f32) + second[...].astype(f32)).astype(bf16)


def shards(columns_in, cotangent, conv_weight, mix_weight, neighbours, rotations, pentagons):
    n, width = columns_in.shape
    taps, channels = conv_weight.shape[:2]
    devices = lax.axis_size("space")
    place = lax.axis_index("space").astype(jnp.int32)
    total_cols = n * devices
    levels = width // channels
    bits = devices.bit_length() - 1

    def near_swap(value):
        return lax.ppermute(value, "space", [(i, i ^ 1) for i in range(devices)])

    def far_swap(value):
        other = lambda i: (i + 1 if i % 2 else i - 1) % devices
        return lax.ppermute(value, "space", [(i, other(i)) for i in range(devices)])

    def swap_by(value, mask):
        return lax.ppermute(value, "space", [(i, i ^ mask) for i in range(devices)])

    def swap(value, bit):
        return swap_by(value, 1 << bit)

    far = far_swap(columns_in)
    near = near_swap(columns_in)
    odd = place & 1
    spots = jnp.stack([place * n, jnp.int32(total_cols), odd * (ROW + n), (1 - odd) * (ROW + n)])
    cot_got = swap(cotangent, 0)
    pairs = (taps - 1) * n
    share = width // devices
    half = width // 2
    mine = jnp.stack([(place >> b) & 1 for b in range(bits)])
    halo_sel, sources, own, wk = call(
        early_kernel,
        [((pairs, 2 * ROW), bf16), ((8, n), jnp.int32), ((pairs, width), bf16), ((taps * WIDE, WIDE), bf16)],
        1 << 30,
        spots,
        neighbours.T,
        rotations[None, :],
        pentagons[None, :],
        columns_in,
        conv_weight,
        scalars=1,
        far=(4, 5),
        scratch=[
            pltpu.VMEM(columns_in.shape, bf16),
            pltpu.VMEM(conv_weight.shape, bf16),
            pltpu.SemaphoreType.DMA((2,)),
        ],
    )
    (up,) = call(up_kernel, [((n, width), f32)], 1 << 29, cotangent, mix_weight)
    (back_sel,) = call(pick_kernel, [((2 * ROW, pairs), bf16)], 1 << 26, spots, sources, scalars=1)
    rows, pre, act, act_send = call(
        functools.partial(front_kernel, share),
        [((pairs, width), bf16), ((n, width), f32), ((half, n), bf16), ((half, n), bf16)],
        3 << 30,
        mine,
        far,
        near,
        halo_sel,
        own,
        wk,
        columns_in,
        scalars=1,
        scratch=[pltpu.VMEM((width, n), bf16)],
    )
    act_got = swap(act_send, 0)
    orders = [list(range(1, bits)), list(range(2, bits)) + [1]]
    lefts = [list(range(bits - 1, 0, -1)) for _ in orders]

    def position(k, bit):
        return len(lefts[k]) - 1 - lefts[k].index(bit)

    def drop(k, *gone):
        lefts[k] = [b for b in lefts[k] if b not in gone]

    rows_left = half // 2
    parts = call(
        functools.partial(
            mix_kernel, share, tuple((order[0], position(k, order[0])) for k, order in enumerate(orders))
        ),
        [((rows_left, half), bf16), ((rows_left, half), f32)] * 2,
        1 << 30,
        mine,
        act,
        act_got,
        cotangent,
        cot_got,
        scalars=1,
    )
    kept, gots = [parts[1], parts[3]], []
    for k in (0, 1):
        gots.append([swap(parts[2 * k], orders[k][0])])
        drop(k, orders[k][0])
    grad, conv = call(
        functools.partial(weights_kernel, channels, 1.0 / float(total_cols * levels) ** 0.5),
        [((n, width), bf16), ((channels, 128), f32)],
        2 << 30,
        up,
        pre,
        columns_in,
        rows,
    )
    terms, to_far, to_near = call(
        terms_kernel,
        [((pairs, width), bf16), ((ROW, width), bf16), ((ROW, width), bf16)],
        3 << 30,
        grad,
        wk,
        back_sel,
    )
    conv = conv + swap(conv, 0)
    conv_got = swap(conv, 1)
    from_far = far_swap(to_far)
    from_near = near_swap(to_near)
    state = [kept[0], *gots[0], kept[1], *gots[1], conv, conv_got]
    for stage in range(1, bits - 1, 2):
        rows_left //= 4
        pair = [order[stage : stage + 2] for order in orders]
        where = tuple((tuple(p), tuple(position(k, b) for b in p)) for k, p in enumerate(pair))
        one, shared, three, keep_a, two_b, three_b, keep_b, conv = call(
            functools.partial(quad_kernel, share, where, stage == 1),
            [
                ((rows_left + 16, half), bf16),
                ((2 * rows_left + 16, half), bf16),
                ((rows_left + 16, half), bf16),
                ((rows_left, half), f32),
                ((rows_left, half), bf16),
                ((rows_left, half), bf16),
                ((rows_left, half), f32),
                ((channels, 128), f32),
            ],
            1 << 20,
            mine,
            *state,
            scalars=1,
        )
        (a_lo, both_bit), (_, b_hi) = pair
        shared = swap(shared, both_bit)
        three = swap_by(three, 1 << a_lo | 1 << both_bit)
        three_b = swap_by(three_b, 1 << both_bit | 1 << b_hi)
        two_b = swap(two_b, b_hi)
        one = swap(one, a_lo)
        state = [keep_a, one, shared, three, keep_b, two_b, three_b, conv]
        for k in (0, 1):
            drop(k, *pair[k])
    (inner,) = call(
        inner_kernel, [((n, width), f32)], 1 << 30, grad, terms, wk, sources, cotangent
    )
    (grad_input,) = call(total_kernel, [((n, width), bf16)], 1 << 20, inner, from_far, from_near)
    grad_mix, grad_conv = call(
        functools.partial(last_kernel, 1.0 / float(total_cols) ** 0.5, channels),
        [((share, width), f32), ((taps, channels, channels), f32)],
        1 << 20,
        *state,
    )
    return grad_input, grad_mix, grad_conv


def solution(mesh):
    return jax.shard_map(
        shards,
        mesh=mesh,
        in_specs=(
            P(("group", "space"), None),
            P(("group", "space"), None),
            P(),
            P(),
            P("space", None),
            P("space"),
            P("space"),
        ),
        out_specs=(P(("group", "space"), None), P("space", "group"), P("group", None, None)),
        check_vma=False,
    )
```
